32 devices in a mesh: ep: 16 (over z, y, x), tp: 2 (over core).
Axes of the slice: x: 2, y: 2, z: 4, core: 2. Of those that a mesh axis runs over, the one named last changes fastest.
Arguments:
- tokens: bfloat16 [4096, 1024], P(('ep', 'tp')), may hold values from -6 to 6
- segment_ids: int32 [16, 256], P('ep'), may hold values from 0 to 5, never falling along the last dimension, each value on 1 to 128 neighbouring positions
- routes: int32 [4096, 8], P(('ep', 'tp')), may hold values from 0 to 15, all different within a row; in each aligned block of 128 rows (0 to 127, 128 to 255, ...) at most 80 rows name the same one
- cotangent: bfloat16 [4096, 1024], P(('ep', 'tp')), may hold values from -6 to 6
- query_weight: bfloat16 [1024, 1024], replicated, may hold values from -0.1875 to 0.1875
- key_weight: bfloat16 [1024, 512], replicated, may hold values from -0.1875 to 0.1875
- value_weight: bfloat16 [1024, 512], replicated, may hold values from -0.1875 to 0.1875
- proj_weight: bfloat16 [1024, 1024], replicated, may hold values from -0.75 to 0.75
- attn_gain: bfloat16 [1024], replicated, may hold values from 0.5 to 1.5
- moe_gain: bfloat16 [1024], replicated, may hold values from 0.5 to 1.5
- router_weight: bfloat16 [1024, 16], replicated, may hold values from -0.1875 to 0.1875
- gate_weight: bfloat16 [16, 1024, 512], P('ep', None, 'tp'), may hold values from -0.1875 to 0.1875
- up_weight: bfloat16 [16, 1024, 512], P('ep', None, 'tp'), may hold values from -0.1875 to 0.1875
- down_weight: bfloat16 [16, 512, 1024], P('ep', 'tp'), may hold values from -0.25 to 0.25
Outputs:
- layer_out: bfloat16 [4096, 1024], P(('ep', 'tp'))
- grad_tokens: bfloat16 [4096, 1024], P(('ep', 'tp'))
- grad_query: float32 [1024, 1024], replicated
- grad_key: float32 [1024, 512], replicated
- grad_value: float32 [1024, 512], replicated
- grad_proj: float32 [1024, 1024], replicated
- grad_attn_gain: float32 [1024], replicated
- grad_moe_gain: float32 [1024], replicated
- grad_router: float32 [1024, 16], replicated
- grad_gate: float32 [16, 1024, 512], P('ep', None, 'tp')
- grad_up: float32 [16, 1024, 512], P('ep', None, 'tp')
- grad_down: float32 [16, 512, 1024], P('ep', 'tp')
The draws below stay inside these ranges and needn't reach their ends.
Inputs may be any that keep to these rules, and one draw needn't show every extreme that they name: `routes`: row t names 8 different experts; among the rows of one device (aligned blocks of 128 rows) no expert is named by more than 80 rows, and in every draw some expert is named by exactly 80 rows of some block. `segment_ids`: within a sequence the ids never fall; a segment holds 1 to 128 positions and some segment holds exactly 128.
All inputs are finite; a program needn't handle non-finite values.
Results may differ from the reference program's by a relative error of at most 0.015.
The reference program's roundings to bfloat16 on the way count: a program that leaves them out, or rounds other values in their place, can miss the bound.
Values may be sent and summed in bfloat16 or wider, within the bound.
No kernel may reach another device: no remote copies, remote signals or barrier semaphores. Data moves between devices by JAX's collectives and lax.ppermute only.
A program may use at most 256 MiB of HBM per device.

```python
import math
import jax
import jax.numpy as jnp
import numpy as np
from jax import lax

D = 1024
HEADS = 16
KV_HEADS = 8
HEAD_DIM = 64
FF = 512
TOP = 8
TOK_DEV = 128
DOCS = 6
EXPERTS = 16
LEN = 256
SEQS = 16
TOKENS = 4096
CAP = 80


def block_levels(own_key, shape, cuts, low, top_value):
    def one(position, shards_of):
        heights = jax.random.uniform(jax.random.fold_in(jax.random.fold_in(own_key, 6), position), (shards_of,), jnp.float32, low / len(cuts), top_value / len(cuts))
        return jnp.repeat(jnp.exp(heights), shape[position] // shards_of).reshape((-1,) + (1,) * (len(shape) - position - 1))

    level = one(*cuts[0])
    for cut in cuts[1:]:
        level = level * one(*cut)
    return level


def length_profile(amount, total, limit, skew):
    loads = [(1 << 20) // math.isqrt(rank ** skew) + 1 for rank in range(2, amount + 1)]
    spare, given = total - limit - (amount - 1), [1] * (amount - 1)
    while spare > 0:
        free = [i for i in range(amount - 1) if given[i] < limit]
        pool, budget = sum([loads[i] for i in free]), spare
        for i in free:
            extra = min(limit - given[i], max(1, budget * loads[i] // pool), spare)
            given[i] = given[i] + extra
            spare = spare - extra
    return np.array([limit] + given)


def ragged_sizes(key, number_of, total, bound, skew):
    if number_of == 2:
        one = jax.random.randint(key, (), max(1, total - bound), min(bound, total - 1) + 1)
        return jnp.stack([one, total - one])
    lengths = jnp.asarray(length_profile(number_of, total, bound, skew), jnp.int32)
    pairs = (number_of - 1) // 2
    giver, sink = lengths[1:1 + 2 * pairs:2], lengths[2:2 + 2 * pairs:2]
    slack = jnp.minimum(giver - 1, bound - sink)
    passed = jax.random.randint(jax.random.fold_in(key, 1), (pairs,), 0, 1 << 20) % (slack + 1)
    lengths = lengths.at[1:1 + 2 * pairs:2].set(giver - passed).at[2:2 + 2 * pairs:2].set(sink + passed)
    return lengths[jax.random.permutation(jax.random.fold_in(key, 2), number_of)]


def assign_block(stream_key, own, number, rows, amount, top, reach, slope):
    sequence = jax.random.permutation(stream_key, amount)
    packed, usual = load_shares(amount, rows * top, reach, slope, True), load_shares(amount, rows * top, reach, slope, False)
    places = jnp.arange(amount)

    def named(sizes, rotation):
        used = int((sizes > 0).sum())
        fixed = max(1, used // 4)
        moved = fixed + (places - fixed + rotation * (used - fixed)) % max(1, amount - fixed)
        return jnp.zeros((amount,), jnp.int32).at[sequence[jnp.where(places < fixed, places, moved)]].set(jnp.asarray(sizes, jnp.int32))

    sizes = jnp.where(number % 4 == 0, named(packed, number // 4), named(usual, number - number // 4 - 1))
    mixed = jax.random.permutation(jax.random.fold_in(own, 3), amount)
    donor, receiver = mixed[0:amount // 2 * 2:2], mixed[1:amount // 2 * 2:2]
    slack = jnp.minimum(sizes[donor] - 1, reach - sizes[receiver]) // 2
    slack = jnp.where((donor == sequence[0]) | (receiver == sequence[0]) | (sizes[receiver] == 0), 0, jnp.maximum(slack, 0))
    moved = jax.random.randint(jax.random.fold_in(own, 4), (amount // 2,), 0, 1 << 20) % (slack + 1)
    sizes = sizes.at[donor].add(-moved).at[receiver].add(moved)
    items = jnp.searchsorted(jnp.cumsum(sizes), jnp.arange(rows * top), side="right").astype(jnp.int32)
    grid = items.reshape(top, rows).T
    grid = grid[jax.random.permutation(jax.random.fold_in(own, 1), rows)]
    rotation = jax.random.randint(jax.random.fold_in(own, 2), (rows, 1), 0, top)
    return jnp.take_along_axis(grid, (jnp.arange(top)[None, :] + rotation) % top, axis=1)


def load_shares(count, total, reach, lean, full):
    weights = [(1 << 20) // math.isqrt(rank ** lean) + 1 for rank in range(1, count + 1)]
    largest = reach if full else min(reach, max(-(-total // count), total * weights[0] // sum(weights)))
    least = 1 if total - largest >= count - 1 else 0
    holding, spare = [largest] + [least] * (count - 1), total - largest - least * (count - 1)
    while spare > 0:
        movable = [i for i in range(1, count) if holding[i] < largest] or [i for i in range(1, count) if holding[i] < reach]
        pool, remaining = sum([weights[i] for i in movable]), spare
        for i in movable:
            more = min(reach - holding[i], max(1, remaining * weights[i] // pool), spare)
            holding[i] = holding[i] + more
            spare = spare - more
    return np.array(holding)


def normal_values(own_key, extent, width, reach, shards=(), dtype=jnp.bfloat16):
    values = jax.random.normal(own_key, extent, jnp.float32) * width
    if len(shards) > 0:
        values = block_levels(own_key, extent, shards, -0.22, 0.18) * values
    return jnp.clip(values, min=-reach, max=reach).astype(dtype)


def setup_inputs(seed: int = 0) -> dict:
    key_list = jax.random.split(jax.random.key(seed), 15)
    tokens = normal_values(key_list[0], (TOKENS, D), 1.0, 6.0, ((0, 32),))
    segment_ids = jax.vmap(lambda own: jnp.searchsorted(jnp.cumsum(ragged_sizes(own, DOCS, LEN, LEN // 2, 1)), jnp.arange(LEN), side="right"))(jax.random.split(key_list[1], SEQS)).reshape((SEQS, LEN)).astype(jnp.int32)
    routes_keys = jax.random.split(jax.random.fold_in(key_list[2], 1), TOKENS // TOK_DEV)
    routes_turns = jax.random.permutation(jax.random.fold_in(key_list[2], 3), TOKENS // TOK_DEV)
    routes = jax.vmap(lambda own, number: assign_block(jax.random.fold_in(key_list[2], 2), own, number, TOK_DEV, EXPERTS, TOP, CAP, 2))(routes_keys, routes_turns).reshape((TOKENS, TOP))
    cotangent = normal_values(key_list[3], (TOKENS, D), 1.0, 6.0, ((0, 32),))
    query_weight = normal_values(key_list[4], (D, HEADS * HEAD_DIM), D ** -0.5, 0.1875)
    key_weight = normal_values(key_list[5], (D, KV_HEADS * HEAD_DIM), D ** -0.5, 0.1875)
    value_weight = normal_values(key_list[6], (D, KV_HEADS * HEAD_DIM), D ** -0.5, 0.1875)
    proj_weight = normal_values(key_list[7], (HEADS * HEAD_DIM, D), (D // 16) ** -0.5, 0.75)
    attn_gain = jnp.clip(1.0 + 0.1 * jax.random.normal(key_list[8], (D,), jnp.float32), 0.5, 1.5).astype(jnp.bfloat16)
    moe_gain = jnp.clip(1.0 + 0.1 * jax.random.normal(key_list[9], (D,), jnp.float32), 0.5, 1.5).astype(jnp.bfloat16)
    router_weight = normal_values(key_list[10], (D, EXPERTS), D ** -0.5, 0.1875)
    gate_weight = normal_values(key_list[11], (EXPERTS, D, FF), D ** -0.5, 0.1875, ((0, 16), (2, 2)))
    up_weight = normal_values(key_list[12], (EXPERTS, D, FF), D ** -0.5, 0.1875, ((0, 16), (2, 2)))
    down_weight = normal_values(key_list[13], (EXPERTS, FF, D), FF ** -0.5, 0.25, ((0, 16), (1, 2)))
    return dict(tokens=tokens, segment_ids=segment_ids, routes=routes, cotangent=cotangent, query_weight=query_weight, key_weight=key_weight, value_weight=value_weight, proj_weight=proj_weight, attn_gain=attn_gain, moe_gain=moe_gain, router_weight=router_weight, gate_weight=gate_weight, up_weight=up_weight, down_weight=down_weight)


@jax.custom_vjp
def low(v):
    return lax.optimization_barrier(v.astype(jnp.bfloat16)).astype(jnp.float32)

@jax.custom_vjp
def low_back(v):
    return v

def low_keep(v):
    return (low(v), None)

def low_pass(kept, grad):
    return (grad,)

def back_keep(v):
    return (v, None)

def back_low(kept, grad):
    return (low(grad),)
low.defvjp(low_keep, low_pass)
low_back.defvjp(back_keep, back_low)
EPS = 1e-06
THETA = 10000.0
MASKED = -1000000000.0
HIGH = lax.Precision.HIGHEST

def mult(left, right):
    return jnp.dot(left, right, preferred_element_type=jnp.float32, precision=HIGH)

def rms_apply(values, gain_vec):
    return values * lax.rsqrt(lax.optimization_barrier(jnp.mean(values * values, axis=-1, keepdims=True)) + EPS) * gain_vec

def rope_tables(positions):
    half_dim = HEAD_DIM // 2
    inverse_freq = THETA ** (-(jnp.arange(half_dim).astype(jnp.float32) * 2.0) / HEAD_DIM)
    angles = positions.astype(jnp.float32)[:, None] * inverse_freq[None, :]
    return (jnp.cos(angles), jnp.sin(angles))

def rotate(values, cosine, sine_table):
    half_dim = values.shape[-1] // 2
    leading = values[..., :half_dim]
    trailing = values[..., half_dim:]
    cos_rows = cosine[:, None, :]
    sin_rows = sine_table[:, None, :]
    return jnp.concatenate([leading * cos_rows - trailing * sin_rows, trailing * cos_rows + leading * sin_rows], axis=-1)

def attend_sequence(operands):
    queries, key_rows, values, segment_row = operands
    group_size = HEADS // KV_HEADS
    grouped = queries.reshape(LEN, KV_HEADS, group_size, HEAD_DIM)
    scores = jnp.einsum('tkgd,skd->kgts', grouped, key_rows, precision=HIGH) * HEAD_DIM ** (-0.5)
    scores = low_back(scores)
    places = jnp.arange(LEN)
    allowed = (places[:, None] >= places[None, :]) & (segment_row[:, None] == segment_row[None, :])
    scores = jnp.where(allowed[None, None], scores, MASKED)
    soft_weights = low(jax.nn.softmax(scores, axis=-1))
    blended = jnp.einsum('kgts,skd->tkgd', soft_weights, values, precision=HIGH)
    return blended.reshape(LEN, HEADS * HEAD_DIM)

def forward(floats, segment_ids, routes):
    tokens, query_weight, key_weight, value_weight, proj_weight, attn_gain, moe_gain, router_weight, gate_weight, up_weight, down_weight = floats
    normed_one = low(rms_apply(tokens, attn_gain))
    query_raw = low_back(mult(normed_one, query_weight))
    key_raw = low_back(mult(normed_one, key_weight))
    values = low_back(low(mult(normed_one, value_weight)))
    positions = jnp.arange(TOKENS) % LEN
    cosine, sine_table = rope_tables(positions)
    queries = low_back(low(rotate(query_raw.reshape(TOKENS, HEADS, HEAD_DIM), cosine, sine_table)))
    key_rows = low_back(low(rotate(key_raw.reshape(TOKENS, KV_HEADS, HEAD_DIM), cosine, sine_table)))
    attended = lax.map(jax.checkpoint(attend_sequence), (queries.reshape(SEQS, LEN, HEADS, HEAD_DIM), key_rows.reshape(SEQS, LEN, KV_HEADS, HEAD_DIM), values.reshape(SEQS, LEN, KV_HEADS, HEAD_DIM), segment_ids))
    attended = low_back(low(attended.reshape(TOKENS, HEADS * HEAD_DIM)))
    hidden = tokens + low_back(mult(attended, proj_weight))
    normed_two = low(rms_apply(hidden, moe_gain))
    logits = low_back(mult(normed_two, router_weight))
    chosen = (routes[:, :, None] == jnp.arange(EXPERTS)[None, None, :]).astype(jnp.float32)
    picked = lax.optimization_barrier(jnp.sum(chosen * logits[:, None, :], axis=-1))
    gate_probs = jax.nn.softmax(picked, axis=-1)
    route_weights = lax.optimization_barrier(jnp.sum(gate_probs[:, :, None] * chosen, axis=1))

    def expert_step(running, operands):
        gate_one, up_one, down_one, route_weight = operands
        gate_act = low_back(mult(normed_two, gate_one))
        up_act = low_back(mult(normed_two, up_one))
        acted = low(jax.nn.silu(gate_act) * up_act)
        outputs = low_back(low(mult(acted, down_one)))
        return (running + route_weight[:, None] * outputs, None)
    blended, unused = lax.scan(jax.checkpoint(expert_step), jnp.zeros_like(hidden), (gate_weight, up_weight, down_weight, route_weights.T))
    return hidden + blended

def reference(tokens, segment_ids, routes, cotangent, query_weight, key_weight, value_weight, proj_weight, attn_gain, moe_gain, router_weight, gate_weight, up_weight, down_weight):
    floats = tuple((array_item.astype(jnp.float32) for array_item in (tokens, query_weight, key_weight, value_weight, proj_weight, attn_gain, moe_gain, router_weight, gate_weight, up_weight, down_weight)))

    def wrapped(*primals):
        return forward(primals, segment_ids, routes)
    result, pullback = jax.vjp(wrapped, *floats)
    gradients = pullback(cotangent.astype(jnp.float32))
    return (result.astype(jnp.bfloat16), gradients[0].astype(jnp.bfloat16), gradients[1], gradients[2], gradients[3], gradients[4], gradients[5], gradients[6], gradients[7], gradients[8], gradients[9], gradients[10])
```

```python
import jax
import jax.numpy as jnp
from jax import lax
from jax.sharding import PartitionSpec as P

HEADS = 16
KV_HEADS = 8
HEAD_DIM = 64
TOP = 8


EPS = 1e-06
THETA = 10000.0
MASKED = -1000000000.0


def rope_tables(positions):
    half_dim = HEAD_DIM // 2
    inverse_freq = THETA ** (-(jnp.arange(half_dim).astype(jnp.float32) * 2.0) / HEAD_DIM)
    angles = positions.astype(jnp.float32)[:, None] * inverse_freq[None, :]
    return (jnp.cos(angles), jnp.sin(angles))


def rotate(values, cosine, sine_table):
    half_dim = values.shape[-1] // 2
    leading = values[..., :half_dim]
    trailing = values[..., half_dim:]
    cos_rows = cosine[:, None, :]
    sin_rows = sine_table[:, None, :]
    return jnp.concatenate(
        [leading * cos_rows - trailing * sin_rows, trailing * cos_rows + leading * sin_rows],
        axis=-1,
    )


def unrotate(upstream, cosine, sine_table):
    half_dim = upstream.shape[-1] // 2
    leading = upstream[..., :half_dim]
    trailing = upstream[..., half_dim:]
    cos_rows = cosine[:, None, :]
    sin_rows = sine_table[:, None, :]
    return jnp.concatenate(
        [leading * cos_rows + trailing * sin_rows, trailing * cos_rows - leading * sin_rows],
        axis=-1,
    )


def norm_forward(values, gain_vec):
    inverse = lax.rsqrt(jnp.mean(values * values, axis=-1, keepdims=True) + EPS)
    return (values * inverse * gain_vec, inverse)


def norm_backward(values, inverse, gain_vec, upstream):
    scaled = values * inverse
    grad_gain = jnp.sum(upstream * scaled, axis=0)
    weighted = upstream * gain_vec
    grad_values = inverse * (
        weighted - scaled * jnp.mean(weighted * scaled, axis=-1, keepdims=True)
    )
    return (grad_values, grad_gain)


LINE, SIDE = 4, 2


def on_grid():
    return lax.axis_size("ep") == LINE * SIDE * SIDE and lax.axis_size("tp") == SIDE


def shift_line(array, step):
    count = LINE * SIDE * SIDE
    stride = SIDE * SIDE * step
    return lax.ppermute(array, "ep", [(i, (i + stride) % count) for i in range(count)])


def swap_side(array, bit):
    return lax.ppermute(array, "ep", [(i, i ^ bit) for i in range(LINE * SIDE * SIDE)])


def swap_core(array):
    return lax.ppermute(array, "tp", [(0, 1), (1, 0)])


def add_low(left, right):
    return (left.astype(jnp.float32) + right.astype(jnp.float32)).astype(jnp.bfloat16)


def group_orders():
    members = lax.axis_size("ep")
    if not on_grid():
        return (jnp.arange(members), jnp.arange(members))
    me = lax.axis_index("ep")
    near = me % (SIDE * SIDE)
    line = me // (SIDE * SIDE)
    back = (line - jnp.arange(LINE) + LINE) % LINE * (SIDE * SIDE)
    first = jnp.stack([back + (near ^ flip) for flip in (0, 1, 2, 3)]).reshape(-1)
    second = jnp.stack([back + (near ^ flip) for flip in (0, 2, 1, 3)]).reshape(-1)
    return (first, second)


def gather_group(chunk):
    rows, width = chunk.shape
    half = rows // 2
    if not on_grid():
        whole = lax.all_gather(chunk, "ep", axis=0)
        return (whole[:, :half], whole[:, half:])
    line = [chunk]
    for _ in range(LINE - 1):
        line.append(shift_line(line[-1], 1))
    first = jnp.stack([part[:half] for part in line])
    second = jnp.stack([part[half:] for part in line])
    first = jnp.stack([first, swap_side(first, 1)])
    second = jnp.stack([second, swap_side(second, 2)])
    first = jnp.stack([first, swap_side(first, 2)])
    second = jnp.stack([second, swap_side(second, 1)])
    members = lax.axis_size("ep")
    return (first.reshape(members, half, width), second.reshape(members, half, width))


def scatter_group(first, second):
    members, half, width = first.shape
    if not on_grid():
        whole = jnp.concatenate([first, second], axis=1)
        return lax.psum_scatter(whole, "ep", scatter_dimension=0, tiled=False)
    first = first.reshape(SIDE, SIDE, LINE, half, width)
    second = second.reshape(SIDE, SIDE, LINE, half, width)
    first = add_low(first[0], swap_side(first[1], 2))
    second = add_low(second[0], swap_side(second[1], 1))
    first = add_low(first[0], swap_side(first[1], 1))
    second = add_low(second[0], swap_side(second[1], 2))
    both = jnp.concatenate([first, second], axis=1)
    total = both[LINE - 1]
    for step in range(LINE - 2, 0, -1):
        total = add_low(both[step], shift_line(total, -1))
    return both[0].astype(jnp.float32) + shift_line(total, -1).astype(jnp.float32)


def pick_rows(array, order):
    return jnp.stack(
        [lax.dynamic_index_in_dim(array, order[i], 0, False) for i in range(array.shape[0])]
    )


def undo(order):
    return jnp.argmax(order[None, :] == jnp.arange(order.shape[0])[:, None], axis=1)


def sum_everywhere(array, orders):
    if not on_grid():
        return lax.psum(array, ("ep", "tp"))
    rows, width = array.shape
    members = lax.axis_size("ep")
    core = lax.axis_index("tp")
    low = array.astype(jnp.bfloat16).reshape(SIDE, members, rows // (SIDE * members), width)
    mine = lax.dynamic_index_in_dim(low, core, 0, False)
    other = lax.dynamic_index_in_dim(low, 1 - core, 0, False)
    mine = add_low(mine, swap_core(other))
    half = mine.shape[1] // 2
    total = scatter_group(
        pick_rows(mine[:, :half], orders[0]), pick_rows(mine[:, half:], orders[1])
    ).astype(jnp.bfloat16)
    first, second = gather_group(total)
    whole = jnp.concatenate(
        [pick_rows(first, undo(orders[0])), pick_rows(second, undo(orders[1]))], axis=1
    ).reshape(rows // SIDE, width)
    other = swap_core(whole)
    lower = jnp.where(core == 0, whole, other)
    upper = jnp.where(core == 0, other, whole)
    return jnp.concatenate([lower, upper], axis=0).astype(jnp.float32)


def whole_expert(part, axis):
    if on_grid():
        return jnp.concatenate([part, swap_core(part)], axis=axis)
    return lax.all_gather(part, "tp", axis=axis, tiled=True)


def own_part(grad, axis):
    if on_grid():
        width = grad.shape[axis] // SIDE
        return lax.slice_in_dim(grad, 0, width, axis=axis) + swap_core(
            lax.slice_in_dim(grad, width, 2 * width, axis=axis)
        )
    return lax.psum_scatter(grad, "tp", scatter_dimension=axis, tiled=True)


def expert_all(rows, cots, gates, gate_full, up_full, down_full):
    gate_act = jnp.dot(rows, gate_full, preferred_element_type=jnp.float32)
    up_act = jnp.dot(rows, up_full, preferred_element_type=jnp.float32)
    back = lax.dot_general(
        cots, down_full, (((1,), (1,)), ((), ())), preferred_element_type=jnp.float32
    )
    sigmoid_gate = jax.nn.sigmoid(gate_act)
    silu_gate = gate_act * sigmoid_gate
    acted = (silu_gate * up_act).astype(jnp.bfloat16).astype(jnp.float32)
    grad_gates = jnp.sum(acted * back, axis=1)
    acted_low = (acted * gates[:, None]).astype(jnp.bfloat16)
    grad_acted = back * gates[:, None]
    grad_up_act = (grad_acted * silu_gate).astype(jnp.bfloat16)
    grad_gate_act = (
        grad_acted * up_act * sigmoid_gate * (1.0 + gate_act * (1.0 - sigmoid_gate))
    ).astype(jnp.bfloat16)
    outputs = jnp.dot(acted_low, down_full, preferred_element_type=jnp.float32)
    inner = (((1,), (1,)), ((), ()))
    outer = (((0,), (0,)), ((), ()))
    grad_input = lax.dot_general(
        grad_gate_act, gate_full, inner, preferred_element_type=jnp.float32
    ) + lax.dot_general(grad_up_act, up_full, inner, preferred_element_type=jnp.float32)
    grad_down = lax.dot_general(acted_low, cots, outer, preferred_element_type=jnp.float32)
    grad_gate = lax.dot_general(rows, grad_gate_act, outer, preferred_element_type=jnp.float32)
    grad_up = lax.dot_general(rows, grad_up_act, outer, preferred_element_type=jnp.float32)
    return (
        outputs.astype(jnp.bfloat16),
        grad_input.astype(jnp.bfloat16),
        grad_gates,
        grad_gate,
        grad_up,
        grad_down,
    )


def per_device(
    tokens,
    segment_ids,
    routes,
    cotangent,
    query_weight,
    key_weight,
    value_weight,
    proj_weight,
    attn_gain,
    moe_gain,
    router_weight,
    gate_weight,
    up_weight,
    down_weight,
):
    tok_count = tokens.shape[0]
    model_dim = tokens.shape[1]
    seq_len = segment_ids.shape[1]
    experts = router_weight.shape[1]
    local_experts = gate_weight.shape[0]
    group_size = HEADS // KV_HEADS
    score_scale = HEAD_DIM ** (-0.5)
    first_row = lax.axis_index("tp") * tok_count
    positions = first_row + jnp.arange(tok_count, dtype=jnp.int32)
    cosine, sine_table = rope_tables(positions)
    key_places = jnp.arange(seq_len, dtype=jnp.int32)
    segment_row = segment_ids[0]
    query_segment = lax.dynamic_slice_in_dim(segment_row, first_row, tok_count)
    allowed = (positions[:, None] >= key_places[None, :]) & (
        query_segment[:, None] == segment_row[None, :]
    )
    residual_in = tokens.astype(jnp.float32)
    gain_one = attn_gain.astype(jnp.float32)
    normed_one, inverse_one = norm_forward(residual_in, gain_one)
    normed_low = normed_one.astype(jnp.bfloat16)
    query_raw = jnp.dot(normed_low, query_weight, preferred_element_type=jnp.float32)
    key_raw = jnp.dot(normed_low, key_weight, preferred_element_type=jnp.float32)
    value_low = jnp.dot(normed_low, value_weight, preferred_element_type=jnp.float32).astype(
        jnp.bfloat16
    )
    query_rot = rotate(query_raw.reshape(tok_count, HEADS, HEAD_DIM), cosine, sine_table).astype(
        jnp.bfloat16
    )
    key_rot = rotate(key_raw.reshape(tok_count, KV_HEADS, HEAD_DIM), cosine, sine_table).astype(
        jnp.bfloat16
    )
    key_rot = key_rot.reshape(tok_count, KV_HEADS * HEAD_DIM)
    key_all, value_all = (
        lax.all_gather(key_rot, "tp", axis=0, tiled=True),
        lax.all_gather(value_low, "tp", axis=0, tiled=True),
    )
    query_heads = query_rot.reshape(tok_count, KV_HEADS, group_size, HEAD_DIM).transpose(1, 0, 2, 3)
    key_heads = key_all.reshape(seq_len, KV_HEADS, HEAD_DIM).transpose(1, 0, 2)
    value_heads = value_all.reshape(seq_len, KV_HEADS, HEAD_DIM).transpose(1, 0, 2)

    def attend(operands):
        query_block, key_block, value_block = operands
        scores = (
            jnp.einsum("tgd,sd->gts", query_block, key_block, preferred_element_type=jnp.float32)
            * score_scale
        )
        scores = jnp.where(allowed[None], scores, MASKED)
        highest = jnp.max(scores, axis=-1, keepdims=True)
        exponent = jnp.exp(scores - highest)
        totals = jnp.sum(exponent, axis=-1, keepdims=True)
        soft_weights = (exponent / totals).astype(jnp.bfloat16)
        blended = jnp.einsum(
            "gts,sd->tgd", soft_weights, value_block, preferred_element_type=jnp.float32
        )
        return (blended, (highest + jnp.log(totals))[..., 0])

    blended_heads, log_totals = lax.map(attend, (query_heads, key_heads, value_heads))
    attended = (
        blended_heads.transpose(1, 0, 2, 3)
        .reshape(tok_count, HEADS * HEAD_DIM)
        .astype(jnp.bfloat16)
    )
    projected = jnp.dot(attended, proj_weight, preferred_element_type=jnp.float32)
    hidden_one = residual_in + projected
    gain_two = moe_gain.astype(jnp.float32)
    normed_two, inverse_two = norm_forward(hidden_one, gain_two)
    moe_input = normed_two.astype(jnp.bfloat16)
    logits = jnp.dot(moe_input, router_weight, preferred_element_type=jnp.float32)
    chosen = (routes[:, :, None] == jnp.arange(experts, dtype=jnp.int32)[None, None, :]).astype(
        jnp.float32
    )
    picked = jnp.sum(chosen * logits[:, None, :], axis=-1)
    gate_probs = jax.nn.softmax(picked, axis=-1)
    members = lax.axis_size("ep")
    half = tok_count // 2
    orders = group_orders()
    named = jnp.sum(jnp.left_shift(1, routes), axis=1).astype(jnp.int32)
    named_all = lax.all_gather(named, "ep", axis=0)
    named_all = jnp.concatenate(
        [
            pick_rows(named_all[:, :half], orders[0]).reshape(-1),
            pick_rows(named_all[:, half:], orders[1]).reshape(-1),
        ]
    )
    gate_full = whole_expert(gate_weight[0], 1)
    up_full = whole_expert(up_weight[0], 1)
    down_full = whole_expert(down_weight[0], 0)
    cots = jnp.concatenate([part.reshape(-1, model_dim) for part in gather_group(cotangent)])
    rows = jnp.concatenate([part.reshape(-1, model_dim) for part in gather_group(moe_input)])
    rows_logits = jnp.dot(rows, router_weight, preferred_element_type=jnp.float32)
    expert_ids = jnp.arange(experts, dtype=jnp.int32)
    has = (jnp.right_shift(named_all[:, None], expert_ids[None, :]) & 1) == 1
    rows_logits = jnp.where(has, rows_logits, -jnp.inf)
    weight = jnp.exp(rows_logits - jnp.max(rows_logits, axis=1, keepdims=True))
    mine = expert_ids[None, :] == lax.axis_index("ep")
    gates = jnp.sum(jnp.where(mine, weight, 0.0), axis=1) / jnp.sum(weight, axis=1)
    outputs, grad_inputs, grad_gates, grad_gate, grad_up, grad_down = expert_all(
        rows, cots, gates, gate_full, up_full, down_full
    )

    def halves(array):
        split = array.shape[0] // 2
        shape = (members, half) + array.shape[1:]
        return (array[:split].reshape(shape), array[split:].reshape(shape))

    blended = scatter_group(*halves(outputs))
    layer_out = (hidden_one + blended.astype(jnp.float32)).astype(jnp.bfloat16)
    grad_rows_in = scatter_group(*halves(grad_inputs)).astype(jnp.float32)
    gates_first, gates_second = halves(grad_gates)
    grad_gates_all = jnp.concatenate(
        [pick_rows(gates_first, undo(orders[0])), pick_rows(gates_second, undo(orders[1]))], axis=1
    )
    grad_gates_own = lax.all_to_all(grad_gates_all, "ep", split_axis=0, concat_axis=0, tiled=True)
    upstream = cotangent.astype(jnp.float32)
    grad_gate_probs = jnp.sum(chosen * grad_gates_own.T[:, None, :], axis=-1)
    grad_picked = gate_probs * (
        grad_gate_probs - jnp.sum(gate_probs * grad_gate_probs, axis=-1, keepdims=True)
    )
    grad_logits = jnp.sum(grad_picked[:, :, None] * chosen, axis=1).astype(jnp.bfloat16)
    grad_router = jnp.dot(moe_input.T, grad_logits, preferred_element_type=jnp.float32)
    grad_normed_two = jnp.dot(grad_logits, router_weight.T, preferred_element_type=jnp.float32)
    grad_normed_two = grad_normed_two + grad_rows_in
    grad_hidden_norm, grad_gain_two = norm_backward(
        hidden_one, inverse_two, gain_two, grad_normed_two
    )
    grad_hidden = upstream + grad_hidden_norm
    grad_branch = grad_hidden.astype(jnp.bfloat16)
    grad_proj = jnp.dot(attended.T, grad_branch, preferred_element_type=jnp.float32)
    grad_attended = jnp.dot(grad_branch, proj_weight.T, preferred_element_type=jnp.float32).astype(
        jnp.bfloat16
    )
    grad_heads = grad_attended.reshape(tok_count, KV_HEADS, group_size, HEAD_DIM).transpose(
        1, 0, 2, 3
    )

    def attend_back(operands):
        query_block, key_block, value_block, grad_block, log_block = operands
        scores = (
            jnp.einsum("tgd,sd->gts", query_block, key_block, preferred_element_type=jnp.float32)
            * score_scale
        )
        scores = jnp.where(allowed[None], scores, MASKED)
        soft_weights = jnp.exp(scores - log_block[..., None])
        soft_low = soft_weights.astype(jnp.bfloat16)
        grad_value_block = jnp.einsum(
            "gts,tgd->sd", soft_low, grad_block, preferred_element_type=jnp.float32
        )
        grad_soft = jnp.einsum(
            "tgd,sd->gts", grad_block, value_block, preferred_element_type=jnp.float32
        )
        row_delta = jnp.sum(soft_weights * grad_soft, axis=-1, keepdims=True)
        grad_scores = (soft_weights * (grad_soft - row_delta)).astype(jnp.bfloat16)
        grad_query_block = (
            jnp.einsum("gts,sd->tgd", grad_scores, key_block, preferred_element_type=jnp.float32)
            * score_scale
        )
        grad_key_block = (
            jnp.einsum("gts,tgd->sd", grad_scores, query_block, preferred_element_type=jnp.float32)
            * score_scale
        )
        return (grad_query_block, grad_key_block, grad_value_block)

    grad_query_heads, grad_key_heads, grad_value_heads = lax.map(
        attend_back, (query_heads, key_heads, value_heads, grad_heads, log_totals)
    )
    grad_key_rows = grad_key_heads.transpose(1, 0, 2).reshape(seq_len, KV_HEADS * HEAD_DIM)
    grad_value_rows = grad_value_heads.transpose(1, 0, 2).reshape(seq_len, KV_HEADS * HEAD_DIM)
    grad_key_own, grad_value_own = (
        lax.psum_scatter(
            grad_key_rows.astype(jnp.bfloat16), "tp", scatter_dimension=0, tiled=True
        ).astype(jnp.float32),
        lax.psum_scatter(
            grad_value_rows.astype(jnp.bfloat16), "tp", scatter_dimension=0, tiled=True
        ).astype(jnp.float32),
    )
    grad_key_rot = lax.optimization_barrier(grad_key_own.astype(jnp.bfloat16)).astype(jnp.float32)
    grad_key_raw = unrotate(grad_key_rot.reshape(tok_count, KV_HEADS, HEAD_DIM), cosine, sine_table)
    grad_key_raw = grad_key_raw.astype(jnp.bfloat16).reshape(tok_count, KV_HEADS * HEAD_DIM)
    grad_value_low = grad_value_own.astype(jnp.bfloat16)
    grad_query_rot = grad_query_heads.transpose(1, 0, 2, 3).reshape(tok_count, HEADS, HEAD_DIM)
    grad_query_rot = lax.optimization_barrier(grad_query_rot.astype(jnp.bfloat16)).astype(
        jnp.float32
    )
    grad_query_raw = (
        unrotate(grad_query_rot, cosine, sine_table)
        .astype(jnp.bfloat16)
        .reshape(tok_count, HEADS * HEAD_DIM)
    )
    grad_query = jnp.dot(normed_low.T, grad_query_raw, preferred_element_type=jnp.float32)
    grad_key = jnp.dot(normed_low.T, grad_key_raw, preferred_element_type=jnp.float32)
    grad_value = jnp.dot(normed_low.T, grad_value_low, preferred_element_type=jnp.float32)
    grad_normed_one = jnp.dot(grad_query_raw, query_weight.T, preferred_element_type=jnp.float32)
    grad_normed_one = grad_normed_one + jnp.dot(
        grad_key_raw, key_weight.T, preferred_element_type=jnp.float32
    )
    grad_normed_one = grad_normed_one + jnp.dot(
        grad_value_low, value_weight.T, preferred_element_type=jnp.float32
    )
    grad_input_norm, grad_gain_one = norm_backward(
        residual_in, inverse_one, gain_one, grad_normed_one
    )
    grad_tokens = (grad_hidden + grad_input_norm).astype(jnp.bfloat16)
    pad = jnp.zeros((model_dim, 128 - experts - 1), jnp.float32)
    early = sum_everywhere(
        jnp.concatenate([grad_proj, grad_router, grad_gain_two[:, None], pad], axis=1), orders
    )
    pad = jnp.zeros((model_dim, 127), jnp.float32)
    late = sum_everywhere(
        jnp.concatenate([grad_query, grad_key, grad_value, grad_gain_one[:, None], pad], axis=1),
        orders,
    )
    query_end = HEADS * HEAD_DIM
    key_end = query_end + KV_HEADS * HEAD_DIM
    value_end = key_end + KV_HEADS * HEAD_DIM
    return (
        layer_out,
        grad_tokens,
        late[:, :query_end],
        late[:, query_end:key_end],
        late[:, key_end:value_end],
        early[:, :model_dim],
        late[:, value_end],
        early[:, model_dim + experts],
        early[:, model_dim : model_dim + experts],
        own_part(grad_gate, 1)[None],
        own_part(grad_up, 1)[None],
        own_part(grad_down, 0)[None],
    )


def solution(mesh):
    placed = (
        P(("ep", "tp"), None),
        P("ep", None),
        P(("ep", "tp"), None),
        P(("ep", "tp"), None),
        P(),
        P(),
        P(),
        P(),
        P(),
        P(),
        P(),
        P("ep", None, "tp"),
        P("ep", None, "tp"),
        P("ep", "tp", None),
    )
    return jax.shard_map(
        per_device,
        mesh=mesh,
        in_specs=placed,
        out_specs=(
            P(("ep", "tp"), None),
            P(("ep", "tp"), None),
            P(),
            P(),
            P(),
            P(),
            P(),
            P(),
            P(),
            P("ep", None, "tp"),
            P("ep", None, "tp"),
            P("ep", "tp", None),
        ),
        check_vma=False,
    )
```

```python
import jax
import jax.numpy as jnp
import numpy as np
from jax import lax
from jax.experimental import pallas as pl
from jax.experimental.pallas import tpu as pltpu
from jax.sharding import PartitionSpec as P

HEADS = 16
KV_HEADS = 8
HEAD_DIM = 64
GROUP = HEADS // KV_HEADS
LANES = 128

EPS = 1e-06
THETA = 10000.0
MASKED = -1000000000.0


LINE, SIDE = 4, 2
BF, F32 = jnp.bfloat16, jnp.float32
INNER = (((1,), (1,)), ((), ()))
OUTER = (((0,), (0,)), ((), ()))
VMEM_LIMIT = 60 * 1024 * 1024


def on_grid():
    return lax.axis_size("ep") == LINE * SIDE * SIDE and lax.axis_size("tp") == SIDE


def shift_line(array, step):
    count = LINE * SIDE * SIDE
    stride = SIDE * SIDE * step
    return lax.ppermute(array, "ep", [(i, (i + stride) % count) for i in range(count)])


def swap_side(array, bit):
    return lax.ppermute(array, "ep", [(i, i ^ bit) for i in range(LINE * SIDE * SIDE)])


def swap_core(array):
    return lax.ppermute(array, "tp", [(0, 1), (1, 0)])


def add_low(*arrays):
    return sum(array.astype(F32) for array in arrays).astype(BF)


def group_orders():
    members = lax.axis_size("ep")
    if not on_grid():
        return (list(range(members)), list(range(members)))
    me = lax.axis_index("ep")
    near = lax.rem(me, SIDE * SIDE)
    back = [lax.rem(me - near + (LINE - k) * SIDE * SIDE, members) for k in range(LINE)]
    sides = [lax.bitwise_xor(near, flip) for flip in range(SIDE * SIDE)]
    first = [b + sides[flip] for flip in (0, 1, 2, 3) for b in back]
    second = [b + sides[flip] for flip in (0, 2, 1, 3) for b in back]
    return (first, second)


def group_places():
    members = lax.axis_size("ep")
    if not on_grid():
        return (list(range(members)), list(range(members)))
    me = lax.axis_index("ep")
    near = lax.rem(me, SIDE * SIDE)
    line = lax.div(me, SIDE * SIDE)
    first, second = [], []
    for member in range(members):
        far = lax.rem(line - member // (SIDE * SIDE) + LINE, LINE)
        flip = lax.bitwise_xor(near, member % (SIDE * SIDE))
        turned = lax.div(flip, SIDE) + SIDE * lax.rem(flip, SIDE)
        first.append(flip * LINE + far)
        second.append(turned * LINE + far)
    return (first, second)


def gather_group(chunk):
    rows, width = chunk.shape
    half = rows // 2
    if not on_grid():
        whole = lax.all_gather(chunk, "ep", axis=0)
        return (whole[:, :half], whole[:, half:])
    line = [chunk] + [shift_line(chunk, step) for step in range(1, LINE)]
    first = jnp.stack([part[:half] for part in line])
    second = jnp.stack([part[half:] for part in line])
    first = jnp.stack([first, swap_side(first, 1)])
    second = jnp.stack([second, swap_side(second, 2)])
    first = jnp.stack([first, swap_side(first, 2)])
    second = jnp.stack([second, swap_side(second, 1)])
    members = lax.axis_size("ep")
    return (first.reshape(members, half, width), second.reshape(members, half, width))


def scatter_group(first, second):
    members, half, width = first.shape
    if not on_grid():
        whole = jnp.concatenate([first, second], axis=1)
        return lax.psum_scatter(whole, "ep", scatter_dimension=0, tiled=False).astype(F32)
    first = first.reshape(SIDE, SIDE, LINE, half, width)
    second = second.reshape(SIDE, SIDE, LINE, half, width)
    first = add_low(first[0], swap_side(first[1], 2))
    second = add_low(second[0], swap_side(second[1], 1))
    first = add_low(first[0], swap_side(first[1], 1))
    second = add_low(second[0], swap_side(second[1], 2))
    both = jnp.concatenate([first, second], axis=1)
    parts = [both[0]] + [shift_line(both[step], -step) for step in range(1, LINE)]
    return sum(part.astype(F32) for part in parts)


def pick_rows(array, order):
    return jnp.stack([lax.dynamic_index_in_dim(array, place, 0, False) for place in order])


def sum_everywhere(low, orders, places):
    if not on_grid():
        return lax.psum(low.astype(F32), ("ep", "tp"))
    rows, width = low.shape
    members = lax.axis_size("ep")
    core = lax.axis_index("tp")
    low = low.reshape(SIDE, members, rows // (SIDE * members), width)
    mine = lax.dynamic_index_in_dim(low, core, 0, False)
    other = lax.dynamic_index_in_dim(low, 1 - core, 0, False)
    mine = add_low(mine, swap_core(other))
    half = mine.shape[1] // 2
    total = scatter_group(
        pick_rows(mine[:, :half], orders[0]), pick_rows(mine[:, half:], orders[1])
    ).astype(BF)
    first, second = gather_group(total)
    whole = jnp.concatenate(
        [pick_rows(first, places[0]), pick_rows(second, places[1])], axis=1
    ).reshape(rows // SIDE, width)
    other = swap_core(whole)
    lower = jnp.where(core == 0, whole, other)
    upper = jnp.where(core == 0, other, whole)
    return jnp.concatenate([lower, upper], axis=0).astype(F32)


def whole_expert(part, axis):
    if on_grid():
        return jnp.concatenate([part, swap_core(part)], axis=axis)
    return lax.all_gather(part, "tp", axis=axis, tiled=True)


def own_part(grad, axis):
    if on_grid():
        width = grad.shape[axis] // SIDE
        return lax.slice_in_dim(grad, 0, width, axis=axis) + swap_core(
            lax.slice_in_dim(grad, width, 2 * width, axis=axis)
        )
    return lax.psum_scatter(grad, "tp", scatter_dimension=axis, tiled=True)


def rope_tables(seq_len):
    half_dim = HEAD_DIM // 2
    freq = THETA ** (-(np.arange(half_dim, dtype=np.float64) * 2.0) / HEAD_DIM)
    angles = np.arange(seq_len, dtype=np.float64)[:, None] * freq[None, :]
    cosine, sine = np.cos(angles), np.sin(angles)
    repeats = LANES // HEAD_DIM
    cosine = np.tile(np.concatenate([cosine, cosine], axis=1), (1, repeats))
    sine = np.tile(np.concatenate([-sine, sine], axis=1), (1, repeats))
    return (cosine.astype(np.float32), sine.astype(np.float32))


def swap_halves(values):
    lane = lax.broadcasted_iota(jnp.int32, values.shape, 1)
    leading = lax.rem(lane, HEAD_DIM) < HEAD_DIM // 2
    half = HEAD_DIM // 2
    return jnp.where(
        leading, pltpu.roll(values, LANES - half, 1), pltpu.roll(values, half, 1)
    )


def blocks(width):
    return [slice(start, start + LANES) for start in range(0, width, LANES)]


def head_slice(index):
    return slice(index * HEAD_DIM, (index + 1) * HEAD_DIM)


def call(kernel, out_shape, name, flops, nbytes, **options):
    return pl.pallas_call(
        kernel,
        out_shape=out_shape,
        name=name,
        compiler_params=pltpu.CompilerParams(vmem_limit_bytes=VMEM_LIMIT),
        cost_estimate=pl.CostEstimate(flops=flops, bytes_accessed=nbytes, transcendentals=0),
        **options,
    )


def project_kernel(
    tok_ref, gain_ref, wq_ref, wk_ref, wv_ref, cos_ref, sin_ref, norm_ref, q_ref, kv_ref
):
    values = tok_ref[...].astype(F32)
    inverse = lax.rsqrt(jnp.mean(values * values, axis=1, keepdims=True) + EPS)
    normed = (values * inverse * gain_ref[...].astype(F32)).astype(BF)
    norm_ref[...] = normed
    cosine, sine = cos_ref[...], sin_ref[...]
    query = jnp.dot(normed, wq_ref[...], preferred_element_type=F32)
    for cols in blocks(query.shape[1]):
        part = query[:, cols]
        q_ref[:, cols] = (part * cosine + swap_halves(part) * sine).astype(BF)
    key = jnp.dot(normed, wk_ref[...], preferred_element_type=F32)
    for cols in blocks(key.shape[1]):
        part = key[:, cols]
        kv_ref[:, cols] = (part * cosine + swap_halves(part) * sine).astype(BF)
    value = jnp.dot(normed, wv_ref[...], preferred_element_type=F32)
    kv_ref[:, key.shape[1] :] = value.astype(BF)


def pair_rows(ref, group):
    left = ref[:, head_slice(GROUP * group)]
    right = ref[:, head_slice(GROUP * group + 1)]
    return jnp.concatenate([left, right], axis=0)


def pair_columns(values):
    rows = values.shape[0] // GROUP
    return jnp.concatenate([values[:rows], values[rows:]], axis=1)


def allowed_pairs(qinfo_ref, kinfo_ref):
    qpos, qseg = qinfo_ref[:, 0:1], qinfo_ref[:, 1:2]
    kpos, kseg = kinfo_ref[0:1, :], kinfo_ref[1:2, :]
    allowed = jnp.where((qpos >= kpos) & (qseg == kseg), 1.0, 0.0)
    return jnp.concatenate([allowed] * GROUP, axis=0) > 0.5


def gate_rows(logits, has):
    has = has > 0
    logits = jnp.where(has, logits, -jnp.inf)
    weight = jnp.exp(logits - jnp.max(logits, axis=1, keepdims=True))
    return weight / jnp.sum(weight, axis=1, keepdims=True)


def attend_kernel(
    q_ref, kv_ref, qinfo_ref, kinfo_ref, wp_ref, tok_ref, gain_ref, router_ref, has_ref,
    att_ref, lse_ref, hid_ref, moe_ref, gates_ref,
):
    allowed = allowed_pairs(qinfo_ref, kinfo_ref)
    rows = q_ref.shape[0]
    lane = lax.broadcasted_iota(jnp.int32, (rows, LANES), 1)
    kept = jnp.zeros((rows, LANES), F32)
    for group in range(KV_HEADS):
        query = pair_rows(q_ref, group)
        key = kv_ref[:, head_slice(group)]
        value = kv_ref[:, head_slice(KV_HEADS + group)]
        scores = lax.dot_general(query, key, INNER, preferred_element_type=F32)
        scores = jnp.where(allowed, scores * HEAD_DIM ** (-0.5), MASKED)
        highest = jnp.max(scores, axis=1, keepdims=True)
        exponent = jnp.exp(scores - highest)
        totals = jnp.sum(exponent, axis=1, keepdims=True)
        probs = (exponent / totals).astype(BF)
        blended = jnp.dot(probs, value, preferred_element_type=F32)
        cols = slice(group * GROUP * HEAD_DIM, (group + 1) * GROUP * HEAD_DIM)
        att_ref[:, cols] = pair_columns(blended).astype(BF)
        log_total = highest + jnp.log(totals)
        for which in range(GROUP):
            column = log_total[which * rows : (which + 1) * rows]
            kept = jnp.where(lane == GROUP * group + which, column, kept)
    lse_ref[...] = kept
    hidden = tok_ref[...].astype(F32) + jnp.dot(
        att_ref[...], wp_ref[...], preferred_element_type=F32
    )
    hid_ref[...] = hidden
    inverse = lax.rsqrt(jnp.mean(hidden * hidden, axis=1, keepdims=True) + EPS)
    normed = (hidden * inverse * gain_ref[...].astype(F32)).astype(BF)
    moe_ref[...] = normed
    logits = jnp.dot(normed, router_ref[...], preferred_element_type=F32)
    gates_ref[...] = gate_rows(logits, has_ref[...])


def expert_kernel(
    rows_ref, cots_ref, wg_ref, wu_ref, wd_ref, router_ref, mine_ref,
    out_ref, gin_ref, dgate_ref, gg_ref, gu_ref, gd_ref,
):
    width = rows_ref.shape[1]
    rows = rows_ref[...]
    cots = cots_ref[:, :width]
    logits = jnp.dot(rows, router_ref[...], preferred_element_type=F32)
    gates = gate_rows(logits, cots_ref[:, width:])
    gates = jnp.sum(gates * mine_ref[...], axis=1, keepdims=True)
    gate_act = jnp.dot(rows, wg_ref[...], preferred_element_type=F32)
    up_act = jnp.dot(rows, wu_ref[...], preferred_element_type=F32)
    back = lax.dot_general(cots, wd_ref[...], INNER, preferred_element_type=F32)
    sigmoid_gate = 1.0 / (1.0 + jnp.exp(-gate_act))
    silu_gate = gate_act * sigmoid_gate
    acted = (silu_gate * up_act).astype(BF).astype(F32)
    product = acted * back
    coarse = product.astype(BF)
    fine = (product - coarse.astype(F32)).astype(BF)
    ones = jnp.ones((8, product.shape[1]), BF)
    dgate_ref[...] = lax.dot_general(
        ones, coarse, INNER, preferred_element_type=F32
    ) + lax.dot_general(ones, fine, INNER, preferred_element_type=F32)
    acted_low = (acted * gates).astype(BF)
    grad_acted = back * gates
    grad_up_act = (grad_acted * silu_gate).astype(BF)
    grad_gate_act = (
        grad_acted * up_act * sigmoid_gate * (1.0 + gate_act * (1.0 - sigmoid_gate))
    ).astype(BF)
    out_ref[...] = jnp.dot(acted_low, wd_ref[...], preferred_element_type=F32).astype(BF)
    gin_ref[...] = (
        lax.dot_general(grad_gate_act, wg_ref[...], INNER, preferred_element_type=F32)
        + lax.dot_general(grad_up_act, wu_ref[...], INNER, preferred_element_type=F32)
    ).astype(BF)
    grad_down = lax.dot_general(acted_low, cots, OUTER, preferred_element_type=F32)
    grad_gate = lax.dot_general(rows, grad_gate_act, OUTER, preferred_element_type=F32)
    grad_up = lax.dot_general(rows, grad_up_act, OUTER, preferred_element_type=F32)

    @pl.when(pl.program_id(0) == 0)
    def _():
        gd_ref[...] = grad_down
        gg_ref[...] = grad_gate
        gu_ref[...] = grad_up

    @pl.when(pl.program_id(0) > 0)
    def _():
        gd_ref[...] += grad_down
        gg_ref[...] += grad_gate
        gu_ref[...] += grad_up


def run_expert(rows, cots, wg, wu, wd, router, mine):
    count, width = rows.shape
    wide = cots.shape[1]
    hidden = wg.shape[1]
    block = min(512, count)

    def whole(array):
        return pl.BlockSpec(array.shape, lambda i: (0,) * array.ndim)

    def by_rows(columns):
        return pl.BlockSpec((block, columns), lambda i: (i, 0))

    def fixed(shape):
        return pl.BlockSpec(shape, lambda i: (0, 0))

    return call(
        expert_kernel,
        (
            jax.ShapeDtypeStruct((count, width), BF),
            jax.ShapeDtypeStruct((count, width), BF),
            jax.ShapeDtypeStruct((8, count), F32),
            jax.ShapeDtypeStruct((width, hidden), F32),
            jax.ShapeDtypeStruct((width, hidden), F32),
            jax.ShapeDtypeStruct((hidden, width), F32),
        ),
        "expert",
        18 * count * width * hidden,
        8 * count * width + 18 * width * hidden,
        grid=(count // block,),
        in_specs=[
            by_rows(width), by_rows(wide), whole(wg), whole(wu), whole(wd), whole(router),
            whole(mine),
        ],
        out_specs=[
            by_rows(width), by_rows(width), pl.BlockSpec((8, block), lambda i: (0, i)),
            fixed((width, hidden)), fixed((width, hidden)), fixed((hidden, width)),
        ],
    )(rows, cots, wg, wu, wd, router, mine)


def column_sums(product):
    coarse = product.astype(BF)
    fine = (product - coarse.astype(F32)).astype(BF)
    ones = jnp.ones((product.shape[0], LANES), BF)
    return lax.dot_general(coarse, ones, OUTER, preferred_element_type=F32) + lax.dot_general(
        fine, ones, OUTER, preferred_element_type=F32
    )


def branch_kernel(
    gin_ref, hid_ref, gain_ref, cot_ref, gates_ref, dgate_ref, router_ref, moe_ref, att_ref,
    wp_ref, ghid_ref, gatt_ref, pay_ref,
):
    gates, dgate = gates_ref[...], dgate_ref[...]
    total = jnp.sum(gates * dgate, axis=1, keepdims=True)
    grad_logits = (gates * (dgate - total)).astype(BF)
    upstream = gin_ref[...] + lax.dot_general(
        grad_logits, router_ref[...], INNER, preferred_element_type=F32
    )
    hidden = hid_ref[...]
    inverse = lax.rsqrt(jnp.mean(hidden * hidden, axis=1, keepdims=True) + EPS)
    scaled = hidden * inverse
    product = upstream * scaled
    weighted = upstream * gain_ref[...].astype(F32)
    mean = jnp.mean(weighted * scaled, axis=1, keepdims=True)
    grad_hidden = cot_ref[...].astype(F32) + inverse * (weighted - scaled * mean)
    ghid_ref[...] = grad_hidden
    grad_branch = grad_hidden.astype(BF)
    gatt_ref[...] = lax.dot_general(
        grad_branch, wp_ref[...], INNER, preferred_element_type=F32
    ).astype(BF)
    width = hidden.shape[1]
    pay_ref[:, :width] = lax.dot_general(
        att_ref[...], grad_branch, OUTER, preferred_element_type=F32
    ).astype(BF)
    grad_router = lax.dot_general(moe_ref[...], grad_logits, OUTER, preferred_element_type=F32)
    lane = lax.broadcasted_iota(jnp.int32, grad_router.shape, 1)
    pay_ref[:, width:] = jnp.where(lane == LANES - 1, column_sums(product), grad_router).astype(BF)


def attend_back_kernel(
    gatt_ref, q_ref, kv_ref, lse_ref, qinfo_ref, kinfo_ref, cos_ref, sin_ref, gq_ref, gkv_ref
):
    allowed = allowed_pairs(qinfo_ref, kinfo_ref)
    cosine, sine = cos_ref[...], sin_ref[...]
    kept = lse_ref[...]
    scale = HEAD_DIM ** (-0.5)
    for pair in range(KV_HEADS // 2):
        grad_keys, grad_values = [], []
        for group in (2 * pair, 2 * pair + 1):
            query = pair_rows(q_ref, group)
            grad = pair_rows(gatt_ref, group)
            key = kv_ref[:, head_slice(group)]
            value = kv_ref[:, head_slice(KV_HEADS + group)]
            log_total = jnp.concatenate(
                [kept[:, GROUP * group + i : GROUP * group + i + 1] for i in range(GROUP)], axis=0
            )
            scores = lax.dot_general(query, key, INNER, preferred_element_type=F32)
            scores = jnp.where(allowed, scores * scale, MASKED)
            probs = jnp.exp(scores - log_total)
            grad_values.append(
                lax.dot_general(probs.astype(BF), grad, OUTER, preferred_element_type=F32)
            )
            grad_probs = lax.dot_general(grad, value, INNER, preferred_element_type=F32)
            delta = jnp.sum(probs * grad_probs, axis=1, keepdims=True)
            grad_scores = (probs * (grad_probs - delta)).astype(BF)
            grad_query = jnp.dot(grad_scores, key, preferred_element_type=F32) * scale
            grad_query = pair_columns(grad_query).astype(BF).astype(F32)
            cols = slice(group * GROUP * HEAD_DIM, (group + 1) * GROUP * HEAD_DIM)
            gq_ref[:, cols] = (grad_query * cosine - swap_halves(grad_query) * sine).astype(BF)
            grad_keys.append(
                lax.dot_general(grad_scores, query, OUTER, preferred_element_type=F32) * scale
            )
        cols = slice(pair * LANES, (pair + 1) * LANES)
        gkv_ref[:, cols] = jnp.concatenate(grad_keys, axis=1).astype(BF)
        shift = KV_HEADS * HEAD_DIM
        cols = slice(shift + pair * LANES, shift + (pair + 1) * LANES)
        gkv_ref[:, cols] = jnp.concatenate(grad_values, axis=1).astype(BF)


def project_back_kernel(
    norm_ref, gq_ref, gkv_ref, cos_ref, sin_ref, wq_ref, wk_ref, wv_ref, tok_ref, gain_ref,
    ghid_ref, gtok_ref, pay_ref, gkraw_ref,
):
    cosine, sine = cos_ref[...], sin_ref[...]
    kwidth = wk_ref.shape[1]
    for cols in blocks(kwidth):
        part = gkv_ref[:, cols].astype(F32)
        gkraw_ref[:, cols] = (part * cosine - swap_halves(part) * sine).astype(BF)
    grad_query, grad_key, grad_value = gq_ref[...], gkraw_ref[...], gkv_ref[:, kwidth:]
    upstream = lax.dot_general(grad_query, wq_ref[...], INNER, preferred_element_type=F32)
    upstream += lax.dot_general(grad_key, wk_ref[...], INNER, preferred_element_type=F32)
    upstream += lax.dot_general(grad_value, wv_ref[...], INNER, preferred_element_type=F32)
    normed = norm_ref[...]
    start = 0
    for grad in (grad_query, grad_key, grad_value):
        pay_ref[:, start : start + grad.shape[1]] = lax.dot_general(
            normed, grad, OUTER, preferred_element_type=F32
        ).astype(BF)
        start += grad.shape[1]
    values = tok_ref[...].astype(F32)
    inverse = lax.rsqrt(jnp.mean(values * values, axis=1, keepdims=True) + EPS)
    scaled = values * inverse
    pay_ref[:, start:] = column_sums(upstream * scaled).astype(BF)
    weighted = upstream * gain_ref[...].astype(F32)
    mean = jnp.mean(weighted * scaled, axis=1, keepdims=True)
    gtok_ref[...] = (ghid_ref[...] + inverse * (weighted - scaled * mean)).astype(BF)


def sds(shape, dtype):
    return jax.ShapeDtypeStruct(shape, dtype)


def per_device(
    tokens,
    segment_ids,
    routes,
    cotangent,
    query_weight,
    key_weight,
    value_weight,
    proj_weight,
    attn_gain,
    moe_gain,
    router_weight,
    gate_weight,
    up_weight,
    down_weight,
):
    tok_count, model_dim = tokens.shape
    seq_len = segment_ids.shape[1]
    experts = router_weight.shape[1]
    members = lax.axis_size("ep")
    cores = lax.axis_size("tp")
    query_dim, kv_dim = HEADS * HEAD_DIM, KV_HEADS * HEAD_DIM
    half = tok_count // 2
    core = lax.axis_index("tp")
    first_row = core * tok_count
    orders, places = group_orders(), group_places()

    has = (routes[:, :, None] == jnp.arange(LANES, dtype=jnp.int32)[None, None, :]).any(axis=1)
    has = has.astype(BF)
    sent_cots = jnp.concatenate([cotangent, has], axis=1)
    cots = jnp.concatenate(
        [part.reshape(-1, model_dim + LANES) for part in gather_group(sent_cots)]
    )
    wg = whole_expert(gate_weight[0], 1)
    wu = whole_expert(up_weight[0], 1)
    wd = whole_expert(down_weight[0], 0)

    cos_table, sin_table = rope_tables(seq_len)
    cosine = lax.dynamic_slice_in_dim(jnp.asarray(cos_table), first_row, tok_count)
    sine = lax.dynamic_slice_in_dim(jnp.asarray(sin_table), first_row, tok_count)
    gain_one, gain_two = attn_gain[None, :], moe_gain[None, :]
    router = jnp.pad(router_weight, ((0, 0), (0, LANES - experts)))

    normed, query, kv = call(
        project_kernel,
        (
            sds((tok_count, model_dim), BF),
            sds((tok_count, query_dim), BF),
            sds((tok_count, 2 * kv_dim), BF),
        ),
        "project",
        4 * tok_count * model_dim * model_dim,
        5 * model_dim * model_dim,
    )(tokens, gain_one, query_weight, key_weight, value_weight, cosine, sine)

    own_pos = first_row + jnp.arange(tok_count, dtype=jnp.int32)
    segment_row = segment_ids[0]
    own_seg = lax.dynamic_slice_in_dim(segment_row, first_row, tok_count)
    qinfo = jnp.stack([own_pos, own_seg], axis=1)
    if on_grid():
        kv_all = jnp.concatenate([kv, swap_core(kv)], axis=0)
        other_row = (1 - core) * tok_count
        other_seg = lax.dynamic_slice_in_dim(segment_row, other_row, tok_count)
        other_pos = other_row + jnp.arange(tok_count, dtype=jnp.int32)
        kinfo = jnp.stack(
            [jnp.concatenate([own_pos, other_pos]), jnp.concatenate([own_seg, other_seg])]
        )
    else:
        kv_all = lax.all_gather(kv, "tp", axis=0, tiled=True)
        kinfo = jnp.stack([jnp.arange(seq_len, dtype=jnp.int32), segment_row])

    attended, log_totals, hidden, moe_input, gates = call(
        attend_kernel,
        (
            sds((tok_count, query_dim), BF),
            sds((tok_count, LANES), F32),
            sds((tok_count, model_dim), F32),
            sds((tok_count, model_dim), BF),
            sds((tok_count, LANES), F32),
        ),
        "attend",
        4 * tok_count * model_dim * model_dim,
        5 * model_dim * model_dim,
    )(query, kv_all, qinfo, kinfo, proj_weight, tokens, gain_two, router, has)

    rows = jnp.concatenate([part.reshape(-1, model_dim) for part in gather_group(moe_input)])
    mine = (jnp.arange(LANES, dtype=jnp.int32) == lax.axis_index("ep")).astype(F32)[None, :]
    outputs, grad_inputs, grad_gates, grad_gate, grad_up, grad_down = run_expert(
        rows, cots, wg, wu, wd, router, mine
    )

    def halves(array):
        split = array.shape[0] // 2
        shape = (members, half) + array.shape[1:]
        return (array[:split].reshape(shape), array[split:].reshape(shape))

    grad_rows_in = scatter_group(*halves(grad_inputs))
    first, second = halves(grad_gates[0])
    grad_gates = jnp.concatenate(
        [pick_rows(first, places[0]), pick_rows(second, places[1])], axis=1
    )
    grad_gates = lax.all_to_all(grad_gates, "ep", split_axis=0, concat_axis=0, tiled=True)
    grad_gates = jnp.pad(grad_gates.T, ((0, 0), (0, LANES - experts)))
    blended = scatter_group(*halves(outputs))
    layer_out = (hidden + blended).astype(BF)

    grad_hidden, grad_attended, early = call(
        branch_kernel,
        (
            sds((tok_count, model_dim), F32),
            sds((tok_count, query_dim), BF),
            sds((model_dim, model_dim + LANES), BF),
        ),
        "branch",
        4 * tok_count * model_dim * model_dim,
        5 * model_dim * model_dim,
    )(
        grad_rows_in, hidden, gain_two, cotangent, gates, grad_gates, router, moe_input, attended,
        proj_weight,
    )
    early = sum_everywhere(early, orders, places)

    grad_query, grad_kv = call(
        attend_back_kernel,
        (sds((tok_count, query_dim), BF), sds((seq_len, 2 * kv_dim), BF)),
        "attend_back",
        4 * tok_count * model_dim * model_dim,
        5 * model_dim * model_dim,
    )(grad_attended, query, kv_all, log_totals, qinfo, kinfo, cosine, sine)
    if on_grid():
        grad_kv = add_low(grad_kv[:tok_count], swap_core(grad_kv[tok_count:]))
    else:
        grad_kv = lax.psum_scatter(grad_kv, "tp", scatter_dimension=0, tiled=True)

    grad_tokens, late = call(
        project_back_kernel,
        (
            sds((tok_count, model_dim), BF),
            sds((model_dim, query_dim + 2 * kv_dim + LANES), BF),
        ),
        "project_back",
        8 * tok_count * model_dim * model_dim,
        9 * model_dim * model_dim,
        scratch_shapes=[pltpu.VMEM((tok_count, kv_dim), BF)],
    )(
        normed, grad_query, grad_kv, cosine, sine, query_weight, key_weight, value_weight, tokens,
        gain_one, grad_hidden,
    )
    late = sum_everywhere(late, orders, places)
    key_end = query_dim + kv_dim
    value_end = key_end + kv_dim
    return (
        layer_out,
        grad_tokens,
        late[:, :query_dim],
        late[:, query_dim:key_end],
        late[:, key_end:value_end],
        early[:, :model_dim],
        late[:, value_end],
        early[:, model_dim + LANES - 1],
        early[:, model_dim : model_dim + experts],
        own_part(grad_gate, 1)[None],
        own_part(grad_up, 1)[None],
        own_part(grad_down, 0)[None],
    )


def solution(mesh):
    placed = (
        P(("ep", "tp"), None),
        P("ep", None),
        P(("ep", "tp"), None),
        P(("ep", "tp"), None),
        P(),
        P(),
        P(),
        P(),
        P(),
        P(),
        P(),
        P("ep", None, "tp"),
        P("ep", None, "tp"),
        P("ep", "tp", None),
    )
    return jax.shard_map(
        per_device,
        mesh=mesh,
        in_specs=placed,
        out_specs=(
            P(("ep", "tp"), None),
            P(("ep", "tp"), None),
            P(),
            P(),
            P(),
            P(),
            P(),
            P(),
            P(),
            P("ep", None, "tp"),
            P("ep", None, "tp"),
            P("ep", "tp", None),
        ),
        check_vma=False,
    )
```

```python
import functools

import jax
import jax.numpy as jnp
import numpy as np
from jax import lax
from jax.experimental import pallas as pl
from jax.experimental.pallas import tpu as pltpu
from jax.sharding import PartitionSpec as P

HEADS = 16
KV_HEADS = 8
HEAD_DIM = 64
GROUP = HEADS // KV_HEADS
LANES = 128

EPS = 1e-06
THETA = 10000.0
MASKED = -1000000000.0


LINE, SIDE = 4, 2
NEAR, FAR = 4, 8
HALF_LANES = LANES // 2
BF, F32 = jnp.bfloat16, jnp.float32
INNER = (((1,), (1,)), ((), ()))
OUTER = (((0,), (0,)), ((), ()))
VMEM_LIMIT = 60 * 1024 * 1024


def on_grid():
    return lax.axis_size("ep") == LINE * SIDE * SIDE and lax.axis_size("tp") == SIDE


def shift_line(array, step):
    count = LINE * SIDE * SIDE
    stride = SIDE * SIDE * step
    return lax.ppermute(array, "ep", [(i, (i + stride) % count) for i in range(count)])


def swap_side(array, bit):
    return lax.ppermute(array, "ep", [(i, i ^ bit) for i in range(LINE * SIDE * SIDE)])


def swap_core(array):
    return lax.ppermute(array, "tp", [(0, 1), (1, 0)])


def add_low(*arrays):
    return sum(array.astype(F32) for array in arrays).astype(BF)


def group_orders():
    members = lax.axis_size("ep")
    if not on_grid():
        return (list(range(members)), list(range(members)))
    me = lax.axis_index("ep")
    near = lax.rem(me, SIDE * SIDE)
    back = [lax.rem(me - near + (LINE - k) * SIDE * SIDE, members) for k in range(LINE)]
    sides = [lax.bitwise_xor(near, flip) for flip in range(SIDE * SIDE)]
    first = [b + sides[flip] for flip in (0, 1, 2, 3) for b in back]
    second = [b + sides[flip] for flip in (0, 2, 1, 3) for b in back]
    return (first, second)


def group_places():
    members = lax.axis_size("ep")
    if not on_grid():
        return (list(range(members)), list(range(members)))
    me = lax.axis_index("ep")
    near = lax.rem(me, SIDE * SIDE)
    line = lax.div(me, SIDE * SIDE)
    first, second = [], []
    for member in range(members):
        far = lax.rem(line - member // (SIDE * SIDE) + LINE, LINE)
        flip = lax.bitwise_xor(near, member % (SIDE * SIDE))
        turned = lax.div(flip, SIDE) + SIDE * lax.rem(flip, SIDE)
        first.append(flip * LINE + far)
        second.append(turned * LINE + far)
    return (first, second)


def gather_sum(chunk):
    rows, width = chunk.shape
    half = rows // 2
    line = [chunk] + [shift_line(chunk, step) for step in range(1, LINE)]
    first = jnp.stack([part[:half] for part in line])
    second = jnp.stack([part[half:] for part in line])
    first = jnp.stack([first, swap_side(first, 1)])
    second = jnp.stack([second, swap_side(second, 2)])
    first = jnp.stack([first, swap_side(first, 2)])
    second = jnp.stack([second, swap_side(second, 1)])
    members = lax.axis_size("ep")
    return (first.reshape(members, half, width), second.reshape(members, half, width))


def scatter_sum(first, second):
    members, half, width = first.shape
    first = first.reshape(SIDE, SIDE, LINE, half, width)
    second = second.reshape(SIDE, SIDE, LINE, half, width)
    first = add_low(first[0], swap_side(first[1], 2))
    second = add_low(second[0], swap_side(second[1], 1))
    first = add_low(first[0], swap_side(first[1], 1))
    second = add_low(second[0], swap_side(second[1], 2))
    both = jnp.concatenate([first, second], axis=1)
    parts = [both[0]] + [shift_line(both[step], -step) for step in range(1, LINE)]
    return sum(part.astype(F32) for part in parts)


def gather_rows(chunk):
    rows, width = chunk.shape
    if not on_grid():
        whole = lax.all_gather(chunk, "ep", axis=0, tiled=True)
        block = min(512, whole.shape[0])
        return [[whole[i : i + block]] for i in range(0, whole.shape[0], block)]
    half = rows // 2
    far = swap_side(chunk, FAR)
    near, away = [], []
    for rest, bits in ((slice(0, half), (1, 2)), (slice(half, rows), (2, 1))):
        part = jnp.concatenate([chunk[rest], far[rest]])
        part = jnp.concatenate([part, swap_side(part, bits[0])])
        near.append(part)
        away.append(swap_side(part, bits[1]))
    return [near, away]


def scatter_rows(blocks):
    if not on_grid():
        whole = jnp.concatenate([array for part in blocks for array in part])
        return (lax.psum_scatter(whole, "ep", scatter_dimension=0, tiled=True), None)
    near, away = blocks
    mine, theirs = [], []
    for own, sent, bits in ((near[0], away[0], (1, 2)), (near[1], away[1], (2, 1))):
        other = swap_side(sent, bits[1])
        count = own.shape[0] // 2
        far = swap_side(add_low(own[count:], other[count:]), bits[0])
        kept = add_low(own[:count], other[:count])
        count //= 2
        theirs.append(add_low(kept[count:], far[count:]))
        mine.append(add_low(kept[:count], far[:count]))
    return (jnp.concatenate(mine), swap_side(jnp.concatenate(theirs), FAR))


def pick_rows(array, order):
    return jnp.stack([lax.dynamic_index_in_dim(array, place, 0, False) for place in order])


def sum_everywhere(low, orders, places):
    if not on_grid():
        return lax.psum(low.astype(F32), ("ep", "tp"))
    rows, width = low.shape
    members = lax.axis_size("ep")
    core = lax.axis_index("tp")
    low = low.reshape(SIDE, members, rows // (SIDE * members), width)
    mine = lax.dynamic_index_in_dim(low, core, 0, False)
    other = lax.dynamic_index_in_dim(low, 1 - core, 0, False)
    mine = add_low(mine, swap_core(other))
    half = mine.shape[1] // 2
    total = scatter_sum(
        pick_rows(mine[:, :half], orders[0]), pick_rows(mine[:, half:], orders[1])
    ).astype(BF)
    first, second = gather_sum(total)
    whole = jnp.concatenate(
        [pick_rows(first, places[0]), pick_rows(second, places[1])], axis=1
    ).reshape(rows // SIDE, width)
    other = swap_core(whole)
    lower = jnp.where(core == 0, whole, other)
    upper = jnp.where(core == 0, other, whole)
    return jnp.concatenate([lower, upper], axis=0).astype(F32)


def expert_pieces(weights, axes):
    if not on_grid():
        whole = [lax.all_gather(w, "tp", axis=axis, tiled=True) for w, axis in zip(weights, axes)]
        return ([whole], (0,))
    near = [swap_side(w, NEAR) for w in weights]
    across = [swap_core(w) for w in weights]
    return ([list(weights), across, near, [swap_core(w) for w in near]], (0, 0, 1, 1))


def rope_tables(seq_len):
    half_dim = HEAD_DIM // 2
    freq = THETA ** (-(np.arange(half_dim, dtype=np.float64) * 2.0) / HEAD_DIM)
    angles = np.arange(seq_len, dtype=np.float64)[:, None] * freq[None, :]
    cosine, sine = np.cos(angles), np.sin(angles)
    repeats = LANES // HEAD_DIM
    cosine = np.tile(np.concatenate([cosine, cosine], axis=1), (1, repeats))
    sine = np.tile(np.concatenate([-sine, sine], axis=1), (1, repeats))
    return (cosine.astype(np.float32), sine.astype(np.float32))


def swap_halves(values):
    lane = lax.broadcasted_iota(jnp.int32, values.shape, 1)
    leading = lax.rem(lane, HEAD_DIM) < HEAD_DIM // 2
    half = HEAD_DIM // 2
    return jnp.where(
        leading, pltpu.roll(values, LANES - half, 1), pltpu.roll(values, half, 1)
    )


def blocks(width):
    return [slice(start, start + LANES) for start in range(0, width, LANES)]


def head_slice(index):
    return slice(index * HEAD_DIM, (index + 1) * HEAD_DIM)


def call(kernel, out_shape, name, flops, nbytes, **options):
    return pl.pallas_call(
        kernel,
        out_shape=out_shape,
        name=name,
        compiler_params=pltpu.CompilerParams(vmem_limit_bytes=VMEM_LIMIT),
        cost_estimate=pl.CostEstimate(flops=flops, bytes_accessed=nbytes, transcendentals=0),
        **options,
    )


def project_kernel(
    tok_ref, gain_ref, wq_ref, wk_ref, wv_ref, cos_ref, sin_ref, norm_ref, q_ref, kv_ref
):
    values = tok_ref[...].astype(F32)
    inverse = lax.rsqrt(jnp.mean(values * values, axis=1, keepdims=True) + EPS)
    normed = (values * inverse * gain_ref[...].astype(F32)).astype(BF)
    norm_ref[...] = normed
    cosine, sine = cos_ref[...], sin_ref[...]
    query = jnp.dot(normed, wq_ref[...], preferred_element_type=F32)
    for cols in blocks(query.shape[1]):
        part = query[:, cols]
        q_ref[:, cols] = (part * cosine + swap_halves(part) * sine).astype(BF)
    key = jnp.dot(normed, wk_ref[...], preferred_element_type=F32)
    for cols in blocks(key.shape[1]):
        part = key[:, cols]
        kv_ref[:, cols] = (part * cosine + swap_halves(part) * sine).astype(BF)
    value = jnp.dot(normed, wv_ref[...], preferred_element_type=F32)
    kv_ref[:, key.shape[1] :] = value.astype(BF)


def pair_rows(ref, group):
    left = ref[:, head_slice(GROUP * group)]
    right = ref[:, head_slice(GROUP * group + 1)]
    return jnp.concatenate([left, right], axis=0)


def pair_columns(values):
    rows = values.shape[0] // GROUP
    return jnp.concatenate([values[:rows], values[rows:]], axis=1)


def allowed_pairs(qinfo_ref, kinfo_ref):
    qpos, qseg = qinfo_ref[:, 0:1], qinfo_ref[:, 1:2]
    kpos, kseg = kinfo_ref[0:1, :], kinfo_ref[1:2, :]
    allowed = jnp.where((qpos >= kpos) & (qseg == kseg), 1.0, 0.0)
    return jnp.concatenate([allowed] * GROUP, axis=0) > 0.5


def gate_rows(logits, has):
    has = has > 0
    logits = jnp.where(has, logits, -jnp.inf)
    weight = jnp.exp(logits - jnp.max(logits, axis=1, keepdims=True))
    return weight / jnp.sum(weight, axis=1, keepdims=True)


def attend_kernel(
    q_ref, kv_ref, qinfo_ref, kinfo_ref, wp_ref, tok_ref, gain_ref, router_ref, has_ref,
    att_ref, lse_ref, hid_ref, moe_ref, gates_ref,
):
    allowed = allowed_pairs(qinfo_ref, kinfo_ref)
    rows = q_ref.shape[0]
    lane = lax.broadcasted_iota(jnp.int32, (rows, LANES), 1)
    kept = jnp.zeros((rows, LANES), F32)
    for group in range(KV_HEADS):
        query = pair_rows(q_ref, group)
        key = kv_ref[:, head_slice(group)]
        value = kv_ref[:, head_slice(KV_HEADS + group)]
        scores = lax.dot_general(query, key, INNER, preferred_element_type=F32)
        scores = jnp.where(allowed, scores * HEAD_DIM ** (-0.5), MASKED)
        highest = jnp.max(scores, axis=1, keepdims=True)
        exponent = jnp.exp(scores - highest)
        totals = jnp.sum(exponent, axis=1, keepdims=True)
        probs = (exponent / totals).astype(BF)
        blended = jnp.dot(probs, value, preferred_element_type=F32)
        cols = slice(group * GROUP * HEAD_DIM, (group + 1) * GROUP * HEAD_DIM)
        att_ref[:, cols] = pair_columns(blended).astype(BF)
        log_total = highest + jnp.log(totals)
        for which in range(GROUP):
            column = log_total[which * rows : (which + 1) * rows]
            kept = jnp.where(lane == GROUP * group + which, column, kept)
    lse_ref[...] = kept
    hidden = tok_ref[...].astype(F32) + jnp.dot(
        att_ref[...], wp_ref[...], preferred_element_type=F32
    )
    hid_ref[...] = hidden
    inverse = lax.rsqrt(jnp.mean(hidden * hidden, axis=1, keepdims=True) + EPS)
    normed = (hidden * inverse * gain_ref[...].astype(F32)).astype(BF)
    moe_ref[...] = normed
    logits = jnp.dot(normed, router_ref[...], preferred_element_type=F32)
    gates_ref[...] = gate_rows(logits, has_ref[...])


def expert_kernel(count, slots, *refs):
    pieces = len(slots)
    row_refs, cot_refs = refs[:count], refs[count : 2 * count]
    weight_refs = refs[2 * count : 2 * count + 3 * pieces]
    router_ref, mine_ref = refs[2 * count + 3 * pieces : 2 * count + 3 * pieces + 2]
    results = refs[2 * count + 3 * pieces + 2 :]
    for block in range(count):
        out_ref, gin_ref, act_ref, gga_ref, gua_ref = results[block::count]
        rows = row_refs[block][...]
        width = rows.shape[1]
        cots = cot_refs[block][:, :width]
        logits = jnp.dot(rows, router_ref[...], preferred_element_type=F32)
        gates = gate_rows(logits, cot_refs[block][:, width:])
        lane = lax.broadcasted_iota(jnp.int32, gates.shape, 1)
        out = gin = None
        gate_grads = [None] * (1 + max(slots))
        for piece, slot in enumerate(slots):
            wg_ref, wu_ref, wd_ref = weight_refs[3 * piece : 3 * piece + 3]
            gate = jnp.sum(gates * mine_ref[slot : slot + 1, :], axis=1, keepdims=True)
            gate_act = jnp.dot(rows, wg_ref[...], preferred_element_type=F32)
            up_act = jnp.dot(rows, wu_ref[...], preferred_element_type=F32)
            back = lax.dot_general(cots, wd_ref[...], INNER, preferred_element_type=F32)
            sigmoid_gate = 1.0 / (1.0 + jnp.exp(-gate_act))
            silu_gate = gate_act * sigmoid_gate
            acted = (silu_gate * up_act).astype(BF).astype(F32)
            part = jnp.sum(acted * back, axis=1, keepdims=True)
            gate_grads[slot] = part if gate_grads[slot] is None else gate_grads[slot] + part
            acted_low = (acted * gate).astype(BF)
            grad_acted = back * gate
            grad_up_act = (grad_acted * silu_gate).astype(BF)
            grad_gate_act = (
                grad_acted * up_act * sigmoid_gate * (1.0 + gate_act * (1.0 - sigmoid_gate))
            ).astype(BF)
            hidden = wg_ref.shape[1]
            cols = slice(piece * hidden, (piece + 1) * hidden)
            act_ref[:, cols], gga_ref[:, cols], gua_ref[:, cols] = (
                acted_low, grad_gate_act, grad_up_act,
            )
            part = jnp.dot(acted_low, wd_ref[...], preferred_element_type=F32)
            out = part if out is None else out + part
            part = lax.dot_general(
                grad_gate_act, wg_ref[...], INNER, preferred_element_type=F32
            ) + lax.dot_general(grad_up_act, wu_ref[...], INNER, preferred_element_type=F32)
            gin = part if gin is None else gin + part
        out_ref[...] = out.astype(BF)
        gin_ref[:, :width] = gin.astype(BF)
        kept = jnp.zeros(gates.shape, F32)
        for slot, grad in enumerate(gate_grads):
            coarse = grad.astype(BF).astype(F32)
            chosen = mine_ref[slot : slot + 1, :]
            kept += coarse * chosen + (grad - coarse) * pltpu.roll(
                jnp.broadcast_to(chosen, gates.shape), HALF_LANES, 1
            )
        gin_ref[:, width:] = kept.astype(BF)


def run_expert(rows, cots, pieces, slots, router, mine):
    count = len(rows)
    width, hidden = pieces[0][0].shape
    total = sum(part.shape[0] for part in rows)
    wide = hidden * len(pieces)
    columns = (width, width + LANES, wide, wide, wide)
    out = call(
        functools.partial(expert_kernel, count, slots),
        [sds((part.shape[0], cols), BF) for cols in columns for part in rows],
        "expert",
        12 * total * width * wide,
        6 * width * wide + 10 * total * width,
    )(*rows, *cots, *[w for piece in pieces for w in piece], router, mine)
    return [out[i * count : (i + 1) * count] for i in range(len(columns))]


def weights_kernel(count, slots, hidden, *refs):
    rows, cots, acts, ggas, guas = (
        [ref for ref in refs[i * count : (i + 1) * count]] for i in range(5)
    )
    results = refs[5 * count :]
    width = rows[0].shape[1]

    def tall(parts, cols):
        return jnp.concatenate([ref[:, cols] for ref in parts], axis=0)

    rows = tall(rows, slice(0, width))
    cots = tall(cots, slice(0, width))
    for piece in range(len(slots)):
        cols = slice(piece * hidden, (piece + 1) * hidden)
        gate = lax.dot_general(rows, tall(ggas, cols), OUTER, preferred_element_type=F32)
        up = lax.dot_general(rows, tall(guas, cols), OUTER, preferred_element_type=F32)
        down = lax.dot_general(tall(acts, cols), cots, OUTER, preferred_element_type=F32)
        if piece % 2:
            wide_ref, tall_ref = results[-2:]
            at = (piece // 2) * 2 * hidden
            wide_ref[:, at : at + hidden] = gate.astype(BF)
            wide_ref[:, at + hidden : at + 2 * hidden] = up.astype(BF)
            at = (piece // 2) * hidden
            tall_ref[at : at + hidden, :] = down.astype(BF)
        else:
            gate_ref, up_ref, down_ref = results[3 * (piece // 2) : 3 * (piece // 2) + 3]
            gate_ref[...], up_ref[...], down_ref[...] = gate, up, down


def weight_grads(rows, cots, acts, ggas, guas, slots):
    count = len(rows)
    width = rows[0].shape[1]
    wide = acts[0].shape[1]
    hidden = wide // len(slots)
    total = sum(part.shape[0] for part in rows)
    shapes = []
    for piece in range(0, len(slots), 2):
        shapes += [sds((width, hidden), F32), sds((width, hidden), F32), sds((hidden, width), F32)]
    if len(slots) > 1:
        shapes += [sds((width, wide), BF), sds((wide // 2, width), BF)]
    out = call(
        functools.partial(weights_kernel, count, slots, hidden),
        shapes,
        "weight_grads",
        6 * total * width * wide,
        12 * width * wide + 4 * total * (width + wide),
    )(*rows, *cots, *acts, *ggas, *guas)
    if not on_grid():
        return [
            lax.psum_scatter(grad, "tp", scatter_dimension=axis, tiled=True)
            for grad, axis in zip(out, (1, 1, 0))
        ]
    wide_part, tall_part = swap_core(out[6]), swap_core(out[7])
    slabs = [wide_part[:, i * hidden : (i + 1) * hidden] for i in range(4)]
    near_wide = jnp.concatenate([out[3] + slabs[2], out[4] + slabs[3]], axis=1).astype(BF)
    near_tall = (out[5] + tall_part[hidden:]).astype(BF)
    near_wide, near_tall = swap_side(near_wide, NEAR), swap_side(near_tall, NEAR)
    return [
        out[0] + slabs[0] + near_wide[:, :hidden],
        out[1] + slabs[1] + near_wide[:, hidden:],
        out[2] + tall_part[:hidden] + near_tall,
    ]


def column_sums(product):
    coarse = product.astype(BF)
    fine = (product - coarse.astype(F32)).astype(BF)
    ones = jnp.ones((product.shape[0], LANES), BF)
    return lax.dot_general(coarse, ones, OUTER, preferred_element_type=F32) + lax.dot_general(
        fine, ones, OUTER, preferred_element_type=F32
    )


def branch_kernel(
    gin_refs, hid_ref, gain_ref, cot_ref, gates_ref, router_ref, moe_ref, att_ref, wp_ref,
    ghid_ref, gatt_ref, pay_ref,
):
    width = hid_ref.shape[1]
    gates = gates_ref[...]
    grads = sum(ref[:, :width].astype(F32) for ref in gin_refs)
    dgate = sum(ref[:, width:].astype(F32) for ref in gin_refs)
    dgate = dgate + pltpu.roll(dgate, HALF_LANES, 1)
    total = jnp.sum(gates * dgate, axis=1, keepdims=True)
    grad_logits = (gates * (dgate - total)).astype(BF)
    upstream = grads + lax.dot_general(
        grad_logits, router_ref[...], INNER, preferred_element_type=F32
    )
    hidden = hid_ref[...]
    inverse = lax.rsqrt(jnp.mean(hidden * hidden, axis=1, keepdims=True) + EPS)
    scaled = hidden * inverse
    product = upstream * scaled
    weighted = upstream * gain_ref[...].astype(F32)
    mean = jnp.mean(weighted * scaled, axis=1, keepdims=True)
    grad_hidden = cot_ref[...].astype(F32) + inverse * (weighted - scaled * mean)
    ghid_ref[...] = grad_hidden
    grad_branch = grad_hidden.astype(BF)
    gatt_ref[...] = lax.dot_general(
        grad_branch, wp_ref[...], INNER, preferred_element_type=F32
    ).astype(BF)
    pay_ref[:, :width] = lax.dot_general(
        att_ref[...], grad_branch, OUTER, preferred_element_type=F32
    ).astype(BF)
    grad_router = lax.dot_general(moe_ref[...], grad_logits, OUTER, preferred_element_type=F32)
    lane = lax.broadcasted_iota(jnp.int32, grad_router.shape, 1)
    pay_ref[:, width:] = jnp.where(lane == LANES - 1, column_sums(product), grad_router).astype(BF)


def attend_back_kernel(
    gatt_ref, q_ref, kv_ref, lse_ref, qinfo_ref, kinfo_ref, cos_ref, sin_ref, gq_ref, gkv_ref
):
    allowed = allowed_pairs(qinfo_ref, kinfo_ref)
    cosine, sine = cos_ref[...], sin_ref[...]
    kept = lse_ref[...]
    scale = HEAD_DIM ** (-0.5)
    for pair in range(KV_HEADS // 2):
        grad_keys, grad_values = [], []
        for group in (2 * pair, 2 * pair + 1):
            query = pair_rows(q_ref, group)
            grad = pair_rows(gatt_ref, group)
            key = kv_ref[:, head_slice(group)]
            value = kv_ref[:, head_slice(KV_HEADS + group)]
            log_total = jnp.concatenate(
                [kept[:, GROUP * group + i : GROUP * group + i + 1] for i in range(GROUP)], axis=0
            )
            scores = lax.dot_general(query, key, INNER, preferred_element_type=F32)
            scores = jnp.where(allowed, scores * scale, MASKED)
            probs = jnp.exp(scores - log_total)
            grad_values.append(
                lax.dot_general(probs.astype(BF), grad, OUTER, preferred_element_type=F32)
            )
            grad_probs = lax.dot_general(grad, value, INNER, preferred_element_type=F32)
            delta = jnp.sum(probs * grad_probs, axis=1, keepdims=True)
            grad_scores = (probs * (grad_probs - delta)).astype(BF)
            grad_query = jnp.dot(grad_scores, key, preferred_element_type=F32) * scale
            grad_query = pair_columns(grad_query).astype(BF).astype(F32)
            cols = slice(group * GROUP * HEAD_DIM, (group + 1) * GROUP * HEAD_DIM)
            gq_ref[:, cols] = (grad_query * cosine - swap_halves(grad_query) * sine).astype(BF)
            grad_keys.append(
                lax.dot_general(grad_scores, query, OUTER, preferred_element_type=F32) * scale
            )
        cols = slice(pair * LANES, (pair + 1) * LANES)
        gkv_ref[:, cols] = jnp.concatenate(grad_keys, axis=1).astype(BF)
        shift = KV_HEADS * HEAD_DIM
        cols = slice(shift + pair * LANES, shift + (pair + 1) * LANES)
        gkv_ref[:, cols] = jnp.concatenate(grad_values, axis=1).astype(BF)


def project_back_kernel(
    norm_ref, gq_ref, gkv_ref, cos_ref, sin_ref, wq_ref, wk_ref, wv_ref, tok_ref, gain_ref,
    ghid_ref, gtok_ref, pay_ref, gkraw_ref,
):
    cosine, sine = cos_ref[...], sin_ref[...]
    kwidth = wk_ref.shape[1]
    for cols in blocks(kwidth):
        part = gkv_ref[:, cols].astype(F32)
        gkraw_ref[:, cols] = (part * cosine - swap_halves(part) * sine).astype(BF)
    grad_query, grad_key, grad_value = gq_ref[...], gkraw_ref[...], gkv_ref[:, kwidth:]
    upstream = lax.dot_general(grad_query, wq_ref[...], INNER, preferred_element_type=F32)
    upstream += lax.dot_general(grad_key, wk_ref[...], INNER, preferred_element_type=F32)
    upstream += lax.dot_general(grad_value, wv_ref[...], INNER, preferred_element_type=F32)
    normed = norm_ref[...]
    start = 0
    for grad in (grad_query, grad_key, grad_value):
        pay_ref[:, start : start + grad.shape[1]] = lax.dot_general(
            normed, grad, OUTER, preferred_element_type=F32
        ).astype(BF)
        start += grad.shape[1]
    values = tok_ref[...].astype(F32)
    inverse = lax.rsqrt(jnp.mean(values * values, axis=1, keepdims=True) + EPS)
    scaled = values * inverse
    pay_ref[:, start:] = column_sums(upstream * scaled).astype(BF)
    weighted = upstream * gain_ref[...].astype(F32)
    mean = jnp.mean(weighted * scaled, axis=1, keepdims=True)
    gtok_ref[...] = (ghid_ref[...] + inverse * (weighted - scaled * mean)).astype(BF)


def sds(shape, dtype):
    return jax.ShapeDtypeStruct(shape, dtype)


def per_device(
    tokens,
    segment_ids,
    routes,
    cotangent,
    query_weight,
    key_weight,
    value_weight,
    proj_weight,
    attn_gain,
    moe_gain,
    router_weight,
    gate_weight,
    up_weight,
    down_weight,
):
    tok_count, model_dim = tokens.shape
    seq_len = segment_ids.shape[1]
    experts = router_weight.shape[1]
    query_dim, kv_dim = HEADS * HEAD_DIM, KV_HEADS * HEAD_DIM
    core = lax.axis_index("tp")
    first_row = core * tok_count
    orders, places = group_orders(), group_places()

    has = (routes[:, :, None] == jnp.arange(LANES, dtype=jnp.int32)[None, None, :]).any(axis=1)
    has = has.astype(BF)
    cots = gather_rows(jnp.concatenate([cotangent, has], axis=1))
    pieces, slots = expert_pieces((gate_weight[0], up_weight[0], down_weight[0]), (1, 1, 0))

    cos_table, sin_table = rope_tables(seq_len)
    cosine = lax.dynamic_slice_in_dim(jnp.asarray(cos_table), first_row, tok_count)
    sine = lax.dynamic_slice_in_dim(jnp.asarray(sin_table), first_row, tok_count)
    gain_one, gain_two = attn_gain[None, :], moe_gain[None, :]
    router = jnp.pad(router_weight, ((0, 0), (0, LANES - experts)))

    normed, query, kv = call(
        project_kernel,
        (
            sds((tok_count, model_dim), BF),
            sds((tok_count, query_dim), BF),
            sds((tok_count, 2 * kv_dim), BF),
        ),
        "project",
        4 * tok_count * model_dim * model_dim,
        5 * model_dim * model_dim,
    )(tokens, gain_one, query_weight, key_weight, value_weight, cosine, sine)

    own_pos = first_row + jnp.arange(tok_count, dtype=jnp.int32)
    segment_row = segment_ids[0]
    own_seg = lax.dynamic_slice_in_dim(segment_row, first_row, tok_count)
    qinfo = jnp.stack([own_pos, own_seg], axis=1)
    if on_grid():
        kv_all = jnp.concatenate([kv, swap_core(kv)], axis=0)
        other_row = (1 - core) * tok_count
        other_seg = lax.dynamic_slice_in_dim(segment_row, other_row, tok_count)
        other_pos = other_row + jnp.arange(tok_count, dtype=jnp.int32)
        kinfo = jnp.stack(
            [jnp.concatenate([own_pos, other_pos]), jnp.concatenate([own_seg, other_seg])]
        )
    else:
        kv_all = lax.all_gather(kv, "tp", axis=0, tiled=True)
        kinfo = jnp.stack([jnp.arange(seq_len, dtype=jnp.int32), segment_row])

    attended, log_totals, hidden, moe_input, gates = call(
        attend_kernel,
        (
            sds((tok_count, query_dim), BF),
            sds((tok_count, LANES), F32),
            sds((tok_count, model_dim), F32),
            sds((tok_count, model_dim), BF),
            sds((tok_count, LANES), F32),
        ),
        "attend",
        4 * tok_count * model_dim * model_dim,
        5 * model_dim * model_dim,
    )(query, kv_all, qinfo, kinfo, proj_weight, tokens, gain_two, router, has)

    rows = gather_rows(moe_input)
    own = lax.axis_index("ep")
    owned = jnp.stack([lax.bitwise_xor(own, NEAR * slot) for slot in range(1 + max(slots))])
    mine = (jnp.arange(LANES, dtype=jnp.int32)[None, :] == owned[:, None]).astype(F32)
    done = [run_expert(*part, pieces, slots, router, mine) for part in zip(rows, cots)]
    outputs, grad_inputs, acts, ggas, guas = zip(*done)
    grad_rows_in = scatter_rows(grad_inputs)

    def flat(blocks):
        return [array for part in blocks for array in part]

    grad_gate, grad_up, grad_down = weight_grads(
        flat(rows), flat(cots), flat(acts), flat(ggas), flat(guas), slots
    )
    blended = [part for part in scatter_rows(outputs) if part is not None]
    layer_out = (hidden + sum(part.astype(F32) for part in blended)).astype(BF)

    grad_hidden, grad_attended, early = call(
        branch_kernel,
        (
            sds((tok_count, model_dim), F32),
            sds((tok_count, query_dim), BF),
            sds((model_dim, model_dim + LANES), BF),
        ),
        "branch",
        4 * tok_count * model_dim * model_dim,
        5 * model_dim * model_dim,
    )(
        [part for part in grad_rows_in if part is not None], hidden, gain_two, cotangent, gates,
        router, moe_input, attended, proj_weight,
    )
    early = sum_everywhere(early, orders, places)

    grad_query, grad_kv = call(
        attend_back_kernel,
        (sds((tok_count, query_dim), BF), sds((seq_len, 2 * kv_dim), BF)),
        "attend_back",
        4 * tok_count * model_dim * model_dim,
        5 * model_dim * model_dim,
    )(grad_attended, query, kv_all, log_totals, qinfo, kinfo, cosine, sine)
    if on_grid():
        grad_kv = add_low(grad_kv[:tok_count], swap_core(grad_kv[tok_count:]))
    else:
        grad_kv = lax.psum_scatter(grad_kv, "tp", scatter_dimension=0, tiled=True)

    grad_tokens, late = call(
        project_back_kernel,
        (
            sds((tok_count, model_dim), BF),
            sds((model_dim, query_dim + 2 * kv_dim + LANES), BF),
        ),
        "project_back",
        8 * tok_count * model_dim * model_dim,
        9 * model_dim * model_dim,
        scratch_shapes=[pltpu.VMEM((tok_count, kv_dim), BF)],
    )(
        normed, grad_query, grad_kv, cosine, sine, query_weight, key_weight, value_weight, tokens,
        gain_one, grad_hidden,
    )
    late = sum_everywhere(late, orders, places)
    key_end = query_dim + kv_dim
    value_end = key_end + kv_dim
    return (
        layer_out,
        grad_tokens,
        late[:, :query_dim],
        late[:, query_dim:key_end],
        late[:, key_end:value_end],
        early[:, :model_dim],
        late[:, value_end],
        early[:, model_dim + LANES - 1],
        early[:, model_dim : model_dim + experts],
        grad_gate[None],
        grad_up[None],
        grad_down[None],
    )


def solution(mesh):
    placed = (
        P(("ep", "tp"), None),
        P("ep", None),
        P(("ep", "tp"), None),
        P(("ep", "tp"), None),
        P(),
        P(),
        P(),
        P(),
        P(),
        P(),
        P(),
        P("ep", None, "tp"),
        P("ep", None, "tp"),
        P("ep", "tp", None),
    )
    return jax.shard_map(
        per_device,
        mesh=mesh,
        in_specs=placed,
        out_specs=(
            P(("ep", "tp"), None),
            P(("ep", "tp"), None),
            P(),
            P(),
            P(),
            P(),
            P(),
            P(),
            P(),
            P("ep", None, "tp"),
            P("ep", None, "tp"),
            P("ep", "tp", None),
        ),
        check_vma=False,
    )
```

```python
import functools

import jax
import jax.numpy as jnp
import numpy as np
from jax import lax
from jax.experimental import pallas as pl
from jax.experimental.pallas import tpu as pltpu
from jax.sharding import PartitionSpec as P


HEADS = 16
KV_HEADS = 8
HEAD_DIM = 64
GROUP = HEADS // KV_HEADS
LANES = 128

EPS = 1e-06
THETA = 10000.0
MASKED = -1000000000.0


LINE, SIDE = 4, 2
NEAR, FAR = 4, 8
HALF_LANES = LANES // 2
BF, F32 = jnp.bfloat16, jnp.float32
INNER = (((1,), (1,)), ((), ()))
OUTER = (((0,), (0,)), ((), ()))
VMEM_LIMIT = 60 * 1024 * 1024


def on_grid():
    return lax.axis_size("ep") == LINE * SIDE * SIDE and lax.axis_size("tp") == SIDE


def shift_line(array, step):
    count = LINE * SIDE * SIDE
    stride = SIDE * SIDE * step
    return lax.ppermute(array, "ep", [(i, (i + stride) % count) for i in range(count)])


def swap_side(array, bit):
    return lax.ppermute(array, "ep", [(i, i ^ bit) for i in range(LINE * SIDE * SIDE)])


def swap_core(array):
    return lax.ppermute(array, "tp", [(0, 1), (1, 0)])


def add_low(*arrays):
    return sum(array.astype(F32) for array in arrays).astype(BF)


def group_orders():
    me = lax.axis_index("ep")
    near = lax.rem(me, SIDE * SIDE)
    members = LINE * SIDE * SIDE
    back = [lax.rem(me - near + (LINE - k) * SIDE * SIDE, members) for k in range(LINE)]
    sides = [lax.bitwise_xor(near, flip) for flip in range(SIDE * SIDE)]
    first = [b + sides[flip] for flip in (0, 1, 2, 3) for b in back]
    second = [b + sides[flip] for flip in (0, 2, 1, 3) for b in back]
    return jnp.stack(first + second + [lax.axis_index("tp")]).astype(jnp.int32)


def sum_everywhere(mine, other):
    other = swap_core(other)
    half = LINE * SIDE
    kept, sent = [], []
    for part, bit in ((0, 2), (1, 1)):
        sent.append(swap_side(add_low(mine[part, half:], other[part, half:]), bit))
        kept.append(add_low(mine[part, :half], other[part, :half]))
    pieces = []
    for keep, got, bit in ((kept[0], sent[0], 1), (kept[1], sent[1], 2)):
        pieces.append(
            (add_low(keep[:LINE], got[:LINE]), swap_side(add_low(keep[LINE:], got[LINE:]), bit))
        )
    both = jnp.concatenate([add_low(*pair) for pair in pieces], axis=1)
    parts = [both[0]] + [shift_line(both[step], -step) for step in range(1, LINE)]
    total = add_low(*parts)
    line = [total] + [shift_line(total, step) for step in range(1, LINE)]
    rows = total.shape[0] // 2
    near, far = [], []
    for rest, bit in ((slice(0, rows), 1), (slice(rows, 2 * rows), 2)):
        part = jnp.stack([array[rest] for array in line])
        near.append(jnp.concatenate([part, swap_side(part, bit)]))
    far = [swap_side(near[0], 2), swap_side(near[1], 1)]
    others = [swap_core(part) for part in near]
    others += [swap_core(part) for part in far]
    return [*near, *far, *others]


def finish_kernel(count, orders_ref, *refs):
    pieces, outs = refs[:count], refs[count:]
    places, rows, _ = pieces[0].shape
    members = LINE * SIDE * SIDE
    core = orders_ref[2 * members]

    def step(place, carry):
        for which, ref in enumerate(pieces):
            half = which % 2
            far = which // 2 % 2
            owner = core if which < count // 2 else 1 - core
            member = orders_ref[half * members + far * places + place]
            start = owner * (members * 2 * rows) + member * (2 * rows) + half * rows
            start = pl.multiple_of(start, rows)
            column = 0
            for out in outs:
                width = out.shape[1]
                out[pl.ds(start, rows), :] = ref[place, :, column : column + width].astype(F32)
                column += width
        return carry

    lax.fori_loop(0, places, step, 0)


def finish(pieces, orders, widths):
    rows = SIDE * LINE * SIDE * SIDE * 2 * pieces[0].shape[1]
    return call(
        functools.partial(finish_kernel, len(pieces)),
        [sds((rows, width), F32) for width in widths],
        0,
        6 * rows * sum(widths),
        in_specs=[pl.BlockSpec(memory_space=pltpu.SMEM)] + [pl.BlockSpec()] * len(pieces),
    )(orders, *pieces)


def split_sum(low_ref, orders_ref, mine_ref, other_ref):
    _, members, rows, _ = mine_ref.shape
    core = orders_ref[2 * members]

    def step(place, carry):
        for half in range(2):
            member = orders_ref[half * members + place]
            for owner, ref in ((core, mine_ref), (1 - core, other_ref)):
                start = owner * (members * 2 * rows) + member * (2 * rows) + half * rows
                ref[half, place] = low_ref[pl.ds(pl.multiple_of(start, rows), rows), :]
        return carry

    lax.fori_loop(0, members, step, 0)


def sum_shapes(rows, width):
    if not on_grid():
        return ([sds((rows, width), BF)], [])
    members = LINE * SIDE * SIDE
    part = sds((2, members, rows // (2 * SIDE * members), width), BF)
    return ([part, part], [pltpu.VMEM((rows, width), BF)])


def gather_rows(chunk):
    rows, _ = chunk.shape
    if not on_grid():
        whole = lax.all_gather(chunk, "ep", axis=0, tiled=True)
        block = min(512, whole.shape[0])
        return [[whole[i : i + block]] for i in range(0, whole.shape[0], block)]
    half = rows // 2
    far = swap_side(chunk, FAR)
    near, away = [], []
    for rest, bits in ((slice(0, half), (1, 2)), (slice(half, rows), (2, 1))):
        part = jnp.concatenate([chunk[rest], far[rest]])
        part = jnp.concatenate([part, swap_side(part, bits[0])])
        near.append(part)
        away.append(swap_side(part, bits[1]))
    return [near, away]


def scatter_rows(blocks):
    if not on_grid():
        whole = jnp.concatenate([array for part in blocks for array in part])
        return (lax.psum_scatter(whole, "ep", scatter_dimension=0, tiled=True), None)
    near, away = blocks
    mine, theirs = [], []
    for own, sent, bits in ((near[0], away[0], (1, 2)), (near[1], away[1], (2, 1))):
        other = swap_side(sent, bits[1])
        count = own.shape[0] // 2
        far = swap_side(add_low(own[count:], other[count:]), bits[0])
        kept = add_low(own[:count], other[:count])
        count //= 2
        theirs.append(add_low(kept[count:], far[count:]))
        mine.append(add_low(kept[:count], far[:count]))
    return (jnp.concatenate(mine), swap_side(jnp.concatenate(theirs), FAR))


def expert_pieces(weights, axes):
    if not on_grid():
        whole = [lax.all_gather(w, "tp", axis=axis, tiled=True) for w, axis in zip(weights, axes)]
        return ([whole], (0,))
    near = [swap_side(w, NEAR) for w in weights]
    across = [swap_core(w) for w in weights]
    return ([list(weights), across, near, [swap_core(w) for w in near]], (0, 0, 1, 1))


def rope_tables(seq_len):
    half_dim = HEAD_DIM // 2
    freq = THETA ** (-(np.arange(half_dim, dtype=np.float64) * 2.0) / HEAD_DIM)
    angles = np.arange(seq_len, dtype=np.float64)[:, None] * freq[None, :]
    cosine, sine = np.cos(angles), np.sin(angles)
    repeats = LANES // HEAD_DIM
    cosine = np.tile(np.concatenate([cosine, cosine], axis=1), (1, repeats))
    sine = np.tile(np.concatenate([-sine, sine], axis=1), (1, repeats))
    return (cosine.astype(np.float32), sine.astype(np.float32))


def swap_halves(values):
    lane = lax.broadcasted_iota(jnp.int32, values.shape, 1)
    leading = lax.rem(lane, HEAD_DIM) < HEAD_DIM // 2
    half = HEAD_DIM // 2
    return jnp.where(
        leading, pltpu.roll(values, LANES - half, 1), pltpu.roll(values, half, 1)
    )


def blocks(width):
    return [slice(start, start + LANES) for start in range(0, width, LANES)]


def head_slice(index):
    return slice(index * HEAD_DIM, (index + 1) * HEAD_DIM)


def call(kernel, out_shape, flops, nbytes, **options):
    return pl.pallas_call(
        kernel,
        out_shape=out_shape,
        compiler_params=pltpu.CompilerParams(vmem_limit_bytes=VMEM_LIMIT),
        cost_estimate=pl.CostEstimate(flops=flops, bytes_accessed=nbytes, transcendentals=0),
        **options,
    )


def project_kernel(
    tok_ref, gain_ref, wq_ref, wk_ref, wv_ref, cos_ref, sin_ref, norm_ref, q_ref, kv_ref
):
    values = tok_ref[...].astype(F32)
    inverse = lax.rsqrt(jnp.mean(values * values, axis=1, keepdims=True) + EPS)
    normed = (values * inverse * gain_ref[...].astype(F32)).astype(BF)
    norm_ref[...] = normed
    cosine, sine = cos_ref[...], sin_ref[...]
    query = jnp.dot(normed, wq_ref[...], preferred_element_type=F32)
    for cols in blocks(query.shape[1]):
        part = query[:, cols]
        q_ref[:, cols] = (part * cosine + swap_halves(part) * sine).astype(BF)
    key = jnp.dot(normed, wk_ref[...], preferred_element_type=F32)
    for cols in blocks(key.shape[1]):
        part = key[:, cols]
        kv_ref[:, cols] = (part * cosine + swap_halves(part) * sine).astype(BF)
    value = jnp.dot(normed, wv_ref[...], preferred_element_type=F32)
    kv_ref[:, key.shape[1] :] = value.astype(BF)


def pair_rows(ref, group):
    left = ref[:, head_slice(GROUP * group)]
    right = ref[:, head_slice(GROUP * group + 1)]
    return jnp.concatenate([left, right], axis=0)


def pair_columns(values):
    rows = values.shape[0] // GROUP
    return jnp.concatenate([values[:rows], values[rows:]], axis=1)


def allowed_pairs(qinfo_ref, kinfo_ref):
    qpos, qseg = qinfo_ref[:, 0:1], qinfo_ref[:, 1:2]
    kpos, kseg = kinfo_ref[0:1, :], kinfo_ref[1:2, :]
    allowed = jnp.where((qpos >= kpos) & (qseg == kseg), 1.0, 0.0)
    return jnp.concatenate([allowed] * GROUP, axis=0) > 0.5


def gate_rows(logits, has):
    has = has > 0
    logits = jnp.where(has, logits, -jnp.inf)
    weight = jnp.exp(logits - jnp.max(logits, axis=1, keepdims=True))
    return weight / jnp.sum(weight, axis=1, keepdims=True)


def attend_kernel(
    q_ref, kv_ref, qinfo_ref, kinfo_ref, wp_ref, tok_ref, gain_ref, router_ref, has_ref,
    att_ref, lse_ref, hid_ref, moe_ref, gates_ref,
):
    allowed = allowed_pairs(qinfo_ref, kinfo_ref)
    rows = q_ref.shape[0]
    lane = lax.broadcasted_iota(jnp.int32, (rows, LANES), 1)
    kept = jnp.zeros((rows, LANES), F32)
    for group in range(KV_HEADS):
        query = pair_rows(q_ref, group)
        key = kv_ref[:, head_slice(group)]
        value = kv_ref[:, head_slice(KV_HEADS + group)]
        scores = lax.dot_general(query, key, INNER, preferred_element_type=F32)
        scores = jnp.where(allowed, scores * HEAD_DIM ** (-0.5), MASKED)
        highest = jnp.max(scores, axis=1, keepdims=True)
        exponent = jnp.exp(scores - highest)
        totals = jnp.sum(exponent, axis=1, keepdims=True)
        probs = (exponent / totals).astype(BF)
        blended = jnp.dot(probs, value, preferred_element_type=F32)
        cols = slice(group * GROUP * HEAD_DIM, (group + 1) * GROUP * HEAD_DIM)
        att_ref[:, cols] = pair_columns(blended).astype(BF)
        log_total = highest + jnp.log(totals)
        for which in range(GROUP):
            column = log_total[which * rows : (which + 1) * rows]
            kept = jnp.where(lane == GROUP * group + which, column, kept)
    lse_ref[...] = kept
    hidden = tok_ref[...].astype(F32) + jnp.dot(
        att_ref[...], wp_ref[...], preferred_element_type=F32
    )
    hid_ref[...] = hidden
    inverse = lax.rsqrt(jnp.mean(hidden * hidden, axis=1, keepdims=True) + EPS)
    normed = (hidden * inverse * gain_ref[...].astype(F32)).astype(BF)
    moe_ref[...] = normed
    logits = jnp.dot(normed, router_ref[...], preferred_element_type=F32)
    gates_ref[...] = gate_rows(logits, has_ref[...])


def expert_kernel(count, slots, *refs):
    pieces = len(slots)
    row_refs, cot_refs = refs[:count], refs[count : 2 * count]
    weight_refs = refs[2 * count : 2 * count + 3 * pieces]
    router_ref, mine_ref = refs[2 * count + 3 * pieces : 2 * count + 3 * pieces + 2]
    results = refs[2 * count + 3 * pieces + 2 :]
    for block in range(count):
        out_ref, gin_ref, act_ref, gga_ref, gua_ref = results[block::count]
        rows = row_refs[block][...]
        width = rows.shape[1]
        cots = cot_refs[block][:, :width]
        logits = jnp.dot(rows, router_ref[...], preferred_element_type=F32)
        gates = gate_rows(logits, cot_refs[block][:, width:])
        lane = lax.broadcasted_iota(jnp.int32, gates.shape, 1)
        out = gin = None
        gate_grads = [None] * (1 + max(slots))
        for piece, slot in enumerate(slots):
            wg_ref, wu_ref, wd_ref = weight_refs[3 * piece : 3 * piece + 3]
            gate = jnp.sum(gates * mine_ref[slot : slot + 1, :], axis=1, keepdims=True)
            gate_act = jnp.dot(rows, wg_ref[...], preferred_element_type=F32)
            up_act = jnp.dot(rows, wu_ref[...], preferred_element_type=F32)
            back = lax.dot_general(cots, wd_ref[...], INNER, preferred_element_type=F32)
            sigmoid_gate = 1.0 / (1.0 + jnp.exp(-gate_act))
            silu_gate = gate_act * sigmoid_gate
            acted = (silu_gate * up_act).astype(BF).astype(F32)
            part = jnp.sum(acted * back, axis=1, keepdims=True)
            gate_grads[slot] = part if gate_grads[slot] is None else gate_grads[slot] + part
            acted_low = (acted * gate).astype(BF)
            grad_acted = back * gate
            grad_up_act = (grad_acted * silu_gate).astype(BF)
            grad_gate_act = (
                grad_acted * up_act * sigmoid_gate * (1.0 + gate_act * (1.0 - sigmoid_gate))
            ).astype(BF)
            hidden = wg_ref.shape[1]
            cols = slice(piece * hidden, (piece + 1) * hidden)
            act_ref[:, cols], gga_ref[:, cols], gua_ref[:, cols] = (
                acted_low, grad_gate_act, grad_up_act,
            )
            part = jnp.dot(acted_low, wd_ref[...], preferred_element_type=F32)
            out = part if out is None else out + part
            part = lax.dot_general(
                grad_gate_act, wg_ref[...], INNER, preferred_element_type=F32
            ) + lax.dot_general(grad_up_act, wu_ref[...], INNER, preferred_element_type=F32)
            gin = part if gin is None else gin + part
        out_ref[...] = out.astype(BF)
        gin_ref[:, :width] = gin.astype(BF)
        kept = jnp.zeros(gates.shape, F32)
        for slot, grad in enumerate(gate_grads):
            coarse = grad.astype(BF).astype(F32)
            chosen = mine_ref[slot : slot + 1, :]
            kept += coarse * chosen + (grad - coarse) * pltpu.roll(
                jnp.broadcast_to(chosen, gates.shape), HALF_LANES, 1
            )
        gin_ref[:, width:] = kept.astype(BF)


def run_expert(rows, cots, pieces, slots, router, mine):
    count = len(rows)
    width, hidden = pieces[0][0].shape
    total = sum(part.shape[0] for part in rows)
    wide = hidden * len(pieces)
    columns = (width, width + LANES, wide, wide, wide)
    out = call(
        functools.partial(expert_kernel, count, slots),
        [sds((part.shape[0], cols), BF) for cols in columns for part in rows],
        12 * total * width * wide,
        6 * width * wide + 10 * total * width,
    )(*rows, *cots, *[w for piece in pieces for w in piece], router, mine)
    return [out[i * count : (i + 1) * count] for i in range(len(columns))]


def weights_kernel(count, slots, hidden, *refs):
    rows, cots, acts, ggas, guas = (
        [ref for ref in refs[i * count : (i + 1) * count]] for i in range(5)
    )
    results = refs[5 * count :]
    width = rows[0].shape[1]

    def tall(parts, cols):
        return jnp.concatenate([ref[:, cols] for ref in parts], axis=0)

    rows = tall(rows, slice(0, width))
    cots = tall(cots, slice(0, width))
    for piece in range(len(slots)):
        cols = slice(piece * hidden, (piece + 1) * hidden)
        gate = lax.dot_general(rows, tall(ggas, cols), OUTER, preferred_element_type=F32)
        up = lax.dot_general(rows, tall(guas, cols), OUTER, preferred_element_type=F32)
        down = lax.dot_general(tall(acts, cols), cots, OUTER, preferred_element_type=F32)
        if piece % 2:
            wide_ref, tall_ref = results[-2:]
            at = (piece // 2) * 2 * hidden
            wide_ref[:, at : at + hidden] = gate.astype(BF)
            wide_ref[:, at + hidden : at + 2 * hidden] = up.astype(BF)
            at = (piece // 2) * hidden
            tall_ref[at : at + hidden, :] = down.astype(BF)
        else:
            gate_ref, up_ref, down_ref = results[3 * (piece // 2) : 3 * (piece // 2) + 3]
            gate_ref[...], up_ref[...], down_ref[...] = gate, up, down


def weight_grads(rows, cots, acts, ggas, guas, slots):
    count = len(rows)
    width = rows[0].shape[1]
    wide = acts[0].shape[1]
    hidden = wide // len(slots)
    total = sum(part.shape[0] for part in rows)
    shapes = []
    for _ in range(0, len(slots), 2):
        shapes += [sds((width, hidden), F32), sds((width, hidden), F32), sds((hidden, width), F32)]
    if len(slots) > 1:
        shapes += [sds((width, wide), BF), sds((wide // 2, width), BF)]
    out = call(
        functools.partial(weights_kernel, count, slots, hidden),
        shapes,
        6 * total * width * wide,
        12 * width * wide + 4 * total * (width + wide),
    )(*rows, *cots, *acts, *ggas, *guas)
    if not on_grid():
        return [
            lax.psum_scatter(grad, "tp", scatter_dimension=axis, tiled=True)
            for grad, axis in zip(out, (1, 1, 0))
        ]
    wide_part, tall_part = swap_core(out[6]), swap_core(out[7])
    slabs = [wide_part[:, i * hidden : (i + 1) * hidden] for i in range(4)]
    near_wide = jnp.concatenate([out[3] + slabs[2], out[4] + slabs[3]], axis=1).astype(BF)
    near_tall = (out[5] + tall_part[hidden:]).astype(BF)
    near_wide, near_tall = swap_side(near_wide, NEAR), swap_side(near_tall, NEAR)
    return [
        out[0] + slabs[0] + near_wide[:, :hidden],
        out[1] + slabs[1] + near_wide[:, hidden:],
        out[2] + tall_part[:hidden] + near_tall,
    ]


def column_sums(product):
    coarse = product.astype(BF)
    fine = (product - coarse.astype(F32)).astype(BF)
    ones = jnp.ones((product.shape[0], LANES), BF)
    return lax.dot_general(coarse, ones, OUTER, preferred_element_type=F32) + lax.dot_general(
        fine, ones, OUTER, preferred_element_type=F32
    )


def branch_kernel(
    gin_refs, hid_ref, gain_ref, cot_ref, gates_ref, router_ref, moe_ref, att_ref, wp_ref,
    orders_ref, ghid_ref, gatt_ref, *pay_refs,
):
    pay_ref = pay_refs[-1]
    width = hid_ref.shape[1]
    gates = gates_ref[...]
    grads = sum(ref[:, :width].astype(F32) for ref in gin_refs)
    dgate = sum(ref[:, width:].astype(F32) for ref in gin_refs)
    dgate = dgate + pltpu.roll(dgate, HALF_LANES, 1)
    total = jnp.sum(gates * dgate, axis=1, keepdims=True)
    grad_logits = (gates * (dgate - total)).astype(BF)
    upstream = grads + lax.dot_general(
        grad_logits, router_ref[...], INNER, preferred_element_type=F32
    )
    hidden = hid_ref[...]
    inverse = lax.rsqrt(jnp.mean(hidden * hidden, axis=1, keepdims=True) + EPS)
    scaled = hidden * inverse
    product = upstream * scaled
    weighted = upstream * gain_ref[...].astype(F32)
    mean = jnp.mean(weighted * scaled, axis=1, keepdims=True)
    grad_hidden = cot_ref[...].astype(F32) + inverse * (weighted - scaled * mean)
    ghid_ref[...] = grad_hidden
    grad_branch = grad_hidden.astype(BF)
    gatt_ref[...] = lax.dot_general(
        grad_branch, wp_ref[...], INNER, preferred_element_type=F32
    ).astype(BF)
    pay_ref[:, :width] = lax.dot_general(
        att_ref[...], grad_branch, OUTER, preferred_element_type=F32
    ).astype(BF)
    grad_router = lax.dot_general(moe_ref[...], grad_logits, OUTER, preferred_element_type=F32)
    lane = lax.broadcasted_iota(jnp.int32, grad_router.shape, 1)
    pay_ref[:, width:] = jnp.where(lane == LANES - 1, column_sums(product), grad_router).astype(BF)
    if len(pay_refs) > 1:
        split_sum(pay_ref, orders_ref, *pay_refs[:2])


def attend_back_kernel(
    gatt_ref, q_ref, kv_ref, lse_ref, qinfo_ref, kinfo_ref, cos_ref, sin_ref, gq_ref, gkv_ref
):
    allowed = allowed_pairs(qinfo_ref, kinfo_ref)
    cosine, sine = cos_ref[...], sin_ref[...]
    kept = lse_ref[...]
    scale = HEAD_DIM ** (-0.5)
    for pair in range(KV_HEADS // 2):
        grad_keys, grad_values = [], []
        for group in (2 * pair, 2 * pair + 1):
            query = pair_rows(q_ref, group)
            grad = pair_rows(gatt_ref, group)
            key = kv_ref[:, head_slice(group)]
            value = kv_ref[:, head_slice(KV_HEADS + group)]
            log_total = jnp.concatenate(
                [kept[:, GROUP * group + i : GROUP * group + i + 1] for i in range(GROUP)], axis=0
            )
            scores = lax.dot_general(query, key, INNER, preferred_element_type=F32)
            scores = jnp.where(allowed, scores * scale, MASKED)
            probs = jnp.exp(scores - log_total)
            grad_values.append(
                lax.dot_general(probs.astype(BF), grad, OUTER, preferred_element_type=F32)
            )
            grad_probs = lax.dot_general(grad, value, INNER, preferred_element_type=F32)
            delta = jnp.sum(probs * grad_probs, axis=1, keepdims=True)
            grad_scores = (probs * (grad_probs - delta)).astype(BF)
            grad_query = jnp.dot(grad_scores, key, preferred_element_type=F32) * scale
            grad_query = pair_columns(grad_query).astype(BF).astype(F32)
            cols = slice(group * GROUP * HEAD_DIM, (group + 1) * GROUP * HEAD_DIM)
            gq_ref[:, cols] = (grad_query * cosine - swap_halves(grad_query) * sine).astype(BF)
            grad_keys.append(
                lax.dot_general(grad_scores, query, OUTER, preferred_element_type=F32) * scale
            )
        cols = slice(pair * LANES, (pair + 1) * LANES)
        gkv_ref[:, cols] = jnp.concatenate(grad_keys, axis=1).astype(BF)
        shift = KV_HEADS * HEAD_DIM
        cols = slice(shift + pair * LANES, shift + (pair + 1) * LANES)
        gkv_ref[:, cols] = jnp.concatenate(grad_values, axis=1).astype(BF)


def project_back_kernel(
    norm_ref, gq_ref, gkv_ref, cos_ref, sin_ref, wq_ref, wk_ref, wv_ref, tok_ref, gain_ref,
    ghid_ref, orders_ref, gtok_ref, *pay_refs,
):
    gkraw_ref, pay_ref = pay_refs[-1], pay_refs[-2]
    cosine, sine = cos_ref[...], sin_ref[...]
    kwidth = wk_ref.shape[1]
    for cols in blocks(kwidth):
        part = gkv_ref[:, cols].astype(F32)
        gkraw_ref[:, cols] = (part * cosine - swap_halves(part) * sine).astype(BF)
    grad_query, grad_key, grad_value = gq_ref[...], gkraw_ref[...], gkv_ref[:, kwidth:]
    upstream = lax.dot_general(grad_query, wq_ref[...], INNER, preferred_element_type=F32)
    upstream += lax.dot_general(grad_key, wk_ref[...], INNER, preferred_element_type=F32)
    upstream += lax.dot_general(grad_value, wv_ref[...], INNER, preferred_element_type=F32)
    normed = norm_ref[...]
    start = 0
    for grad in (grad_query, grad_key, grad_value):
        pay_ref[:, start : start + grad.shape[1]] = lax.dot_general(
            normed, grad, OUTER, preferred_element_type=F32
        ).astype(BF)
        start += grad.shape[1]
    values = tok_ref[...].astype(F32)
    inverse = lax.rsqrt(jnp.mean(values * values, axis=1, keepdims=True) + EPS)
    scaled = values * inverse
    pay_ref[:, start:] = column_sums(upstream * scaled).astype(BF)
    weighted = upstream * gain_ref[...].astype(F32)
    mean = jnp.mean(weighted * scaled, axis=1, keepdims=True)
    gtok_ref[...] = (ghid_ref[...] + inverse * (weighted - scaled * mean)).astype(BF)
    if len(pay_refs) > 2:
        split_sum(pay_ref, orders_ref, *pay_refs[:2])


def sds(shape, dtype):
    return jax.ShapeDtypeStruct(shape, dtype)


def layer(
    tokens,
    segment_ids,
    routes,
    cotangent,
    query_weight,
    key_weight,
    value_weight,
    proj_weight,
    attn_gain,
    moe_gain,
    router_weight,
    gate_weight,
    up_weight,
    down_weight,
):
    tok_count, model_dim = tokens.shape
    seq_len = segment_ids.shape[1]
    experts = router_weight.shape[1]
    query_dim, kv_dim = HEADS * HEAD_DIM, KV_HEADS * HEAD_DIM
    core = lax.axis_index("tp")
    first_row = core * tok_count
    orders = group_orders() if on_grid() else jnp.zeros((1,), jnp.int32)

    has = (routes[:, :, None] == jnp.arange(LANES, dtype=jnp.int32)[None, None, :]).any(axis=1)
    has = has.astype(BF)
    cots = gather_rows(jnp.concatenate([cotangent, has], axis=1))
    pieces, slots = expert_pieces((gate_weight[0], up_weight[0], down_weight[0]), (1, 1, 0))

    cos_table, sin_table = rope_tables(seq_len)
    cosine = lax.dynamic_slice_in_dim(jnp.asarray(cos_table), first_row, tok_count)
    sine = lax.dynamic_slice_in_dim(jnp.asarray(sin_table), first_row, tok_count)
    gain_one, gain_two = attn_gain[None, :], moe_gain[None, :]
    router = jnp.pad(router_weight, ((0, 0), (0, LANES - experts)))

    normed, query, kv = call(
        project_kernel,
        (
            sds((tok_count, model_dim), BF),
            sds((tok_count, query_dim), BF),
            sds((tok_count, 2 * kv_dim), BF),
        ),
        4 * tok_count * model_dim * model_dim,
        5 * model_dim * model_dim,
    )(tokens, gain_one, query_weight, key_weight, value_weight, cosine, sine)

    own_pos = first_row + jnp.arange(tok_count, dtype=jnp.int32)
    segment_row = segment_ids[0]
    own_seg = lax.dynamic_slice_in_dim(segment_row, first_row, tok_count)
    qinfo = jnp.stack([own_pos, own_seg], axis=1)
    if on_grid():
        kv_all = jnp.concatenate([kv, swap_core(kv)], axis=0)
        other_row = (1 - core) * tok_count
        other_seg = lax.dynamic_slice_in_dim(segment_row, other_row, tok_count)
        other_pos = other_row + jnp.arange(tok_count, dtype=jnp.int32)
        kinfo = jnp.stack(
            [jnp.concatenate([own_pos, other_pos]), jnp.concatenate([own_seg, other_seg])]
        )
    else:
        kv_all = lax.all_gather(kv, "tp", axis=0, tiled=True)
        kinfo = jnp.stack([jnp.arange(seq_len, dtype=jnp.int32), segment_row])

    attended, log_totals, hidden, moe_input, gates = call(
        attend_kernel,
        (
            sds((tok_count, query_dim), BF),
            sds((tok_count, LANES), F32),
            sds((tok_count, model_dim), F32),
            sds((tok_count, model_dim), BF),
            sds((tok_count, LANES), F32),
        ),
        4 * tok_count * model_dim * model_dim,
        5 * model_dim * model_dim,
    )(query, kv_all, qinfo, kinfo, proj_weight, tokens, gain_two, router, has)

    rows = gather_rows(moe_input)
    own = lax.axis_index("ep")
    owned = jnp.stack([lax.bitwise_xor(own, NEAR * slot) for slot in range(1 + max(slots))])
    mine = (jnp.arange(LANES, dtype=jnp.int32)[None, :] == owned[:, None]).astype(F32)
    done = [run_expert(*part, pieces, slots, router, mine) for part in zip(rows, cots)]
    outputs, grad_inputs, acts, ggas, guas = zip(*done)
    grad_rows_in = scatter_rows(grad_inputs)

    def flat(blocks):
        return [array for part in blocks for array in part]

    grad_gate, grad_up, grad_down = weight_grads(
        flat(rows), flat(cots), flat(acts), flat(ggas), flat(guas), slots
    )
    blended = [part for part in scatter_rows(outputs) if part is not None]
    layer_out = (hidden + sum(part.astype(F32) for part in blended)).astype(BF)

    scalars = pl.BlockSpec(memory_space=pltpu.SMEM)
    outs, scratch = sum_shapes(model_dim, model_dim + LANES)
    grad_rows_in = [part for part in grad_rows_in if part is not None]
    grad_hidden, grad_attended, *early = call(
        branch_kernel,
        [sds((tok_count, model_dim), F32), sds((tok_count, query_dim), BF), *outs],
        4 * tok_count * model_dim * model_dim,
        5 * model_dim * model_dim,
        in_specs=[[pl.BlockSpec()] * len(grad_rows_in)] + [pl.BlockSpec()] * 8 + [scalars],
        scratch_shapes=scratch,
    )(
        grad_rows_in, hidden, gain_two, cotangent, gates, router, moe_input, attended, proj_weight,
        orders,
    )

    grad_query, grad_kv = call(
        attend_back_kernel,
        (sds((tok_count, query_dim), BF), sds((seq_len, 2 * kv_dim), BF)),
        4 * tok_count * model_dim * model_dim,
        5 * model_dim * model_dim,
    )(grad_attended, query, kv_all, log_totals, qinfo, kinfo, cosine, sine)
    if on_grid():
        grad_kv = add_low(grad_kv[:tok_count], swap_core(grad_kv[tok_count:]))
    else:
        grad_kv = lax.psum_scatter(grad_kv, "tp", scatter_dimension=0, tiled=True)

    outs, scratch = sum_shapes(model_dim, query_dim + 2 * kv_dim + LANES)
    grad_tokens, *late = call(
        project_back_kernel,
        [sds((tok_count, model_dim), BF), *outs],
        8 * tok_count * model_dim * model_dim,
        9 * model_dim * model_dim,
        in_specs=[pl.BlockSpec()] * 11 + [scalars],
        scratch_shapes=scratch + [pltpu.VMEM((tok_count, kv_dim), BF)],
    )(
        normed, grad_query, grad_kv, cosine, sine, query_weight, key_weight, value_weight, tokens,
        gain_one, grad_hidden, orders,
    )
    early_widths = (model_dim, LANES)
    late_widths = (query_dim, kv_dim, kv_dim, LANES)
    if on_grid():
        early = finish(sum_everywhere(*early), orders, early_widths)
        late = finish(sum_everywhere(*late), orders, late_widths)
    else:
        early, late = (
            jnp.split(lax.psum(low.astype(F32), ("ep", "tp")), np.cumsum(widths)[:-1], axis=1)
            for low, widths in ((early[0], early_widths), (late[0], late_widths))
        )
    return (
        layer_out,
        grad_tokens,
        late[0],
        late[1],
        late[2],
        early[0],
        late[3][:, 0],
        early[1][:, LANES - 1],
        early[1][:, :experts],
        grad_gate[None],
        grad_up[None],
        grad_down[None],
    )


def solution(mesh):
    placed = (
        P(("ep", "tp"), None),
        P("ep", None),
        P(("ep", "tp"), None),
        P(("ep", "tp"), None),
        P(),
        P(),
        P(),
        P(),
        P(),
        P(),
        P(),
        P("ep", None, "tp"),
        P("ep", None, "tp"),
        P("ep", "tp", None),
    )
    step = jax.shard_map(
        layer,
        mesh=mesh,
        in_specs=placed,
        out_specs=(
            P(("ep", "tp"), None),
            P(("ep", "tp"), None),
            P(),
            P(),
            P(),
            P(),
            P(),
            P(),
            P(),
            P("ep", None, "tp"),
            P("ep", None, "tp"),
            P("ep", "tp", None),
        ),
        check_vma=False,
    )
    if mesh.shape["ep"] != LINE * SIDE * SIDE or mesh.shape["tp"] != SIDE:
        return step
    return step
```

```python
import functools

import jax
import jax.numpy as jnp
import numpy as np
from jax import lax
from jax.experimental import pallas as pl
from jax.experimental.pallas import tpu as pltpu
from jax.sharding import PartitionSpec as P


HEADS = 16
KV_HEADS = 8
HEAD_DIM = 64
GROUP = HEADS // KV_HEADS
LANES = 128

EPS = 1e-06
EP, TP = "ep", "tp"
THETA = 10000.0
MASKED = -1000000000.0


LINE, SIDE = 4, 2
NEAR, FAR = 4, 8
HALF_LANES = LANES // 2
BF, F32 = jnp.bfloat16, jnp.float32
INNER = (((1,), (1,)), ((), ()))
OUTER = (((0,), (0,)), ((), ()))
VMEM_LIMIT = 60 * 1024 * 1024


def on_grid():
    return lax.axis_size(EP) == LINE * SIDE * SIDE and lax.axis_size(TP) == SIDE


def shift_line(array, step):
    count = LINE * SIDE * SIDE
    stride = SIDE * SIDE * step
    return lax.ppermute(array, EP, [(i, (i + stride) % count) for i in range(count)])


def swap_side(array, bit):
    return lax.ppermute(array, EP, [(i, i ^ bit) for i in range(LINE * SIDE * SIDE)])


def swap_core(array):
    return lax.ppermute(array, TP, [(0, 1), (1, 0)])


def add_low(*arrays):
    return sum(array.astype(F32) for array in arrays).astype(BF)


def member_at(half, place):
    me = lax.axis_index(EP)
    near = lax.rem(me, SIDE * SIDE)
    flip, back = lax.div(place, LINE), lax.rem(place, LINE)
    if half:
        flip = lax.div(flip, SIDE) + SIDE * lax.rem(flip, SIDE)
    line = lax.rem(lax.div(me, SIDE * SIDE) + LINE - back, LINE)
    return line * SIDE * SIDE + lax.bitwise_xor(near, flip)


def sum_everywhere(mine, other):
    other = swap_core(other)
    half = LINE * SIDE
    kept, sent = [], []
    for part, bit in ((0, 2), (1, 1)):
        sent.append(swap_side(add_low(mine[part, half:], other[part, half:]), bit))
        kept.append(add_low(mine[part, :half], other[part, :half]))
    pieces = []
    for keep, got, bit in ((kept[0], sent[0], 1), (kept[1], sent[1], 2)):
        pieces.append(
            (add_low(keep[:LINE], got[:LINE]), swap_side(add_low(keep[LINE:], got[LINE:]), bit))
        )
    both = jnp.concatenate([add_low(*pair) for pair in pieces], axis=1)
    parts = [both[0]] + [shift_line(both[step], -step) for step in range(1, LINE)]
    total = add_low(*parts)
    line = [total] + [shift_line(total, step) for step in range(1, LINE)]
    rows = total.shape[0] // 2
    near, far = [], []
    for rest, bit in ((slice(0, rows), 1), (slice(rows, 2 * rows), 2)):
        part = jnp.stack([array[rest] for array in line])
        near.append(jnp.concatenate([part, swap_side(part, bit)]))
    far = [swap_side(near[0], 2), swap_side(near[1], 1)]
    others = [swap_core(part) for part in near]
    others += [swap_core(part) for part in far]
    return [*near, *far, *others]


def finish_kernel(count, *refs):
    pieces, (*outs, router_ref, gain_ref) = refs[:count], refs[count:-1]
    side_ref = refs[-1]
    places, rows, _ = pieces[0].shape
    members = LINE * SIDE * SIDE
    core = lax.axis_index(TP)

    def step(place, carry):
        for which, ref in enumerate(pieces):
            half = which % 2
            far = which // 2 % 2
            owner = core if which < count // 2 else 1 - core
            member = member_at(half, far * places + place)
            start = owner * (members * 2 * rows) + member * (2 * rows) + half * rows
            start = pl.multiple_of(start, rows)
            column = 0
            for out in (*outs, side_ref):
                width = out.shape[1]
                out[pl.ds(start, rows), :] = ref[place, :, column : column + width].astype(F32)
                column += width
        return carry

    lax.fori_loop(0, places, step, 0)
    if router_ref is not None:
        router_ref[...] = side_ref[:, : router_ref.shape[1]]
    for block in range(gain_ref.shape[0]):
        turned = side_ref[block * LANES : (block + 1) * LANES, :].T
        gain_ref[block : block + 1, :] = turned[LANES - 1 :, :]


def finish(pieces, widths, experts):
    rows = SIDE * LINE * SIDE * SIDE * 2 * pieces[0].shape[1]
    kernel = functools.partial(finish_kernel, len(pieces))
    if not experts:
        kernel = functools.partial(finish_plain_kernel, len(pieces))
    shapes = [sds((rows, width), F32) for width in widths]
    shapes += [sds((rows, experts), F32)] if experts else []
    return call(
        kernel,
        [*shapes, sds((rows // LANES, LANES), F32)],
        0,
        6 * rows * sum(widths),
        scratch_shapes=[pltpu.VMEM((rows, LANES), F32)],
    )(*pieces)


def finish_plain_kernel(count, *refs):
    finish_kernel(count, *refs[:-2], None, *refs[-2:])


def split_sum(low_ref, mine_ref, other_ref):
    _, members, rows, _ = mine_ref.shape
    core = lax.axis_index(TP)

    def step(place, carry):
        for half in range(2):
            member = member_at(half, place)
            for owner, ref in ((core, mine_ref), (1 - core, other_ref)):
                start = owner * (members * 2 * rows) + member * (2 * rows) + half * rows
                ref[half, place] = low_ref[pl.ds(pl.multiple_of(start, rows), rows), :]
        return carry

    lax.fori_loop(0, members, step, 0)


def sum_shapes(rows, width):
    if not on_grid():
        return ([sds((rows, width), BF)], [])
    members = LINE * SIDE * SIDE
    part = sds((2, members, rows // (2 * SIDE * members), width), BF)
    return ([part, part], [pltpu.VMEM((rows, width), BF)])


def gather_rows(chunk):
    rows, _ = chunk.shape
    if not on_grid():
        whole = lax.all_gather(chunk, EP, axis=0, tiled=True)
        block = min(512, whole.shape[0])
        return [[whole[i : i + block]] for i in range(0, whole.shape[0], block)]
    half = rows // 2
    far = swap_side(chunk, FAR)
    near, away = [], []
    for rest, bits in ((slice(0, half), (1, 2)), (slice(half, rows), (2, 1))):
        part = jnp.concatenate([chunk[rest], far[rest]])
        part = jnp.concatenate([part, swap_side(part, bits[0])])
        near.append(part)
        away.append(swap_side(part, bits[1]))
    return [near, away]


def scatter_rows(blocks):
    if not on_grid():
        whole = jnp.concatenate([array for part in blocks for array in part])
        return (lax.psum_scatter(whole, EP, scatter_dimension=0, tiled=True), None)
    near, away = blocks
    mine, theirs = [], []
    for own, sent, bits in ((near[0], away[0], (1, 2)), (near[1], away[1], (2, 1))):
        other = swap_side(sent, bits[1])
        count = own.shape[0] // 2
        far = swap_side(add_low(own[count:], other[count:]), bits[0])
        kept = add_low(own[:count], other[:count])
        count //= 2
        theirs.append(add_low(kept[count:], far[count:]))
        mine.append(add_low(kept[:count], far[:count]))
    return (jnp.concatenate(mine), swap_side(jnp.concatenate(theirs), FAR))


def expert_pieces(weights, axes):
    if not on_grid():
        whole = [lax.all_gather(w, TP, axis=axis, tiled=True) for w, axis in zip(weights, axes)]
        return ([whole], (0,))
    near = [swap_side(w, NEAR) for w in weights[:2]]
    near.append(swap_side(weights[2], NEAR))
    across = [swap_core(w) for w in weights]
    both = [swap_core(w) for w in near[:2]]
    both.append(swap_core(near[2]))
    return ([list(weights), across, near, both], (0, 0, 1, 1))


def rope_tables(seq_len):
    half_dim = HEAD_DIM // 2
    freq = THETA ** (-(np.arange(half_dim, dtype=np.float64) * 2.0) / HEAD_DIM)
    angles = np.arange(seq_len, dtype=np.float64)[:, None] * freq[None, :]
    cosine, sine = np.cos(angles), np.sin(angles)
    repeats = LANES // HEAD_DIM
    cosine = np.tile(np.concatenate([cosine, cosine], axis=1), (1, repeats))
    sine = np.tile(np.concatenate([-sine, sine], axis=1), (1, repeats))
    return (cosine.astype(np.float32), sine.astype(np.float32))


def swap_halves(values):
    lane = lax.broadcasted_iota(jnp.int32, values.shape, 1)
    leading = lax.rem(lane, HEAD_DIM) < HEAD_DIM // 2
    half = HEAD_DIM // 2
    return jnp.where(
        leading, pltpu.roll(values, LANES - half, 1), pltpu.roll(values, half, 1)
    )


def own_rows(ref, rows):
    return ref[pl.ds(pl.multiple_of(lax.axis_index(TP) * rows, rows), rows), :]


def blocks(width):
    return [slice(start, start + LANES) for start in range(0, width, LANES)]


def head_slice(index):
    return slice(index * HEAD_DIM, (index + 1) * HEAD_DIM)


def call(kernel, out_shape, flops, nbytes, **options):
    return pl.pallas_call(
        kernel,
        out_shape=out_shape,
        compiler_params=pltpu.CompilerParams(vmem_limit_bytes=VMEM_LIMIT),
        cost_estimate=pl.CostEstimate(flops=flops, bytes_accessed=nbytes, transcendentals=0),
        **options,
    )


def project_kernel(
    tok_ref, gain_ref, wq_ref, wk_ref, wv_ref, cos_ref, sin_ref, norm_ref, q_ref, kv_ref
):
    values = tok_ref[...].astype(F32)
    inverse = lax.rsqrt(jnp.mean(values * values, axis=1, keepdims=True) + EPS)
    normed = (values * inverse * gain_ref[...].astype(F32)).astype(BF)
    norm_ref[...] = normed
    cosine, sine = own_rows(cos_ref, values.shape[0]), own_rows(sin_ref, values.shape[0])
    query = jnp.dot(normed, wq_ref[...], preferred_element_type=F32)
    for cols in blocks(query.shape[1]):
        part = query[:, cols]
        q_ref[:, cols] = (part * cosine + swap_halves(part) * sine).astype(BF)
    key = jnp.dot(normed, wk_ref[...], preferred_element_type=F32)
    for cols in blocks(key.shape[1]):
        part = key[:, cols]
        kv_ref[:, cols] = (part * cosine + swap_halves(part) * sine).astype(BF)
    value = jnp.dot(normed, wv_ref[...], preferred_element_type=F32)
    kv_ref[:, key.shape[1] :] = value.astype(BF)


def pair_rows(ref, group):
    left = ref[:, head_slice(GROUP * group)]
    right = ref[:, head_slice(GROUP * group + 1)]
    return jnp.concatenate([left, right], axis=0)


def pair_columns(values):
    rows = values.shape[0] // GROUP
    return jnp.concatenate([values[:rows], values[rows:]], axis=1)


def stacked(refs, cols):
    return jnp.concatenate([ref[:, cols] for ref in refs], axis=0)


def allowed_pairs(seg_ref, rows, own_first):
    seg = seg_ref[...]
    total = seg.shape[1]
    core = lax.axis_index(TP)
    own = seg[:, :rows]
    for part in range(1, total // rows):
        own = jnp.where(core == part, seg[:, part * rows : (part + 1) * rows], own)
    position = lax.broadcasted_iota(jnp.int32, (1, total), 1)
    if own_first:
        other = jnp.where(core == 0, seg[:, rows:], seg[:, :rows])
        seg = jnp.concatenate([own, other], axis=1)
        position = lax.rem(position + core * rows, total)
    column = jnp.broadcast_to(own.astype(F32), (rows, rows)).T[:, 0:1]
    place = core * rows + lax.broadcasted_iota(jnp.int32, (rows, 1), 0)
    allowed = (place >= position) & (column == seg.astype(F32))
    return jnp.concatenate([jnp.where(allowed, 1.0, 0.0)] * GROUP, axis=0) > 0.5


def lanes_of(values):
    rows, experts = values.shape
    return jnp.concatenate([values, jnp.zeros((rows, LANES - experts), values.dtype)], axis=1)


def gate_rows(logits, has):
    has, logits = has > 0, lanes_of(logits)
    logits = jnp.where(has, logits, -jnp.inf)
    weight = jnp.exp(logits - jnp.max(logits, axis=1, keepdims=True))
    return weight / jnp.sum(weight, axis=1, keepdims=True)


def attend_kernel(
    q_ref, kv_refs, seg_ref, wp_ref, tok_ref, gain_ref, router_ref, has_ref,
    att_ref, lse_ref, hid_ref, moe_ref, gates_ref,
):
    rows = q_ref.shape[0]
    allowed = allowed_pairs(seg_ref, rows, len(kv_refs) > 1)
    lane = lax.broadcasted_iota(jnp.int32, (rows, LANES), 1)
    kept = jnp.zeros((rows, LANES), F32)
    for group in range(KV_HEADS):
        query = pair_rows(q_ref, group)
        key = stacked(kv_refs, head_slice(group))
        value = stacked(kv_refs, head_slice(KV_HEADS + group))
        scores = lax.dot_general(query, key, INNER, preferred_element_type=F32)
        scores = jnp.where(allowed, scores * HEAD_DIM ** (-0.5), MASKED)
        highest = jnp.max(scores, axis=1, keepdims=True)
        exponent = jnp.exp(scores - highest)
        totals = jnp.sum(exponent, axis=1, keepdims=True)
        probs = (exponent / totals).astype(BF)
        blended = jnp.dot(probs, value, preferred_element_type=F32)
        cols = slice(group * GROUP * HEAD_DIM, (group + 1) * GROUP * HEAD_DIM)
        att_ref[:, cols] = pair_columns(blended).astype(BF)
        log_total = highest + jnp.log(totals)
        for which in range(GROUP):
            column = log_total[which * rows : (which + 1) * rows]
            kept = jnp.where(lane == GROUP * group + which, column, kept)
    lse_ref[...] = kept
    hidden = tok_ref[...].astype(F32) + jnp.dot(
        att_ref[...], wp_ref[...], preferred_element_type=F32
    )
    hid_ref[...] = hidden
    inverse = lax.rsqrt(jnp.mean(hidden * hidden, axis=1, keepdims=True) + EPS)
    normed = (hidden * inverse * gain_ref[...].astype(F32)).astype(BF)
    moe_ref[...] = normed
    logits = jnp.dot(normed, router_ref[...], preferred_element_type=F32)
    gates_ref[...] = gate_rows(logits, has_ref[...])


def expert_kernel(count, slots, *refs):
    pieces = len(slots)
    row_refs, cot_refs = refs[:count], refs[count : 2 * count]
    weight_refs = refs[2 * count : 2 * count + 3 * pieces]
    router_ref, *results = refs[2 * count + 3 * pieces :]
    lane = lax.broadcasted_iota(jnp.int32, (1, LANES), 1)
    owned = [lax.bitwise_xor(lax.axis_index(EP), NEAR * slot) for slot in range(1 + max(slots))]
    chosen = [jnp.where(lane == expert, 1.0, 0.0) for expert in owned]
    finer = [jnp.where(lane == expert + HALF_LANES, 1.0, 0.0) for expert in owned]
    for block in range(count):
        out_ref, gin_ref, act_ref, gga_ref, gua_ref = results[block::count]
        rows = row_refs[block][...]
        width = rows.shape[1]
        cots = cot_refs[block][:, :width]
        logits = jnp.dot(rows, router_ref[...], preferred_element_type=F32)
        gates = gate_rows(logits, cot_refs[block][:, width:])
        out = gin = None
        gate_grads = [None] * (1 + max(slots))
        for piece, slot in enumerate(slots):
            wg_ref, wu_ref, wd_ref = weight_refs[3 * piece : 3 * piece + 3]
            gate = jnp.sum(gates * chosen[slot], axis=1, keepdims=True)
            gate_act = jnp.dot(rows, wg_ref[...], preferred_element_type=F32)
            up_act = jnp.dot(rows, wu_ref[...], preferred_element_type=F32)
            back = lax.dot_general(cots, wd_ref[...], INNER, preferred_element_type=F32)
            sigmoid_gate = 1.0 / (1.0 + jnp.exp(-gate_act))
            silu_gate = gate_act * sigmoid_gate
            acted = (silu_gate * up_act).astype(BF).astype(F32)
            part = jnp.sum(acted * back, axis=1, keepdims=True)
            gate_grads[slot] = part if gate_grads[slot] is None else gate_grads[slot] + part
            acted_low = (acted * gate).astype(BF)
            grad_acted = back * gate
            grad_up_act = (grad_acted * silu_gate).astype(BF)
            grad_gate_act = (
                grad_acted * up_act * sigmoid_gate * (1.0 + gate_act * (1.0 - sigmoid_gate))
            ).astype(BF)
            hidden = wg_ref.shape[1]
            cols = slice(piece * hidden, (piece + 1) * hidden)
            act_ref[:, cols], gga_ref[:, cols], gua_ref[:, cols] = (
                acted_low, grad_gate_act, grad_up_act,
            )
            part = jnp.dot(acted_low, wd_ref[...], preferred_element_type=F32)
            out = part if out is None else out + part
            part = lax.dot_general(
                grad_gate_act, wg_ref[...], INNER, preferred_element_type=F32
            ) + lax.dot_general(grad_up_act, wu_ref[...], INNER, preferred_element_type=F32)
            gin = part if gin is None else gin + part
        out_ref[...] = out.astype(BF)
        gin_ref[:, :width] = gin.astype(BF)
        kept = jnp.zeros(gates.shape, F32)
        for slot, grad in enumerate(gate_grads):
            coarse = grad.astype(BF).astype(F32)
            kept += coarse * chosen[slot] + (grad - coarse) * finer[slot]
        gin_ref[:, width:] = kept.astype(BF)


def run_expert(rows, cots, pieces, slots, router):
    count = len(rows)
    width, hidden = pieces[0][0].shape
    total = sum(part.shape[0] for part in rows)
    wide = hidden * len(pieces)
    columns = (width, width + LANES, wide, wide, wide)
    out = call(
        functools.partial(expert_kernel, count, slots),
        [sds((part.shape[0], cols), BF) for cols in columns for part in rows],
        12 * total * width * wide,
        6 * width * wide + 10 * total * width,
    )(*rows, *cots, *[w for piece in pieces for w in piece], router)
    return [out[i * count : (i + 1) * count] for i in range(len(columns))]


def weights_kernel(count, slots, hidden, *refs):
    rows, cots, acts, ggas, guas = (
        [ref for ref in refs[i * count : (i + 1) * count]] for i in range(5)
    )
    results = refs[5 * count :]
    width = rows[0].shape[1]

    def tall(parts, cols):
        return jnp.concatenate([ref[:, cols] for ref in parts], axis=0)

    rows = tall(rows, slice(0, width))
    cots = tall(cots, slice(0, width))
    for piece in range(len(slots)):
        cols = slice(piece * hidden, (piece + 1) * hidden)
        gate = lax.dot_general(rows, tall(ggas, cols), OUTER, preferred_element_type=F32)
        up = lax.dot_general(rows, tall(guas, cols), OUTER, preferred_element_type=F32)
        down = lax.dot_general(tall(acts, cols), cots, OUTER, preferred_element_type=F32)
        if piece % 2:
            wide_ref, tall_ref = results[-2:]
            at = (piece // 2) * 2 * hidden
            wide_ref[:, at : at + hidden] = gate.astype(BF)
            wide_ref[:, at + hidden : at + 2 * hidden] = up.astype(BF)
            at = (piece // 2) * hidden
            tall_ref[at : at + hidden, :] = down.astype(BF)
        else:
            gate_ref, up_ref, down_ref = results[3 * (piece // 2) : 3 * (piece // 2) + 3]
            gate_ref[...], up_ref[...], down_ref[...] = gate, up, down


def weight_grads(rows, cots, acts, ggas, guas, slots):
    count = len(rows)
    width = rows[0].shape[1]
    wide = acts[0].shape[1]
    hidden = wide // len(slots)
    total = sum(part.shape[0] for part in rows)
    shapes = []
    for _ in range(0, len(slots), 2):
        shapes += [sds((width, hidden), F32), sds((width, hidden), F32), sds((hidden, width), F32)]
    if len(slots) > 1:
        shapes += [sds((width, wide), BF), sds((wide // 2, width), BF)]
    out = call(
        functools.partial(weights_kernel, count, slots, hidden),
        shapes,
        6 * total * width * wide,
        12 * width * wide + 4 * total * (width + wide),
    )(*rows, *cots, *acts, *ggas, *guas)
    if not on_grid():
        return [
            lax.psum_scatter(grad, TP, scatter_dimension=axis, tiled=True)
            for grad, axis in zip(out, (1, 1, 0))
        ]
    wide_part, tall_part = swap_core(out[6]), swap_core(out[7])
    slabs = [wide_part[:, i * hidden : (i + 1) * hidden] for i in range(4)]
    near_wide = jnp.concatenate([out[3] + slabs[2], out[4] + slabs[3]], axis=1).astype(BF)
    near_tall = (out[5] + tall_part[hidden:]).astype(BF)
    near_wide, near_tall = swap_side(near_wide, NEAR), swap_side(near_tall, NEAR)
    return call(
        grads_sum_kernel, shapes[:3], 0, 40 * width * hidden
    )(*out[:3], wide_part, tall_part, near_wide, near_tall)


def grads_sum_kernel(
    gate_ref, up_ref, down_ref, wide_ref, tall_ref, near_wide_ref, near_tall_ref, *outs
):
    hidden = gate_ref.shape[1]
    for part, (ref, out) in enumerate(zip((gate_ref, up_ref), outs)):
        cols = slice(part * hidden, (part + 1) * hidden)
        out[...] = ref[...] + wide_ref[:, cols].astype(F32) + near_wide_ref[:, cols].astype(F32)
    outs[2][...] = (
        down_ref[...] + tall_ref[:hidden, :].astype(F32) + near_tall_ref[...].astype(F32)
    )


def column_sums(product):
    coarse = product.astype(BF)
    fine = (product - coarse.astype(F32)).astype(BF)
    ones = jnp.ones((product.shape[0], LANES), BF)
    return lax.dot_general(coarse, ones, OUTER, preferred_element_type=F32) + lax.dot_general(
        fine, ones, OUTER, preferred_element_type=F32
    )


def branch_kernel(
    gin_refs, hid_ref, gain_ref, cot_ref, gates_ref, router_ref, moe_ref, att_ref, wp_ref,
    ghid_ref, gatt_ref, *pay_refs,
):
    pay_ref = pay_refs[-1]
    width = hid_ref.shape[1]
    gates = gates_ref[...]
    grads = sum(ref[:, :width].astype(F32) for ref in gin_refs)
    dgate = sum(ref[:, width:].astype(F32) for ref in gin_refs)
    dgate = dgate + pltpu.roll(dgate, HALF_LANES, 1)
    total = jnp.sum(gates * dgate, axis=1, keepdims=True)
    grad_logits = (gates * (dgate - total)).astype(BF)
    experts = router_ref.shape[1]
    upstream = grads + lax.dot_general(
        grad_logits[:, :experts], router_ref[...], INNER, preferred_element_type=F32
    )
    hidden = hid_ref[...]
    inverse = lax.rsqrt(jnp.mean(hidden * hidden, axis=1, keepdims=True) + EPS)
    scaled = hidden * inverse
    product = upstream * scaled
    weighted = upstream * gain_ref[...].astype(F32)
    mean = jnp.mean(weighted * scaled, axis=1, keepdims=True)
    grad_hidden = cot_ref[...].astype(F32) + inverse * (weighted - scaled * mean)
    ghid_ref[...] = grad_hidden
    grad_branch = grad_hidden.astype(BF)
    gatt_ref[...] = lax.dot_general(
        grad_branch, wp_ref[...], INNER, preferred_element_type=F32
    ).astype(BF)
    pay_ref[:, :width] = lax.dot_general(
        att_ref[...], grad_branch, OUTER, preferred_element_type=F32
    ).astype(BF)
    grad_router = lax.dot_general(moe_ref[...], grad_logits, OUTER, preferred_element_type=F32)
    lane = lax.broadcasted_iota(jnp.int32, grad_router.shape, 1)
    pay_ref[:, width:] = jnp.where(lane == LANES - 1, column_sums(product), grad_router).astype(BF)
    if len(pay_refs) > 1:
        split_sum(pay_ref, *pay_refs[:2])


def attend_back_kernel(
    gatt_ref, q_ref, kv_refs, lse_ref, seg_ref, cos_ref, sin_ref, gq_ref, *gkv_refs
):
    rows = q_ref.shape[0]
    allowed = allowed_pairs(seg_ref, rows, len(kv_refs) > 1)
    cosine, sine = own_rows(cos_ref, rows), own_rows(sin_ref, rows)
    kept = lse_ref[...]
    scale = HEAD_DIM ** (-0.5)
    for pair in range(KV_HEADS // 2):
        grad_keys, grad_values = [], []
        for group in (2 * pair, 2 * pair + 1):
            query = pair_rows(q_ref, group)
            grad = pair_rows(gatt_ref, group)
            key = stacked(kv_refs, head_slice(group))
            value = stacked(kv_refs, head_slice(KV_HEADS + group))
            log_total = jnp.concatenate(
                [kept[:, GROUP * group + i : GROUP * group + i + 1] for i in range(GROUP)], axis=0
            )
            scores = lax.dot_general(query, key, INNER, preferred_element_type=F32)
            scores = jnp.where(allowed, scores * scale, MASKED)
            probs = jnp.exp(scores - log_total)
            grad_values.append(
                lax.dot_general(probs.astype(BF), grad, OUTER, preferred_element_type=F32)
            )
            grad_probs = lax.dot_general(grad, value, INNER, preferred_element_type=F32)
            delta = jnp.sum(probs * grad_probs, axis=1, keepdims=True)
            grad_scores = (probs * (grad_probs - delta)).astype(BF)
            grad_query = jnp.dot(grad_scores, key, preferred_element_type=F32) * scale
            grad_query = pair_columns(grad_query).astype(BF).astype(F32)
            cols = slice(group * GROUP * HEAD_DIM, (group + 1) * GROUP * HEAD_DIM)
            gq_ref[:, cols] = (grad_query * cosine - swap_halves(grad_query) * sine).astype(BF)
            grad_keys.append(
                lax.dot_general(grad_scores, query, OUTER, preferred_element_type=F32) * scale
            )
        for shift, grads in ((0, grad_keys), (KV_HEADS * HEAD_DIM, grad_values)):
            cols = slice(shift + pair * LANES, shift + (pair + 1) * LANES)
            both = jnp.concatenate(grads, axis=1).astype(BF)
            for part, ref in enumerate(gkv_refs):
                ref[:, cols] = both[part * ref.shape[0] : (part + 1) * ref.shape[0]]


def project_back_kernel(
    norm_ref, gq_ref, gkv_refs, cos_ref, sin_ref, wq_ref, wk_ref, wv_ref, tok_ref, gain_ref,
    ghid_ref, gtok_ref, *pay_refs,
):
    gkraw_ref, pay_ref = pay_refs[-1], pay_refs[-2]
    rows = norm_ref.shape[0]
    cosine, sine = own_rows(cos_ref, rows), own_rows(sin_ref, rows)
    kwidth = wk_ref.shape[1]

    def total(cols):
        return add_low(*[ref[:, cols] for ref in gkv_refs])

    for cols in blocks(kwidth):
        part = total(cols).astype(F32)
        gkraw_ref[:, cols] = (part * cosine - swap_halves(part) * sine).astype(BF)
    grad_query, grad_key, grad_value = gq_ref[...], gkraw_ref[...], total(slice(kwidth, 2 * kwidth))
    upstream = lax.dot_general(grad_query, wq_ref[...], INNER, preferred_element_type=F32)
    upstream += lax.dot_general(grad_key, wk_ref[...], INNER, preferred_element_type=F32)
    upstream += lax.dot_general(grad_value, wv_ref[...], INNER, preferred_element_type=F32)
    normed = norm_ref[...]
    start = 0
    for grad in (grad_query, grad_key, grad_value):
        pay_ref[:, start : start + grad.shape[1]] = lax.dot_general(
            normed, grad, OUTER, preferred_element_type=F32
        ).astype(BF)
        start += grad.shape[1]
    values = tok_ref[...].astype(F32)
    inverse = lax.rsqrt(jnp.mean(values * values, axis=1, keepdims=True) + EPS)
    scaled = values * inverse
    pay_ref[:, start:] = column_sums(upstream * scaled).astype(BF)
    weighted = upstream * gain_ref[...].astype(F32)
    mean = jnp.mean(weighted * scaled, axis=1, keepdims=True)
    gtok_ref[...] = (ghid_ref[...] + inverse * (weighted - scaled * mean)).astype(BF)
    if len(pay_refs) > 2:
        split_sum(pay_ref, *pay_refs[:2])


def sds(shape, dtype):
    return jax.ShapeDtypeStruct(shape, dtype)


def layer(
    tokens,
    segment_ids,
    routes,
    cotangent,
    query_weight,
    key_weight,
    value_weight,
    proj_weight,
    attn_gain,
    moe_gain,
    router_weight,
    gate_weight,
    up_weight,
    down_weight,
):
    tok_count, model_dim = tokens.shape
    seq_len = segment_ids.shape[1]
    experts = router_weight.shape[1]
    query_dim, kv_dim = HEADS * HEAD_DIM, KV_HEADS * HEAD_DIM

    has = (routes[:, :, None] == jnp.arange(LANES, dtype=jnp.int32)[None, None, :]).any(axis=1)
    has = has.astype(BF)
    cots = gather_rows(jnp.concatenate([cotangent, has], axis=1))
    pieces, slots = expert_pieces((gate_weight[0], up_weight[0], down_weight[0]), (1, 1, 0))

    cosine, sine = (jnp.asarray(table) for table in rope_tables(seq_len))
    gain_one, gain_two = attn_gain[None, :], moe_gain[None, :]

    normed, query, kv = call(
        project_kernel,
        (
            sds((tok_count, model_dim), BF),
            sds((tok_count, query_dim), BF),
            sds((tok_count, 2 * kv_dim), BF),
        ),
        4 * tok_count * model_dim * model_dim,
        5 * model_dim * model_dim,
    )(tokens, gain_one, query_weight, key_weight, value_weight, cosine, sine)

    if on_grid():
        kv_all = [kv, swap_core(kv)]
    else:
        kv_all = [lax.all_gather(kv, TP, axis=0, tiled=True)]

    attended, log_totals, hidden, moe_input, gates = call(
        attend_kernel,
        (
            sds((tok_count, query_dim), BF),
            sds((tok_count, LANES), F32),
            sds((tok_count, model_dim), F32),
            sds((tok_count, model_dim), BF),
            sds((tok_count, LANES), F32),
        ),
        4 * tok_count * model_dim * model_dim,
        5 * model_dim * model_dim,
    )(query, kv_all, segment_ids, proj_weight, tokens, gain_two, router_weight, has)

    rows = gather_rows(moe_input)
    done = []
    for part in zip(rows, cots):
        done.append(run_expert(*part, pieces, slots, router_weight))
    outputs, grad_inputs, acts, ggas, guas = zip(*done)
    grad_rows_in = scatter_rows(grad_inputs)

    def flat(blocks):
        return [array for part in blocks for array in part]

    grad_gate, grad_up, grad_down = weight_grads(
        flat(rows), flat(cots), flat(acts), flat(ggas), flat(guas), slots
    )
    blended = [part for part in scatter_rows(outputs) if part is not None]
    layer_out = (hidden + sum(part.astype(F32) for part in blended)).astype(BF)

    outs, scratch = sum_shapes(model_dim, model_dim + LANES)
    grad_rows_in = [part for part in grad_rows_in if part is not None]
    grad_hidden, grad_attended, *early = call(
        branch_kernel,
        [sds((tok_count, model_dim), F32), sds((tok_count, query_dim), BF), *outs],
        4 * tok_count * model_dim * model_dim,
        5 * model_dim * model_dim,
        scratch_shapes=scratch,
    )(
        grad_rows_in, hidden, gain_two, cotangent, gates, router_weight, moe_input, attended,
        proj_weight,
    )

    count = len(kv_all)
    grad_query, *grad_kv = call(
        attend_back_kernel,
        [sds((tok_count, query_dim), BF)] + [sds((seq_len // count, 2 * kv_dim), BF)] * count,
        4 * tok_count * model_dim * model_dim,
        5 * model_dim * model_dim,
    )(grad_attended, query, kv_all, log_totals, segment_ids, cosine, sine)
    if on_grid():
        grad_kv = [grad_kv[0], swap_core(grad_kv[1])]
    else:
        grad_kv = [lax.psum_scatter(grad_kv[0], TP, scatter_dimension=0, tiled=True)]

    outs, scratch = sum_shapes(model_dim, query_dim + 2 * kv_dim + LANES)
    grad_tokens, *late = call(
        project_back_kernel,
        [sds((tok_count, model_dim), BF), *outs],
        8 * tok_count * model_dim * model_dim,
        9 * model_dim * model_dim,
        scratch_shapes=scratch + [pltpu.VMEM((tok_count, kv_dim), BF)],
    )(
        normed, grad_query, grad_kv, cosine, sine, query_weight, key_weight, value_weight, tokens,
        gain_one, grad_hidden,
    )
    early_widths, late_widths = (model_dim,), (query_dim, kv_dim, kv_dim)
    if on_grid():
        grad_proj, grad_router, gain_grad_two = finish(
            sum_everywhere(*early), early_widths, experts
        )
        *late, gain_grad_one = finish(sum_everywhere(*late), late_widths, 0)
        gain_grad_one, gain_grad_two = gain_grad_one.reshape(-1), gain_grad_two.reshape(-1)
    else:
        early, late = (
            jnp.split(lax.psum(low.astype(F32), (EP, TP)), np.cumsum(widths), axis=1)
            for low, widths in ((early[0], early_widths), (late[0], late_widths))
        )
        grad_proj, side = early
        grad_router, gain_grad_two = side[:, :experts], side[:, LANES - 1]
        gain_grad_one = late.pop()[:, LANES - 1]
    return (
        layer_out,
        grad_tokens,
        *late,
        grad_proj,
        gain_grad_one,
        gain_grad_two,
        grad_router,
        grad_gate[None],
        grad_up[None],
        grad_down[None],
    )


def solution(mesh):
    placed = (
        P((EP, TP), None),
        P(EP, None),
        P((EP, TP), None),
        P((EP, TP), None),
        P(),
        P(),
        P(),
        P(),
        P(),
        P(),
        P(),
        P(EP, None, TP),
        P(EP, None, TP),
        P(EP, TP, None),
    )
    step = jax.shard_map(
        layer,
        mesh=mesh,
        in_specs=placed,
        out_specs=(
            P((EP, TP), None),
            P((EP, TP), None),
            P(),
            P(),
            P(),
            P(),
            P(),
            P(),
            P(),
            P(EP, None, TP),
            P(EP, None, TP),
            P(EP, TP, None),
        ),
        check_vma=False,
    )
    if mesh.shape[EP] != LINE * SIDE * SIDE or mesh.shape[TP] != SIDE:
        return step
    return step
```

```python
import functools

import jax
import jax.numpy as jnp
import numpy as np
from jax import lax
from jax.experimental import pallas as pl
from jax.experimental.pallas import tpu as pltpu
from jax.sharding import PartitionSpec as P


HEADS = 16
KV_HEADS = 8
HEAD_DIM = 64
GROUP = HEADS // KV_HEADS
LANES = 128

EPS = 1e-06
EP, TP = "ep", "tp"
THETA = 10000.0
MASKED = -1000000000.0


LINE, SIDE = 4, 2
NEAR, FAR = 4, 8
HALF_LANES = LANES // 2
BF, F32 = jnp.bfloat16, jnp.float32
INNER = (((1,), (1,)), ((), ()))
OUTER = (((0,), (0,)), ((), ()))
VMEM_LIMIT = 60 * 1024 * 1024


def on_grid():
    return lax.axis_size(EP) == LINE * SIDE * SIDE and lax.axis_size(TP) == SIDE


def shift_line(array, step):
    count = LINE * SIDE * SIDE
    stride = SIDE * SIDE * step
    return lax.ppermute(array, EP, [(i, (i + stride) % count) for i in range(count)])


def swap_side(array, bit):
    return lax.ppermute(array, EP, [(i, i ^ bit) for i in range(LINE * SIDE * SIDE)])


def swap_core(array):
    return lax.ppermute(array, TP, [(0, 1), (1, 0)])


def add_low(*arrays):
    return sum(array.astype(F32) for array in arrays).astype(BF)


def member_at(half, place):
    me = lax.axis_index(EP)
    near = lax.rem(me, SIDE * SIDE)
    flip, back = lax.div(place, LINE), lax.rem(place, LINE)
    if half:
        flip = lax.div(flip, SIDE) + SIDE * lax.rem(flip, SIDE)
    line = lax.rem(lax.div(me, SIDE * SIDE) + LINE - back, LINE)
    return line * SIDE * SIDE + lax.bitwise_xor(near, flip)


def sum_everywhere(mine, other):
    other = swap_core(other)
    half = LINE * SIDE
    kept, sent = [], []
    for part, bit in ((0, 2), (1, 1)):
        sent.append(swap_side(add_low(mine[part, half:], other[part, half:]), bit))
        kept.append(add_low(mine[part, :half], other[part, :half]))
    pieces = []
    for keep, got, bit in ((kept[0], sent[0], 1), (kept[1], sent[1], 2)):
        pieces.append(
            (add_low(keep[:LINE], got[:LINE]), swap_side(add_low(keep[LINE:], got[LINE:]), bit))
        )
    both = jnp.concatenate([add_low(*pair) for pair in pieces], axis=1)
    parts = [both[0]] + [shift_line(both[step], -step) for step in range(1, LINE)]
    total = add_low(*parts)
    line = [total] + [shift_line(total, step) for step in range(1, LINE)]
    rows = total.shape[0] // 2
    near, far = [], []
    for rest, bit in ((slice(0, rows), 1), (slice(rows, 2 * rows), 2)):
        part = jnp.stack([array[rest] for array in line])
        near.append(jnp.concatenate([part, swap_side(part, bit)]))
    far = [swap_side(near[0], 2), swap_side(near[1], 1)]
    others = [swap_core(part) for part in near]
    others += [swap_core(part) for part in far]
    return [*near, *far, *others]


def finish_kernel(count, *refs):
    pieces, (*outs, router_ref, gain_ref) = refs[:count], refs[count:-1]
    side_ref = refs[-1]
    places, rows, _ = pieces[0].shape
    members = LINE * SIDE * SIDE
    core = lax.axis_index(TP)

    def step(place, carry):
        for which, ref in enumerate(pieces):
            half = which % 2
            far = which // 2 % 2
            owner = core if which < count // 2 else 1 - core
            member = member_at(half, far * places + place)
            start = owner * (members * 2 * rows) + member * (2 * rows) + half * rows
            start = pl.multiple_of(start, rows)
            column = 0
            for out in (*outs, side_ref):
                width = out.shape[1]
                out[pl.ds(start, rows), :] = ref[place, :, column : column + width].astype(F32)
                column += width
        return carry

    lax.fori_loop(0, places, step, 0)
    for block in range(gain_ref.shape[0]):
        turned = side_ref[block * LANES : (block + 1) * LANES, :].T
        gain_ref[block : block + 1, :] = turned[LANES - 1 :, :]
        if router_ref is not None:
            cols = slice(block * LANES, (block + 1) * LANES)
            router_ref[:, cols] = turned[: router_ref.shape[0], :]


def finish(pieces, widths, experts):
    rows = SIDE * LINE * SIDE * SIDE * 2 * pieces[0].shape[1]
    kernel = functools.partial(finish_kernel, len(pieces))
    if not experts:
        kernel = functools.partial(finish_plain_kernel, len(pieces))
    shapes = [sds((rows, width), F32) for width in widths]
    shapes += [sds((experts, rows), F32)] if experts else []
    return call(
        kernel,
        [*shapes, sds((rows // LANES, LANES), F32)],
        0,
        6 * rows * sum(widths),
        scratch_shapes=[pltpu.VMEM((rows, LANES), F32)],
    )(*pieces)


def finish_plain_kernel(count, *refs):
    finish_kernel(count, *refs[:-2], None, *refs[-2:])


def split_sum(low_ref, mine_ref, other_ref):
    _, members, rows, _ = mine_ref.shape
    core = lax.axis_index(TP)

    def step(place, carry):
        for half in range(2):
            member = member_at(half, place)
            for owner, ref in ((core, mine_ref), (1 - core, other_ref)):
                start = owner * (members * 2 * rows) + member * (2 * rows) + half * rows
                ref[half, place] = low_ref[pl.ds(pl.multiple_of(start, rows), rows), :]
        return carry

    lax.fori_loop(0, members, step, 0)


def sum_shapes(rows, width):
    if not on_grid():
        return ([sds((rows, width), BF)], [])
    members = LINE * SIDE * SIDE
    part = sds((2, members, rows // (2 * SIDE * members), width), BF)
    return ([part, part], [pltpu.VMEM((rows, width), BF)])


def gather_rows(chunk):
    rows, _ = chunk.shape
    if not on_grid():
        whole = lax.all_gather(chunk, EP, axis=0, tiled=True)
        block = min(512, whole.shape[0])
        return [[whole[i : i + block]] for i in range(0, whole.shape[0], block)]
    half = rows // 2
    far = swap_side(chunk, FAR)
    near, away = [], []
    for rest, bits in ((slice(0, half), (1, 2)), (slice(half, rows), (2, 1))):
        part = jnp.concatenate([chunk[rest], far[rest]])
        part = jnp.concatenate([part, swap_side(part, bits[0])])
        near.append(part)
        away.append(swap_side(part, bits[1]))
    return [near, away]


def scatter_rows(blocks):
    if not on_grid():
        whole = jnp.concatenate([array for part in blocks for array in part])
        return (lax.psum_scatter(whole, EP, scatter_dimension=0, tiled=True), None)
    near, away = blocks
    mine, theirs = [], []
    for own, sent, bits in ((near[0], away[0], (1, 2)), (near[1], away[1], (2, 1))):
        other = swap_side(sent, bits[1])
        count = own.shape[0] // 2
        far = swap_side(add_low(own[count:], other[count:]), bits[0])
        kept = add_low(own[:count], other[:count])
        count //= 2
        theirs.append(add_low(kept[count:], far[count:]))
        mine.append(add_low(kept[:count], far[:count]))
    return (jnp.concatenate(mine), swap_side(jnp.concatenate(theirs), FAR))


def expert_pieces(weights, axes):
    if not on_grid():
        whole = [lax.all_gather(w, TP, axis=axis, tiled=True) for w, axis in zip(weights, axes)]
        return ([whole], (0,))
    near = [swap_side(w, NEAR) for w in weights[:2]]
    near.append(swap_side(weights[2], NEAR))
    across = [swap_core(w) for w in weights]
    both = [swap_core(w) for w in near[:2]]
    both.append(swap_core(near[2]))
    return ([list(weights), across, near, both], (0, 0, 1, 1))


def rope_tables(seq_len):
    half_dim = HEAD_DIM // 2
    freq = THETA ** (-(np.arange(half_dim, dtype=np.float64) * 2.0) / HEAD_DIM)
    angles = np.arange(seq_len, dtype=np.float64)[:, None] * freq[None, :]
    cosine, sine = np.cos(angles), np.sin(angles)
    repeats = LANES // HEAD_DIM
    cosine = np.tile(np.concatenate([cosine, cosine], axis=1), (1, repeats))
    sine = np.tile(np.concatenate([-sine, sine], axis=1), (1, repeats))
    return (cosine.astype(np.float32), sine.astype(np.float32))


def swap_halves(values):
    lane = lax.broadcasted_iota(jnp.int32, values.shape, 1)
    leading = lax.rem(lane, HEAD_DIM) < HEAD_DIM // 2
    half = HEAD_DIM // 2
    return jnp.where(
        leading, pltpu.roll(values, LANES - half, 1), pltpu.roll(values, half, 1)
    )


def own_rows(ref, rows):
    return ref[pl.ds(pl.multiple_of(lax.axis_index(TP) * rows, rows), rows), :]


def blocks(width):
    return [slice(start, start + LANES) for start in range(0, width, LANES)]


def head_slice(index):
    return slice(index * HEAD_DIM, (index + 1) * HEAD_DIM)


def call(kernel, out_shape, flops, nbytes, **options):
    return pl.pallas_call(
        kernel,
        out_shape=out_shape,
        compiler_params=pltpu.CompilerParams(vmem_limit_bytes=VMEM_LIMIT),
        cost_estimate=pl.CostEstimate(flops=flops, bytes_accessed=nbytes, transcendentals=0),
        **options,
    )


def project_kernel(
    tok_ref, gain_ref, wq_ref, wk_ref, wv_ref, cos_ref, sin_ref, norm_ref, q_ref, kv_ref
):
    values = tok_ref[...].astype(F32)
    inverse = lax.rsqrt(jnp.mean(values * values, axis=1, keepdims=True) + EPS)
    normed = (values * inverse * gain_ref[...].astype(F32)).astype(BF)
    norm_ref[...] = normed
    cosine, sine = own_rows(cos_ref, values.shape[0]), own_rows(sin_ref, values.shape[0])
    query = jnp.dot(normed, wq_ref[...], preferred_element_type=F32)
    for cols in blocks(query.shape[1]):
        part = query[:, cols]
        q_ref[:, cols] = (part * cosine + swap_halves(part) * sine).astype(BF)
    key = jnp.dot(normed, wk_ref[...], preferred_element_type=F32)
    for cols in blocks(key.shape[1]):
        part = key[:, cols]
        kv_ref[:, cols] = (part * cosine + swap_halves(part) * sine).astype(BF)
    value = jnp.dot(normed, wv_ref[...], preferred_element_type=F32)
    kv_ref[:, key.shape[1] :] = value.astype(BF)


def pair_rows(ref, group):
    left = ref[:, head_slice(GROUP * group)]
    right = ref[:, head_slice(GROUP * group + 1)]
    return jnp.concatenate([left, right], axis=0)


def pair_columns(values):
    rows = values.shape[0] // GROUP
    return jnp.concatenate([values[:rows], values[rows:]], axis=1)


def stacked(refs, cols):
    return jnp.concatenate([ref[:, cols] for ref in refs], axis=0)


def allowed_pairs(seg_ref, rows, own_first):
    seg = seg_ref[...]
    total = seg.shape[1]
    core = lax.axis_index(TP)
    own = seg[:, :rows]
    for part in range(1, total // rows):
        own = jnp.where(core == part, seg[:, part * rows : (part + 1) * rows], own)
    position = lax.broadcasted_iota(jnp.int32, (1, total), 1)
    if own_first:
        other = jnp.where(core == 0, seg[:, rows:], seg[:, :rows])
        seg = jnp.concatenate([own, other], axis=1)
        position = lax.rem(position + core * rows, total)
    column = jnp.broadcast_to(own.astype(F32), (rows, rows)).T[:, 0:1]
    place = core * rows + lax.broadcasted_iota(jnp.int32, (rows, 1), 0)
    allowed = (place >= position) & (column == seg.astype(F32))
    return jnp.concatenate([jnp.where(allowed, 1.0, 0.0)] * GROUP, axis=0) > 0.5


def lanes_of(values):
    rows, experts = values.shape
    return jnp.concatenate([values, jnp.zeros((rows, LANES - experts), values.dtype)], axis=1)


def gate_rows(logits, has):
    has, logits = has > 0, lanes_of(logits)
    logits = jnp.where(has, logits, -jnp.inf)
    weight = jnp.exp(logits - jnp.max(logits, axis=1, keepdims=True))
    return weight / jnp.sum(weight, axis=1, keepdims=True)


def attend_kernel(
    q_ref, kv_refs, seg_ref, wp_ref, tok_ref, gain_ref, router_ref, has_ref,
    att_ref, lse_ref, hid_ref, moe_ref, gates_ref,
):
    rows = q_ref.shape[0]
    allowed = allowed_pairs(seg_ref, rows, len(kv_refs) > 1)
    lane = lax.broadcasted_iota(jnp.int32, (rows, LANES), 1)
    kept = jnp.zeros((rows, LANES), F32)
    for group in range(KV_HEADS):
        query = pair_rows(q_ref, group)
        key = stacked(kv_refs, head_slice(group))
        value = stacked(kv_refs, head_slice(KV_HEADS + group))
        scores = lax.dot_general(query, key, INNER, preferred_element_type=F32)
        scores = jnp.where(allowed, scores * HEAD_DIM ** (-0.5), MASKED)
        highest = jnp.max(scores, axis=1, keepdims=True)
        exponent = jnp.exp(scores - highest)
        totals = jnp.sum(exponent, axis=1, keepdims=True)
        probs = (exponent / totals).astype(BF)
        blended = jnp.dot(probs, value, preferred_element_type=F32)
        cols = slice(group * GROUP * HEAD_DIM, (group + 1) * GROUP * HEAD_DIM)
        att_ref[:, cols] = pair_columns(blended).astype(BF)
        log_total = highest + jnp.log(totals)
        for which in range(GROUP):
            column = log_total[which * rows : (which + 1) * rows]
            kept = jnp.where(lane == GROUP * group + which, column, kept)
    lse_ref[...] = kept
    hidden = tok_ref[...].astype(F32) + jnp.dot(
        att_ref[...], wp_ref[...], preferred_element_type=F32
    )
    hid_ref[...] = hidden
    inverse = lax.rsqrt(jnp.mean(hidden * hidden, axis=1, keepdims=True) + EPS)
    normed = (hidden * inverse * gain_ref[...].astype(F32)).astype(BF)
    moe_ref[...] = normed
    logits = jnp.dot(normed, router_ref[...], preferred_element_type=F32)
    gates_ref[...] = gate_rows(logits, has_ref[...])


def expert_kernel(count, slots, based, *refs):
    pieces = len(slots)
    row_refs, cot_refs = refs[:count], refs[count : 2 * count]
    weight_refs = refs[2 * count : 2 * count + 3 * pieces]
    router_ref, *results = refs[2 * count + 3 * pieces :]
    base_refs, results = results[: 2 * count * based], results[2 * count * based :]
    lane = lax.broadcasted_iota(jnp.int32, (1, LANES), 1)
    owned = [lax.bitwise_xor(lax.axis_index(EP), NEAR * slot) for slot in range(1 + max(slots))]
    chosen = [jnp.where(lane == expert, 1.0, 0.0) for expert in owned]
    finer = [jnp.where(lane == expert + HALF_LANES, 1.0, 0.0) for expert in owned]
    for block in range(count):
        out_ref, gin_ref, act_ref, gga_ref, gua_ref = results[block::count]
        rows = row_refs[block][...]
        width = rows.shape[1]
        cots = cot_refs[block][:, :width]
        logits = jnp.dot(rows, router_ref[...], preferred_element_type=F32)
        gates = gate_rows(logits, cot_refs[block][:, width:])
        out = gin = None
        kept = jnp.zeros(gates.shape, F32)
        if based:
            out = base_refs[block][...]
            gin = base_refs[count + block][:, :width]
            kept = base_refs[count + block][:, width:]
        gate_grads = {}
        for piece, slot in enumerate(slots):
            wg_ref, wu_ref, wd_ref = weight_refs[3 * piece : 3 * piece + 3]
            gate = jnp.sum(gates * chosen[slot], axis=1, keepdims=True)
            gate_act = jnp.dot(rows, wg_ref[...], preferred_element_type=F32)
            up_act = jnp.dot(rows, wu_ref[...], preferred_element_type=F32)
            back = lax.dot_general(cots, wd_ref[...], INNER, preferred_element_type=F32)
            sigmoid_gate = 1.0 / (1.0 + jnp.exp(-gate_act))
            silu_gate = gate_act * sigmoid_gate
            acted = (silu_gate * up_act).astype(BF).astype(F32)
            part = jnp.sum(acted * back, axis=1, keepdims=True)
            gate_grads[slot] = part + gate_grads.get(slot, 0.0)
            acted_low = (acted * gate).astype(BF)
            grad_acted = back * gate
            grad_up_act = (grad_acted * silu_gate).astype(BF)
            grad_gate_act = (
                grad_acted * up_act * sigmoid_gate * (1.0 + gate_act * (1.0 - sigmoid_gate))
            ).astype(BF)
            hidden = wg_ref.shape[1]
            cols = slice(piece * hidden, (piece + 1) * hidden)
            act_ref[:, cols], gga_ref[:, cols], gua_ref[:, cols] = (
                acted_low, grad_gate_act, grad_up_act,
            )
            part = jnp.dot(acted_low, wd_ref[...], preferred_element_type=F32)
            out = part if out is None else out + part
            part = lax.dot_general(
                grad_gate_act, wg_ref[...], INNER, preferred_element_type=F32
            ) + lax.dot_general(grad_up_act, wu_ref[...], INNER, preferred_element_type=F32)
            gin = part if gin is None else gin + part
        for slot, grad in gate_grads.items():
            coarse = grad.astype(BF).astype(F32)
            kept += coarse * chosen[slot] + (grad - coarse) * finer[slot]
        out_ref[...] = out.astype(out_ref.dtype)
        gin_ref[:, :width] = gin.astype(gin_ref.dtype)
        gin_ref[:, width:] = kept.astype(gin_ref.dtype)


def run_expert(rows, cots, pieces, slots, router, base=(), last=True):
    count = len(rows)
    width, hidden = pieces[0][0].shape
    total = sum(part.shape[0] for part in rows)
    wide = hidden * len(pieces)
    kind = BF if last else F32
    columns = ((width, kind), (width + LANES, kind), (wide, BF), (wide, BF), (wide, BF))
    out = call(
        functools.partial(expert_kernel, count, slots, bool(base)),
        [sds((part.shape[0], cols), dtype) for cols, dtype in columns for part in rows],
        12 * total * width * wide,
        6 * width * wide + 10 * total * width,
    )(*rows, *cots, *[w for piece in pieces for w in piece], router, *base)
    return [out[i * count : (i + 1) * count] for i in range(len(columns))]


def run_near(rows, cots, pieces, slots, router):
    half = len(slots) // 2
    out, gin, *first = run_expert(rows, cots, pieces[:half], slots[:half], router, last=False)
    out, gin, *second = run_expert(
        rows, cots, pieces[half:], slots[half:], router, base=(*out, *gin)
    )
    return [out, gin, *[list(zip(*pair)) for pair in zip(first, second)]]


def weights_kernel(counts, slots, hidden, *refs):
    refs = list(refs)
    rows, cots = [refs.pop(0) for _ in counts], [refs.pop(0) for _ in counts]
    acts, ggas, guas = ([[refs.pop(0) for _ in range(n)] for n in counts] for _ in range(3))
    results = refs
    width = rows[0].shape[1]

    def tall(parts, cols):
        return jnp.concatenate([ref[:, cols] for ref in parts], axis=0)

    def piece_of(parts, piece):
        found = []
        for block in parts:
            each = len(slots) // len(block)
            start = piece % each * hidden
            found.append(block[piece // each][:, start : start + hidden])
        return jnp.concatenate(found, axis=0)

    rows = tall(rows, slice(0, width))
    cots = tall(cots, slice(0, width))
    for piece in range(len(slots)):
        gate = lax.dot_general(rows, piece_of(ggas, piece), OUTER, preferred_element_type=F32)
        up = lax.dot_general(rows, piece_of(guas, piece), OUTER, preferred_element_type=F32)
        down = lax.dot_general(piece_of(acts, piece), cots, OUTER, preferred_element_type=F32)
        if piece % 2:
            wide_ref, tall_ref = results[-2:]
            at = (piece // 2) * 2 * hidden
            wide_ref[:, at : at + hidden] = gate.astype(BF)
            wide_ref[:, at + hidden : at + 2 * hidden] = up.astype(BF)
            at = (piece // 2) * hidden
            tall_ref[at : at + hidden, :] = down.astype(BF)
        else:
            gate_ref, up_ref, down_ref = results[3 * (piece // 2) : 3 * (piece // 2) + 3]
            gate_ref[...], up_ref[...], down_ref[...] = gate, up, down


def weight_grads(rows, cots, acts, ggas, guas, slots, hidden):
    width = rows[0].shape[1]
    wide = hidden * len(slots)
    total = sum(part.shape[0] for part in rows)
    shapes = []
    for _ in range(0, len(slots), 2):
        shapes += [sds((width, hidden), F32), sds((width, hidden), F32), sds((hidden, width), F32)]
    if len(slots) > 1:
        shapes += [sds((width, wide), BF), sds((wide // 2, width), BF)]
    out = call(
        functools.partial(weights_kernel, tuple(len(block) for block in acts), slots, hidden),
        shapes,
        6 * total * width * wide,
        12 * width * wide + 4 * total * (width + wide),
    )(*rows, *cots, *[array for parts in (acts, ggas, guas) for block in parts for array in block])
    if not on_grid():
        return [
            lax.psum_scatter(grad, TP, scatter_dimension=axis, tiled=True)
            for grad, axis in zip(out, (1, 1, 0))
        ], []
    wide_part, tall_part = swap_core(out[6]), swap_core(out[7])
    slabs = [wide_part[:, i * hidden : (i + 1) * hidden] for i in range(4)]
    near_wide = jnp.concatenate([out[3] + slabs[2], out[4] + slabs[3]], axis=1).astype(BF)
    near_tall = (out[5] + tall_part[hidden:]).astype(BF)
    near_wide, near_tall = swap_side(near_wide, NEAR), swap_side(near_tall, NEAR)
    return (out[:3], [wide_part, tall_part, near_wide, near_tall])


def ending_kernel(
    gate_ref, up_ref, down_ref, wide_ref, tall_ref, near_wide_ref, near_tall_ref, hid_ref, *refs
):
    part_refs, outs = refs[:-4], refs[-4:]
    hidden = gate_ref.shape[1]
    for part, (ref, out) in enumerate(zip((gate_ref, up_ref), outs)):
        cols = slice(part * hidden, (part + 1) * hidden)
        out[...] = ref[...] + wide_ref[:, cols].astype(F32) + near_wide_ref[:, cols].astype(F32)
    outs[2][...] = (
        down_ref[...] + tall_ref[:hidden, :].astype(F32) + near_tall_ref[...].astype(F32)
    )
    outs[3][...] = (hid_ref[...] + sum(ref[...].astype(F32) for ref in part_refs)).astype(BF)


def ending(grads, parts, hidden, blended):
    blended = [part for part in blended if part is not None]
    if not parts:
        return (*grads, (hidden + sum(part.astype(F32) for part in blended)).astype(BF))
    return call(
        ending_kernel,
        [*[sds(grad.shape, F32) for grad in grads], sds(hidden.shape, BF)],
        0,
        15 * grads[0].size * 2,
    )(*grads, *parts, hidden, *blended)


def column_sums(product):
    coarse = product.astype(BF)
    fine = (product - coarse.astype(F32)).astype(BF)
    ones = jnp.ones((product.shape[0], LANES), BF)
    return lax.dot_general(coarse, ones, OUTER, preferred_element_type=F32) + lax.dot_general(
        fine, ones, OUTER, preferred_element_type=F32
    )


def branch_kernel(
    gin_refs, hid_ref, gain_ref, cot_ref, gates_ref, router_ref, moe_ref, att_ref, wp_ref,
    ghid_ref, gatt_ref, *pay_refs,
):
    pay_ref = pay_refs[-1]
    width = hid_ref.shape[1]
    gates = gates_ref[...]
    grads = sum(ref[:, :width].astype(F32) for ref in gin_refs)
    dgate = sum(ref[:, width:].astype(F32) for ref in gin_refs)
    dgate = dgate + pltpu.roll(dgate, HALF_LANES, 1)
    total = jnp.sum(gates * dgate, axis=1, keepdims=True)
    grad_logits = (gates * (dgate - total)).astype(BF)
    experts = router_ref.shape[1]
    upstream = grads + lax.dot_general(
        grad_logits[:, :experts], router_ref[...], INNER, preferred_element_type=F32
    )
    hidden = hid_ref[...]
    inverse = lax.rsqrt(jnp.mean(hidden * hidden, axis=1, keepdims=True) + EPS)
    scaled = hidden * inverse
    product = upstream * scaled
    weighted = upstream * gain_ref[...].astype(F32)
    mean = jnp.mean(weighted * scaled, axis=1, keepdims=True)
    grad_hidden = cot_ref[...].astype(F32) + inverse * (weighted - scaled * mean)
    ghid_ref[...] = grad_hidden
    grad_branch = grad_hidden.astype(BF)
    gatt_ref[...] = lax.dot_general(
        grad_branch, wp_ref[...], INNER, preferred_element_type=F32
    ).astype(BF)
    pay_ref[:, :width] = lax.dot_general(
        att_ref[...], grad_branch, OUTER, preferred_element_type=F32
    ).astype(BF)
    grad_router = lax.dot_general(moe_ref[...], grad_logits, OUTER, preferred_element_type=F32)
    lane = lax.broadcasted_iota(jnp.int32, grad_router.shape, 1)
    pay_ref[:, width:] = jnp.where(lane == LANES - 1, column_sums(product), grad_router).astype(BF)
    if len(pay_refs) > 1:
        split_sum(pay_ref, *pay_refs[:2])


def attend_back_kernel(
    gatt_ref, q_ref, kv_refs, lse_ref, seg_ref, cos_ref, sin_ref, gq_ref, *gkv_refs
):
    rows = q_ref.shape[0]
    allowed = allowed_pairs(seg_ref, rows, len(kv_refs) > 1)
    cosine, sine = own_rows(cos_ref, rows), own_rows(sin_ref, rows)
    kept = lse_ref[...]
    scale = HEAD_DIM ** (-0.5)
    for pair in range(KV_HEADS // 2):
        grad_keys, grad_values = [], []
        for group in (2 * pair, 2 * pair + 1):
            query = pair_rows(q_ref, group)
            grad = pair_rows(gatt_ref, group)
            key = stacked(kv_refs, head_slice(group))
            value = stacked(kv_refs, head_slice(KV_HEADS + group))
            log_total = jnp.concatenate(
                [kept[:, GROUP * group + i : GROUP * group + i + 1] for i in range(GROUP)], axis=0
            )
            scores = lax.dot_general(query, key, INNER, preferred_element_type=F32)
            scores = jnp.where(allowed, scores * scale, MASKED)
            probs = jnp.exp(scores - log_total)
            grad_values.append(
                lax.dot_general(probs.astype(BF), grad, OUTER, preferred_element_type=F32)
            )
            grad_probs = lax.dot_general(grad, value, INNER, preferred_element_type=F32)
            delta = jnp.sum(probs * grad_probs, axis=1, keepdims=True)
            grad_scores = (probs * (grad_probs - delta)).astype(BF)
            grad_query = jnp.dot(grad_scores, key, preferred_element_type=F32) * scale
            grad_query = pair_columns(grad_query).astype(BF).astype(F32)
            cols = slice(group * GROUP * HEAD_DIM, (group + 1) * GROUP * HEAD_DIM)
            gq_ref[:, cols] = (grad_query * cosine - swap_halves(grad_query) * sine).astype(BF)
            grad_keys.append(
                lax.dot_general(grad_scores, query, OUTER, preferred_element_type=F32) * scale
            )
        for shift, grads in ((0, grad_keys), (KV_HEADS * HEAD_DIM, grad_values)):
            cols = slice(shift + pair * LANES, shift + (pair + 1) * LANES)
            both = jnp.concatenate(grads, axis=1).astype(BF)
            for part, ref in enumerate(gkv_refs):
                ref[:, cols] = both[part * ref.shape[0] : (part + 1) * ref.shape[0]]


def project_back_kernel(
    norm_ref, gq_ref, gkv_refs, cos_ref, sin_ref, wq_ref, wk_ref, wv_ref, tok_ref, gain_ref,
    ghid_ref, gtok_ref, *pay_refs,
):
    gkraw_ref, pay_ref = pay_refs[-1], pay_refs[-2]
    rows = norm_ref.shape[0]
    cosine, sine = own_rows(cos_ref, rows), own_rows(sin_ref, rows)
    kwidth = wk_ref.shape[1]

    def total(cols):
        return add_low(*[ref[:, cols] for ref in gkv_refs])

    for cols in blocks(kwidth):
        part = total(cols).astype(F32)
        gkraw_ref[:, cols] = (part * cosine - swap_halves(part) * sine).astype(BF)
    grad_query, grad_key, grad_value = gq_ref[...], gkraw_ref[...], total(slice(kwidth, 2 * kwidth))
    upstream = lax.dot_general(grad_query, wq_ref[...], INNER, preferred_element_type=F32)
    upstream += lax.dot_general(grad_key, wk_ref[...], INNER, preferred_element_type=F32)
    upstream += lax.dot_general(grad_value, wv_ref[...], INNER, preferred_element_type=F32)
    normed = norm_ref[...]
    start = 0
    for grad in (grad_query, grad_key, grad_value):
        pay_ref[:, start : start + grad.shape[1]] = lax.dot_general(
            normed, grad, OUTER, preferred_element_type=F32
        ).astype(BF)
        start += grad.shape[1]
    values = tok_ref[...].astype(F32)
    inverse = lax.rsqrt(jnp.mean(values * values, axis=1, keepdims=True) + EPS)
    scaled = values * inverse
    pay_ref[:, start:] = column_sums(upstream * scaled).astype(BF)
    weighted = upstream * gain_ref[...].astype(F32)
    mean = jnp.mean(weighted * scaled, axis=1, keepdims=True)
    gtok_ref[...] = (ghid_ref[...] + inverse * (weighted - scaled * mean)).astype(BF)
    if len(pay_refs) > 2:
        split_sum(pay_ref, *pay_refs[:2])


def sds(shape, dtype):
    return jax.ShapeDtypeStruct(shape, dtype)


def layer(
    tokens,
    segment_ids,
    routes,
    cotangent,
    query_weight,
    key_weight,
    value_weight,
    proj_weight,
    attn_gain,
    moe_gain,
    router_weight,
    gate_weight,
    up_weight,
    down_weight,
):
    tok_count, model_dim = tokens.shape
    seq_len = segment_ids.shape[1]
    experts = router_weight.shape[1]
    query_dim, kv_dim = HEADS * HEAD_DIM, KV_HEADS * HEAD_DIM

    has = (routes[:, :, None] == jnp.arange(LANES, dtype=jnp.int32)[None, None, :]).any(axis=1)
    has = has.astype(BF)
    cots = gather_rows(jnp.concatenate([cotangent, has], axis=1))
    pieces, slots = expert_pieces((gate_weight[0], up_weight[0], down_weight[0]), (1, 1, 0))

    cosine, sine = (jnp.asarray(table) for table in rope_tables(seq_len))
    gain_one, gain_two = attn_gain[None, :], moe_gain[None, :]

    normed, query, kv = call(
        project_kernel,
        (
            sds((tok_count, model_dim), BF),
            sds((tok_count, query_dim), BF),
            sds((tok_count, 2 * kv_dim), BF),
        ),
        4 * tok_count * model_dim * model_dim,
        5 * model_dim * model_dim,
    )(tokens, gain_one, query_weight, key_weight, value_weight, cosine, sine)

    if on_grid():
        kv_all = [kv, swap_core(kv)]
    else:
        kv_all = [lax.all_gather(kv, TP, axis=0, tiled=True)]

    attended, log_totals, hidden, moe_input, gates = call(
        attend_kernel,
        (
            sds((tok_count, query_dim), BF),
            sds((tok_count, LANES), F32),
            sds((tok_count, model_dim), F32),
            sds((tok_count, model_dim), BF),
            sds((tok_count, LANES), F32),
        ),
        4 * tok_count * model_dim * model_dim,
        5 * model_dim * model_dim,
    )(query, kv_all, segment_ids, proj_weight, tokens, gain_two, router_weight, has)

    rows = gather_rows(moe_input)
    done = []
    for index, part in enumerate(zip(rows, cots)):
        if on_grid() and not index:
            done.append(run_near(*part, pieces, slots, router_weight))
            continue
        *sums, acts, ggas, guas = run_expert(*part, pieces, slots, router_weight)
        done.append([*sums, *[[(array,) for array in arrays] for arrays in (acts, ggas, guas)]])
    outputs, grad_inputs, acts, ggas, guas = zip(*done)
    grad_rows_in = scatter_rows(grad_inputs)

    def flat(blocks):
        return [array for part in blocks for array in part]

    grads, parts = weight_grads(
        flat(rows), flat(cots), flat(acts), flat(ggas), flat(guas), slots, pieces[0][0].shape[1]
    )
    grad_gate, grad_up, grad_down, layer_out = ending(grads, parts, hidden, scatter_rows(outputs))

    outs, scratch = sum_shapes(model_dim, model_dim + LANES)
    grad_rows_in = [part for part in grad_rows_in if part is not None]
    grad_hidden, grad_attended, *early = call(
        branch_kernel,
        [sds((tok_count, model_dim), F32), sds((tok_count, query_dim), BF), *outs],
        4 * tok_count * model_dim * model_dim,
        5 * model_dim * model_dim,
        scratch_shapes=scratch,
    )(
        grad_rows_in, hidden, gain_two, cotangent, gates, router_weight, moe_input, attended,
        proj_weight,
    )

    count = len(kv_all)
    grad_query, *grad_kv = call(
        attend_back_kernel,
        [sds((tok_count, query_dim), BF)] + [sds((seq_len // count, 2 * kv_dim), BF)] * count,
        4 * tok_count * model_dim * model_dim,
        5 * model_dim * model_dim,
    )(grad_attended, query, kv_all, log_totals, segment_ids, cosine, sine)
    if on_grid():
        grad_kv = [grad_kv[0], swap_core(grad_kv[1])]
    else:
        grad_kv = [lax.psum_scatter(grad_kv[0], TP, scatter_dimension=0, tiled=True)]

    outs, scratch = sum_shapes(model_dim, query_dim + 2 * kv_dim + LANES)
    grad_tokens, *late = call(
        project_back_kernel,
        [sds((tok_count, model_dim), BF), *outs],
        8 * tok_count * model_dim * model_dim,
        9 * model_dim * model_dim,
        scratch_shapes=scratch + [pltpu.VMEM((tok_count, kv_dim), BF)],
    )(
        normed, grad_query, grad_kv, cosine, sine, query_weight, key_weight, value_weight, tokens,
        gain_one, grad_hidden,
    )
    early_widths, late_widths = (model_dim,), (query_dim, kv_dim, kv_dim)
    if on_grid():
        grad_proj, grad_router, gain_grad_two = finish(
            sum_everywhere(*early), early_widths, experts
        )
        *late, gain_grad_one = finish(sum_everywhere(*late), late_widths, 0)
        gain_grad_one, gain_grad_two = gain_grad_one.reshape(-1), gain_grad_two.reshape(-1)
        grad_router = grad_router.T
    else:
        early, late = (
            jnp.split(lax.psum(low.astype(F32), (EP, TP)), np.cumsum(widths), axis=1)
            for low, widths in ((early[0], early_widths), (late[0], late_widths))
        )
        grad_proj, side = early
        grad_router, gain_grad_two = side[:, :experts], side[:, LANES - 1]
        gain_grad_one = late.pop()[:, LANES - 1]
    return (
        layer_out,
        grad_tokens,
        *late,
        grad_proj,
        gain_grad_one,
        gain_grad_two,
        grad_router,
        grad_gate[None],
        grad_up[None],
        grad_down[None],
    )


def solution(mesh):
    placed = (
        P((EP, TP), None),
        P(EP, None),
        P((EP, TP), None),
        P((EP, TP), None),
        P(),
        P(),
        P(),
        P(),
        P(),
        P(),
        P(),
        P(EP, None, TP),
        P(EP, None, TP),
        P(EP, TP, None),
    )
    step = jax.shard_map(
        layer,
        mesh=mesh,
        in_specs=placed,
        out_specs=(
            P((EP, TP), None),
            P((EP, TP), None),
            P(),
            P(),
            P(),
            P(),
            P(),
            P(),
            P(),
            P(EP, None, TP),
            P(EP, None, TP),
            P(EP, TP, None),
        ),
        check_vma=False,
    )
    if mesh.shape[EP] != LINE * SIDE * SIDE or mesh.shape[TP] != SIDE:
        return step
    return step
```

```python
import functools

import jax
import jax.numpy as jnp
import numpy as np
from jax import lax
from jax.experimental import pallas as pl
from jax.experimental.pallas import tpu as pltpu
from jax.sharding import PartitionSpec as P


HEADS = 16
KV_HEADS = 8
HEAD_DIM = 64
GROUP = HEADS // KV_HEADS
LANES = 128

EPS = 1e-06
EP, TP = "ep", "tp"
THETA = 10000.0
MASKED = -1000000000.0


LINE, SIDE = 4, 2
NEAR, FAR = 4, 8
HALF_LANES = LANES // 2
BF, F32 = jnp.bfloat16, jnp.float32
INNER = (((1,), (1,)), ((), ()))
OUTER = (((0,), (0,)), ((), ()))
VMEM_LIMIT = 60 * 1024 * 1024


def on_grid():
    return lax.axis_size(EP) == LINE * SIDE * SIDE and lax.axis_size(TP) == SIDE


def shift_line(array, step):
    count = LINE * SIDE * SIDE
    stride = SIDE * SIDE * step
    return lax.ppermute(array, EP, [(i, (i + stride) % count) for i in range(count)])


def swap_side(array, bit):
    return lax.ppermute(array, EP, [(i, i ^ bit) for i in range(LINE * SIDE * SIDE)])


def swap_core(array):
    return lax.ppermute(array, TP, [(0, 1), (1, 0)])


def add_low(*arrays):
    return sum(array.astype(F32) for array in arrays).astype(BF)


def member_at(half, place):
    me = lax.axis_index(EP)
    near = lax.rem(me, SIDE * SIDE)
    flip, back = lax.div(place, LINE), lax.rem(place, LINE)
    if half:
        flip = lax.div(flip, SIDE) + SIDE * lax.rem(flip, SIDE)
    line = lax.rem(lax.div(me, SIDE * SIDE) + LINE - back, LINE)
    return line * SIDE * SIDE + lax.bitwise_xor(near, flip)


def share_core(mine, other):
    other = swap_core(other)
    half = LINE * SIDE
    kept = [add_low(mine[part, :half], other[part, :half]) for part in range(2)]
    sent = [add_low(mine[part, half:], other[part, half:]) for part in range(2)]
    return kept + sent


def sum_everywhere(*parts):
    kept, sent = parts[:2], parts[2:]
    sent = [swap_side(sent[0], 2), swap_side(sent[1], 1)]
    pieces = []
    for keep, got, bit in ((kept[0], sent[0], 1), (kept[1], sent[1], 2)):
        pieces.append(
            (add_low(keep[:LINE], got[:LINE]), swap_side(add_low(keep[LINE:], got[LINE:]), bit))
        )
    both = jnp.concatenate([add_low(*pair) for pair in pieces], axis=1)
    parts = [both[0]] + [shift_line(both[step], -step) for step in range(1, LINE)]
    total = add_low(*parts)
    line = [total] + [shift_line(total, step) for step in range(1, LINE)]
    rows = total.shape[0] // 2
    near, far = [], []
    for rest, bit in ((slice(0, rows), 1), (slice(rows, 2 * rows), 2)):
        part = jnp.stack([array[rest] for array in line])
        near.append(jnp.concatenate([part, swap_side(part, bit)]))
    far = [swap_side(near[0], 2), swap_side(near[1], 1)]
    others = [swap_core(part) for part in near]
    others += [swap_core(part) for part in far]
    return [*near, *far, *others]


def finish_kernel(count, *refs):
    pieces, (*outs, router_ref, gain_ref) = refs[:count], refs[count:-1]
    side_ref = refs[-1]
    places, rows, _ = pieces[0].shape
    members = LINE * SIDE * SIDE
    core = lax.axis_index(TP)

    def step(place, carry):
        for which, ref in enumerate(pieces):
            half = which % 2
            far = which // 2 % 2
            owner = core if which < count // 2 else 1 - core
            member = member_at(half, far * places + place)
            start = owner * (members * 2 * rows) + member * (2 * rows) + half * rows
            start = pl.multiple_of(start, rows)
            column = 0
            for out in (*outs, side_ref):
                width = out.shape[1]
                out[pl.ds(start, rows), :] = ref[place, :, column : column + width].astype(F32)
                column += width
        return carry

    lax.fori_loop(0, places, step, 0)
    for block in range(gain_ref.shape[0]):
        cols = slice(block * LANES, (block + 1) * LANES)
        turned = side_ref[cols, :].T
        if router_ref is not None:
            gain_ref[block : block + 1, :] = turned[LANES - 1 :, :]
            router_ref[:, cols] = turned[: router_ref.shape[0], :]
        else:
            gain_ref[block : block + 1, :] = turned[:1, :]
    if router_ref is None:
        count = gain_ref.shape[0]
        for block in range(count):
            turned = side_ref[block * LANES : (block + 1) * LANES, :].T
            place = (block + count // 2) % count
            gain_ref[place : place + 1, :] += turned[LANES - 1 :, :]


def finish(pieces, widths, experts):
    rows = SIDE * LINE * SIDE * SIDE * 2 * pieces[0].shape[1]
    kernel = functools.partial(finish_kernel, len(pieces))
    if not experts:
        kernel = functools.partial(finish_plain_kernel, len(pieces))
    shapes = [sds((rows, width), F32) for width in widths]
    shapes += [sds((experts, rows), F32)] if experts else []
    return call(
        kernel,
        [*shapes, sds((rows // LANES, LANES), F32)],
        0,
        6 * rows * sum(widths),
        scratch_shapes=[pltpu.VMEM((rows, LANES), F32)],
    )(*pieces)


def finish_plain_kernel(count, *refs):
    finish_kernel(count, *refs[:-2], None, *refs[-2:])


def split_sum(low_ref, mine_ref, other_ref):
    _, members, rows, _ = mine_ref.shape
    core = lax.axis_index(TP)

    def step(place, carry):
        for half in range(2):
            member = member_at(half, place)
            for owner, ref in ((core, mine_ref), (1 - core, other_ref)):
                start = owner * (members * 2 * rows) + member * (2 * rows) + half * rows
                ref[half, place] = low_ref[pl.ds(pl.multiple_of(start, rows), rows), :]
        return carry

    lax.fori_loop(0, members, step, 0)


def spread_sum(low_ref, *outs):
    near, rows, _ = outs[0].shape

    def step(place, carry):
        for half in range(2):
            for far in range(2):
                start = member_at(half, far * near + place) * (2 * rows) + half * rows
                outs[2 * far + half][place] = low_ref[pl.ds(pl.multiple_of(start, rows), rows), :]
        return carry

    lax.fori_loop(0, near, step, 0)


def late_shapes(rows, width):
    if not on_grid():
        return ([sds((rows, width), BF)], [])
    members = LINE * SIDE * SIDE
    part = sds((members // 2, rows // (2 * SIDE * members), width), BF)
    return ([part] * 4, [pltpu.VMEM((rows // SIDE, width), BF)])


def sum_shapes(rows, width):
    if not on_grid():
        return ([sds((rows, width), BF)], [])
    members = LINE * SIDE * SIDE
    part = sds((2, members, rows // (2 * SIDE * members), width), BF)
    return ([part, part], [pltpu.VMEM((rows, width), BF)])


def gather_rows(chunk):
    rows, _ = chunk.shape
    if not on_grid():
        whole = lax.all_gather(chunk, EP, axis=0, tiled=True)
        block = min(512, whole.shape[0])
        return [[whole[i : i + block]] for i in range(0, whole.shape[0], block)]
    half = rows // 2
    far = swap_side(chunk, FAR)
    near, away = [], []
    for rest, bits in ((slice(0, half), (1, 2)), (slice(half, rows), (2, 1))):
        part = jnp.concatenate([chunk[rest], far[rest]])
        part = jnp.concatenate([part, swap_side(part, bits[0])])
        near.append(part)
        away.append(swap_side(part, bits[1]))
    return [near, away]


def scatter_rows(blocks):
    if not on_grid():
        whole = jnp.concatenate([array for part in blocks for array in part])
        return (lax.psum_scatter(whole, EP, scatter_dimension=0, tiled=True), None)
    near, away = blocks
    mine, theirs = [], []
    for own, sent, bits in ((near[0], away[0], (1, 2)), (near[1], away[1], (2, 1))):
        other = swap_side(sent, bits[1])
        count = own.shape[0] // 2
        far = swap_side(add_low(own[count:], other[count:]), bits[0])
        kept = add_low(own[:count], other[:count])
        count //= 2
        theirs.append(add_low(kept[count:], far[count:]))
        mine.append(add_low(kept[:count], far[:count]))
    return (jnp.concatenate(mine), swap_side(jnp.concatenate(theirs), FAR))


def expert_pieces(weights, axes):
    if not on_grid():
        whole = [lax.all_gather(w, TP, axis=axis, tiled=True) for w, axis in zip(weights, axes)]
        return ([whole], (0,))
    near = [swap_side(w, NEAR) for w in weights[:2]]
    near.append(swap_side(weights[2], NEAR))
    across = [swap_core(w) for w in weights]
    both = [swap_core(w) for w in near[:2]]
    both.append(swap_core(near[2]))
    return ([list(weights), across, near, both], (0, 0, 1, 1))


def rope_tables(seq_len):
    half_dim = HEAD_DIM // 2
    freq = THETA ** (-(np.arange(half_dim, dtype=np.float64) * 2.0) / HEAD_DIM)
    angles = np.arange(seq_len, dtype=np.float64)[:, None] * freq[None, :]
    cosine, sine = np.cos(angles), np.sin(angles)
    repeats = LANES // HEAD_DIM
    cosine = np.tile(np.concatenate([cosine, cosine], axis=1), (1, repeats))
    sine = np.tile(np.concatenate([-sine, sine], axis=1), (1, repeats))
    return (cosine.astype(np.float32), sine.astype(np.float32))


def swap_halves(values):
    lane = lax.broadcasted_iota(jnp.int32, values.shape, 1)
    leading = lax.rem(lane, HEAD_DIM) < HEAD_DIM // 2
    half = HEAD_DIM // 2
    return jnp.where(
        leading, pltpu.roll(values, LANES - half, 1), pltpu.roll(values, half, 1)
    )


def own_rows(ref, rows, other=False):
    core = lax.axis_index(TP)
    core = 1 - core if other else core
    return ref[pl.ds(pl.multiple_of(core * rows, rows), rows), :]


def blocks(width):
    return [slice(start, start + LANES) for start in range(0, width, LANES)]


def head_slice(index):
    return slice(index * HEAD_DIM, (index + 1) * HEAD_DIM)


def call(kernel, out_shape, flops, nbytes, **options):
    return pl.pallas_call(
        kernel,
        out_shape=out_shape,
        compiler_params=pltpu.CompilerParams(vmem_limit_bytes=VMEM_LIMIT),
        cost_estimate=pl.CostEstimate(flops=flops, bytes_accessed=nbytes, transcendentals=0),
        **options,
    )


def project_kernel(
    tok_ref, gain_ref, wq_ref, wk_ref, wv_ref, cos_ref, sin_ref, norm_ref, q_ref, kv_ref
):
    values = tok_ref[...].astype(F32)
    inverse = lax.rsqrt(jnp.mean(values * values, axis=1, keepdims=True) + EPS)
    normed = (values * inverse * gain_ref[...].astype(F32)).astype(BF)
    norm_ref[...] = normed
    cosine, sine = own_rows(cos_ref, values.shape[0]), own_rows(sin_ref, values.shape[0])
    query = jnp.dot(normed, wq_ref[...], preferred_element_type=F32)
    for cols in blocks(query.shape[1]):
        part = query[:, cols]
        q_ref[:, cols] = (part * cosine + swap_halves(part) * sine).astype(BF)
    key = jnp.dot(normed, wk_ref[...], preferred_element_type=F32)
    for cols in blocks(key.shape[1]):
        part = key[:, cols]
        kv_ref[:, cols] = (part * cosine + swap_halves(part) * sine).astype(BF)
    value = jnp.dot(normed, wv_ref[...], preferred_element_type=F32)
    kv_ref[:, key.shape[1] :] = value.astype(BF)


def pair_rows(ref, group):
    left = ref[:, head_slice(GROUP * group)]
    right = ref[:, head_slice(GROUP * group + 1)]
    return jnp.concatenate([left, right], axis=0)


def pair_columns(values):
    rows = values.shape[0] // GROUP
    return jnp.concatenate([values[:rows], values[rows:]], axis=1)


def stacked(refs, cols):
    return jnp.concatenate([ref[:, cols] for ref in refs], axis=0)


def allowed_pairs(seg_ref, rows, own_first):
    seg = seg_ref[...]
    total = seg.shape[1]
    core = lax.axis_index(TP)
    own = seg[:, :rows]
    for part in range(1, total // rows):
        own = jnp.where(core == part, seg[:, part * rows : (part + 1) * rows], own)
    position = lax.broadcasted_iota(jnp.int32, (1, total), 1)
    if own_first:
        other = jnp.where(core == 0, seg[:, rows:], seg[:, :rows])
        seg = jnp.concatenate([own, other], axis=1)
        position = lax.rem(position + core * rows, total)
    column = jnp.broadcast_to(own.astype(F32), (rows, rows)).T[:, 0:1]
    place = core * rows + lax.broadcasted_iota(jnp.int32, (rows, 1), 0)
    allowed = (place >= position) & (column == seg.astype(F32))
    return jnp.concatenate([jnp.where(allowed, 1.0, 0.0)] * GROUP, axis=0) > 0.5


def lanes_of(values):
    rows, experts = values.shape
    return jnp.concatenate([values, jnp.zeros((rows, LANES - experts), values.dtype)], axis=1)


def gate_rows(logits, has):
    has, logits = has > 0, lanes_of(logits)
    logits = jnp.where(has, logits, -jnp.inf)
    weight = jnp.exp(logits - jnp.max(logits, axis=1, keepdims=True))
    return weight / jnp.sum(weight, axis=1, keepdims=True)


def attend_kernel(
    q_ref, kv_refs, seg_ref, wp_ref, tok_ref, gain_ref, router_ref, has_ref,
    att_ref, lse_ref, hid_ref, moe_ref, gates_ref,
):
    rows = q_ref.shape[0]
    allowed = allowed_pairs(seg_ref, rows, len(kv_refs) > 1)
    lane = lax.broadcasted_iota(jnp.int32, (rows, LANES), 1)
    kept = jnp.zeros((rows, LANES), F32)
    for group in range(KV_HEADS):
        query = pair_rows(q_ref, group)
        key = stacked(kv_refs, head_slice(group))
        value = stacked(kv_refs, head_slice(KV_HEADS + group))
        scores = lax.dot_general(query, key, INNER, preferred_element_type=F32)
        scores = jnp.where(allowed, scores * HEAD_DIM ** (-0.5), MASKED)
        highest = jnp.max(scores, axis=1, keepdims=True)
        exponent = jnp.exp(scores - highest)
        totals = jnp.sum(exponent, axis=1, keepdims=True)
        probs = (exponent / totals).astype(BF)
        blended = jnp.dot(probs, value, preferred_element_type=F32)
        cols = slice(group * GROUP * HEAD_DIM, (group + 1) * GROUP * HEAD_DIM)
        att_ref[:, cols] = pair_columns(blended).astype(BF)
        log_total = highest + jnp.log(totals)
        for which in range(GROUP):
            column = log_total[which * rows : (which + 1) * rows]
            kept = jnp.where(lane == GROUP * group + which, column, kept)
    lse_ref[...] = kept
    hidden = tok_ref[...].astype(F32) + jnp.dot(
        att_ref[...], wp_ref[...], preferred_element_type=F32
    )
    hid_ref[...] = hidden
    inverse = lax.rsqrt(jnp.mean(hidden * hidden, axis=1, keepdims=True) + EPS)
    normed = (hidden * inverse * gain_ref[...].astype(F32)).astype(BF)
    moe_ref[...] = normed
    logits = jnp.dot(normed, router_ref[...], preferred_element_type=F32)
    gates_ref[...] = gate_rows(logits, has_ref[...])


def expert_kernel(count, slots, based, *refs):
    pieces = len(slots)
    row_refs, cot_refs = refs[:count], refs[count : 2 * count]
    weight_refs = refs[2 * count : 2 * count + 3 * pieces]
    router_ref, *results = refs[2 * count + 3 * pieces :]
    base_refs, results = results[: 2 * count * based], results[2 * count * based :]
    lane = lax.broadcasted_iota(jnp.int32, (1, LANES), 1)
    owned = [lax.bitwise_xor(lax.axis_index(EP), NEAR * slot) for slot in range(1 + max(slots))]
    chosen = [jnp.where(lane == expert, 1.0, 0.0) for expert in owned]
    finer = [jnp.where(lane == expert + HALF_LANES, 1.0, 0.0) for expert in owned]
    for block in range(count):
        out_ref, gin_ref, act_ref, gga_ref, gua_ref = results[block::count]
        rows = row_refs[block][...]
        width = rows.shape[1]
        cots = cot_refs[block][:, :width]
        logits = jnp.dot(rows, router_ref[...], preferred_element_type=F32)
        gates = gate_rows(logits, cot_refs[block][:, width:])
        out = gin = None
        kept = jnp.zeros(gates.shape, F32)
        if based:
            out = base_refs[block][...]
            gin = base_refs[count + block][:, :width]
            kept = base_refs[count + block][:, width:]
        gate_grads = {}
        for piece, slot in enumerate(slots):
            wg_ref, wu_ref, wd_ref = weight_refs[3 * piece : 3 * piece + 3]
            gate = jnp.sum(gates * chosen[slot], axis=1, keepdims=True)
            gate_act = jnp.dot(rows, wg_ref[...], preferred_element_type=F32)
            up_act = jnp.dot(rows, wu_ref[...], preferred_element_type=F32)
            back = lax.dot_general(cots, wd_ref[...], INNER, preferred_element_type=F32)
            sigmoid_gate = 1.0 / (1.0 + jnp.exp(-gate_act))
            silu_gate = gate_act * sigmoid_gate
            acted = (silu_gate * up_act).astype(BF).astype(F32)
            part = jnp.sum(acted * back, axis=1, keepdims=True)
            gate_grads[slot] = part + gate_grads.get(slot, 0.0)
            acted_low = (acted * gate).astype(BF)
            grad_acted = back * gate
            grad_up_act = (grad_acted * silu_gate).astype(BF)
            grad_gate_act = (
                grad_acted * up_act * sigmoid_gate * (1.0 + gate_act * (1.0 - sigmoid_gate))
            ).astype(BF)
            hidden = wg_ref.shape[1]
            cols = slice(piece * hidden, (piece + 1) * hidden)
            act_ref[:, cols], gga_ref[:, cols], gua_ref[:, cols] = (
                acted_low, grad_gate_act, grad_up_act,
            )
            part = jnp.dot(acted_low, wd_ref[...], preferred_element_type=F32)
            out = part if out is None else out + part
            part = lax.dot_general(
                grad_gate_act, wg_ref[...], INNER, preferred_element_type=F32
            ) + lax.dot_general(grad_up_act, wu_ref[...], INNER, preferred_element_type=F32)
            gin = part if gin is None else gin + part
        for slot, grad in gate_grads.items():
            coarse = grad.astype(BF).astype(F32)
            kept += coarse * chosen[slot] + (grad - coarse) * finer[slot]
        out_ref[...] = out.astype(out_ref.dtype)
        gin_ref[:, :width] = gin.astype(gin_ref.dtype)
        gin_ref[:, width:] = kept.astype(gin_ref.dtype)


def run_expert(rows, cots, pieces, slots, router, base=(), last=True):
    count = len(rows)
    width, hidden = pieces[0][0].shape
    total = sum(part.shape[0] for part in rows)
    wide = hidden * len(pieces)
    kind = BF if last else F32
    columns = ((width, kind), (width + LANES, kind), (wide, BF), (wide, BF), (wide, BF))
    out = call(
        functools.partial(expert_kernel, count, slots, bool(base)),
        [sds((part.shape[0], cols), dtype) for cols, dtype in columns for part in rows],
        12 * total * width * wide,
        6 * width * wide + 10 * total * width,
    )(*rows, *cots, *[w for piece in pieces for w in piece], router, *base)
    return [out[i * count : (i + 1) * count] for i in range(len(columns))]


def run_near(rows, cots, pieces, slots, router):
    half = len(slots) // 2
    out, gin, *first = run_expert(rows, cots, pieces[:half], slots[:half], router, last=False)
    out, gin, *second = run_expert(
        rows, cots, pieces[half:], slots[half:], router, base=(*out, *gin)
    )
    return [out, gin, *[list(zip(*pair)) for pair in zip(first, second)]]


def weights_kernel(counts, slots, hidden, *refs):
    refs = list(refs)
    rows, cots = [refs.pop(0) for _ in counts], [refs.pop(0) for _ in counts]
    acts, ggas, guas = ([[refs.pop(0) for _ in range(n)] for n in counts] for _ in range(3))
    results = refs
    width = rows[0].shape[1]

    def tall(parts, cols):
        return jnp.concatenate([ref[:, cols] for ref in parts], axis=0)

    def piece_of(parts, piece):
        found = []
        for block in parts:
            each = len(slots) // len(block)
            start = piece % each * hidden
            found.append(block[piece // each][:, start : start + hidden])
        return jnp.concatenate(found, axis=0)

    rows = tall(rows, slice(0, width))
    cots = tall(cots, slice(0, width))
    for piece in range(len(slots)):
        gate = lax.dot_general(rows, piece_of(ggas, piece), OUTER, preferred_element_type=F32)
        up = lax.dot_general(rows, piece_of(guas, piece), OUTER, preferred_element_type=F32)
        down = lax.dot_general(piece_of(acts, piece), cots, OUTER, preferred_element_type=F32)
        if piece % 2:
            wide_ref, tall_ref = results[-2:]
            at = (piece // 2) * 2 * hidden
            wide_ref[:, at : at + hidden] = gate.astype(BF)
            wide_ref[:, at + hidden : at + 2 * hidden] = up.astype(BF)
            at = (piece // 2) * hidden
            tall_ref[at : at + hidden, :] = down.astype(BF)
        else:
            gate_ref, up_ref, down_ref = results[3 * (piece // 2) : 3 * (piece // 2) + 3]
            gate_ref[...], up_ref[...], down_ref[...] = gate, up, down


def weight_grads(rows, cots, acts, ggas, guas, slots, hidden):
    width = rows[0].shape[1]
    wide = hidden * len(slots)
    total = sum(part.shape[0] for part in rows)
    shapes = []
    for _ in range(0, len(slots), 2):
        shapes += [sds((width, hidden), F32), sds((width, hidden), F32), sds((hidden, width), F32)]
    if len(slots) > 1:
        shapes += [sds((width, wide), BF), sds((wide // 2, width), BF)]
    out = call(
        functools.partial(weights_kernel, tuple(len(block) for block in acts), slots, hidden),
        shapes,
        6 * total * width * wide,
        12 * width * wide + 4 * total * (width + wide),
    )(*rows, *cots, *[array for parts in (acts, ggas, guas) for block in parts for array in block])
    if not on_grid():
        return [
            lax.psum_scatter(grad, TP, scatter_dimension=axis, tiled=True)
            for grad, axis in zip(out, (1, 1, 0))
        ], []
    wide_part, tall_part = swap_core(out[6]), swap_core(out[7])
    slabs = [wide_part[:, i * hidden : (i + 1) * hidden] for i in range(4)]
    near_wide = jnp.concatenate([out[3] + slabs[2], out[4] + slabs[3]], axis=1).astype(BF)
    near_tall = (out[5] + tall_part[hidden:]).astype(BF)
    near_wide, near_tall = swap_side(near_wide, NEAR), swap_side(near_tall, NEAR)
    return (out[:3], [wide_part, tall_part, near_wide, near_tall])


def ending_kernel(
    gate_ref, up_ref, down_ref, wide_ref, tall_ref, near_wide_ref, near_tall_ref, *outs
):
    hidden = gate_ref.shape[1]
    for part, (ref, out) in enumerate(zip((gate_ref, up_ref), outs)):
        cols = slice(part * hidden, (part + 1) * hidden)
        out[...] = ref[...] + wide_ref[:, cols].astype(F32) + near_wide_ref[:, cols].astype(F32)
    outs[2][...] = (
        down_ref[...] + tall_ref[:hidden, :].astype(F32) + near_tall_ref[...].astype(F32)
    )


def ending(grads, parts):
    if not parts:
        return grads
    return call(
        ending_kernel, [sds(grad.shape, F32) for grad in grads], 0, 30 * grads[0].size
    )(*grads, *parts)


def column_sums(product):
    coarse = product.astype(BF)
    fine = (product - coarse.astype(F32)).astype(BF)
    ones = jnp.ones((product.shape[0], LANES), BF)
    return lax.dot_general(coarse, ones, OUTER, preferred_element_type=F32) + lax.dot_general(
        fine, ones, OUTER, preferred_element_type=F32
    )


def branch_kernel(
    gin_refs, hid_ref, gain_ref, cot_ref, gates_ref, router_ref, moe_ref, att_ref, wp_ref,
    ghid_ref, gatt_ref, *pay_refs,
):
    pay_ref = pay_refs[-1]
    width = hid_ref.shape[1]
    gates = gates_ref[...]
    grads = sum(ref[:, :width].astype(F32) for ref in gin_refs)
    dgate = sum(ref[:, width:].astype(F32) for ref in gin_refs)
    dgate = dgate + pltpu.roll(dgate, HALF_LANES, 1)
    total = jnp.sum(gates * dgate, axis=1, keepdims=True)
    grad_logits = (gates * (dgate - total)).astype(BF)
    experts = router_ref.shape[1]
    upstream = grads + lax.dot_general(
        grad_logits[:, :experts], router_ref[...], INNER, preferred_element_type=F32
    )
    hidden = hid_ref[...]
    inverse = lax.rsqrt(jnp.mean(hidden * hidden, axis=1, keepdims=True) + EPS)
    scaled = hidden * inverse
    product = upstream * scaled
    weighted = upstream * gain_ref[...].astype(F32)
    mean = jnp.mean(weighted * scaled, axis=1, keepdims=True)
    grad_hidden = cot_ref[...].astype(F32) + inverse * (weighted - scaled * mean)
    ghid_ref[...] = grad_hidden
    grad_branch = grad_hidden.astype(BF)
    gatt_ref[...] = lax.dot_general(
        grad_branch, wp_ref[...], INNER, preferred_element_type=F32
    ).astype(BF)
    pay_ref[:, :width] = lax.dot_general(
        att_ref[...], grad_branch, OUTER, preferred_element_type=F32
    ).astype(BF)
    grad_router = lax.dot_general(moe_ref[...], grad_logits, OUTER, preferred_element_type=F32)
    lane = lax.broadcasted_iota(jnp.int32, grad_router.shape, 1)
    pay_ref[:, width:] = jnp.where(lane == LANES - 1, column_sums(product), grad_router).astype(BF)
    if len(pay_refs) > 1:
        split_sum(pay_ref, *pay_refs[:2])


def attend_back_kernel(
    gatt_ref, q_ref, kv_refs, lse_ref, seg_ref, cos_ref, sin_ref, gq_ref, gkv_ref
):
    rows = q_ref.shape[0]
    allowed = allowed_pairs(seg_ref, rows, len(kv_refs) > 1)
    cosine, sine = own_rows(cos_ref, rows), own_rows(sin_ref, rows)
    kept = lse_ref[...]
    scale = HEAD_DIM ** (-0.5)
    for pair in range(KV_HEADS // 2):
        grad_keys, grad_values = [], []
        for group in (2 * pair, 2 * pair + 1):
            query = pair_rows(q_ref, group)
            grad = pair_rows(gatt_ref, group)
            key = stacked(kv_refs, head_slice(group))
            value = stacked(kv_refs, head_slice(KV_HEADS + group))
            log_total = jnp.concatenate(
                [kept[:, GROUP * group + i : GROUP * group + i + 1] for i in range(GROUP)], axis=0
            )
            scores = lax.dot_general(query, key, INNER, preferred_element_type=F32)
            scores = jnp.where(allowed, scores * scale, MASKED)
            probs = jnp.exp(scores - log_total)
            grad_values.append(
                lax.dot_general(probs.astype(BF), grad, OUTER, preferred_element_type=F32)
            )
            grad_probs = lax.dot_general(grad, value, INNER, preferred_element_type=F32)
            delta = jnp.sum(probs * grad_probs, axis=1, keepdims=True)
            grad_scores = (probs * (grad_probs - delta)).astype(BF)
            grad_query = jnp.dot(grad_scores, key, preferred_element_type=F32) * scale
            grad_query = pair_columns(grad_query).astype(BF).astype(F32)
            cols = slice(group * GROUP * HEAD_DIM, (group + 1) * GROUP * HEAD_DIM)
            gq_ref[:, cols] = (grad_query * cosine - swap_halves(grad_query) * sine).astype(BF)
            grad_keys.append(
                lax.dot_general(grad_scores, query, OUTER, preferred_element_type=F32) * scale
            )
        for shift, grads in ((0, grad_keys), (KV_HEADS * HEAD_DIM, grad_values)):
            cols = slice(shift + pair * LANES, shift + (pair + 1) * LANES)
            gkv_ref[:, cols] = jnp.concatenate(grads, axis=1).astype(BF)


def project_back_kernel(
    norm_refs, gq_refs, gkv_refs, cos_ref, sin_ref, wq_ref, wk_ref, wv_ref, tok_ref, gain_ref,
    ghid_ref, gtok_ref, *pay_refs,
):
    gkraw_ref, pay_ref = pay_refs[-1], pay_refs[-2]
    rows = tok_ref.shape[0]
    kwidth = wk_ref.shape[1]
    shared = len(gkv_refs) > 1

    def total(who, cols):
        parts = [gkv_refs[0][who * rows : (who + 1) * rows, cols]]
        if shared:
            parts.append(gkv_refs[1][(1 - who) * rows : (2 - who) * rows, cols])
        return add_low(*parts)

    for who in range(len(gkv_refs)):
        cosine, sine = own_rows(cos_ref, rows, who > 0), own_rows(sin_ref, rows, who > 0)
        for cols in blocks(kwidth):
            part = total(who, cols).astype(F32)
            gkraw_ref[who * rows : (who + 1) * rows, cols] = (
                part * cosine - swap_halves(part) * sine
            ).astype(BF)
    grad_query = jnp.concatenate([ref[...] for ref in gq_refs], axis=0)
    grad_key = gkraw_ref[...]
    values_cols = slice(kwidth, 2 * kwidth)
    grad_value = jnp.concatenate([total(who, values_cols) for who in range(len(gkv_refs))], axis=0)
    upstream = lax.dot_general(grad_query[:rows], wq_ref[...], INNER, preferred_element_type=F32)
    upstream += lax.dot_general(grad_key[:rows], wk_ref[...], INNER, preferred_element_type=F32)
    upstream += lax.dot_general(grad_value[:rows], wv_ref[...], INNER, preferred_element_type=F32)
    normed = jnp.concatenate([ref[...] for ref in norm_refs], axis=0)
    half = normed.shape[1] // 2
    low = lax.axis_index(TP) == 0
    if shared:
        normed = jnp.where(low, normed[:, :half], normed[:, half:])
    start = 0
    for grad in (grad_query, grad_key, grad_value):
        pay_ref[:, start : start + grad.shape[1]] = lax.dot_general(
            normed, grad, OUTER, preferred_element_type=F32
        ).astype(BF)
        start += grad.shape[1]
    values = tok_ref[...].astype(F32)
    inverse = lax.rsqrt(jnp.mean(values * values, axis=1, keepdims=True) + EPS)
    scaled = values * inverse
    sums = column_sums(upstream * scaled)
    if shared:
        lane = lax.broadcasted_iota(jnp.int32, (half, LANES), 1)
        sums = jnp.where((lane < HALF_LANES) == low, sums[:half], sums[half:])
    pay_ref[:, start:] = sums.astype(BF)
    weighted = upstream * gain_ref[...].astype(F32)
    mean = jnp.mean(weighted * scaled, axis=1, keepdims=True)
    gtok_ref[...] = (ghid_ref[...] + inverse * (weighted - scaled * mean)).astype(BF)
    if shared:
        spread_sum(pay_ref, *pay_refs[:4])


def sds(shape, dtype):
    return jax.ShapeDtypeStruct(shape, dtype)


def layer(
    tokens,
    segment_ids,
    routes,
    cotangent,
    query_weight,
    key_weight,
    value_weight,
    proj_weight,
    attn_gain,
    moe_gain,
    router_weight,
    gate_weight,
    up_weight,
    down_weight,
):
    tok_count, model_dim = tokens.shape
    seq_len = segment_ids.shape[1]
    experts = router_weight.shape[1]
    query_dim, kv_dim = HEADS * HEAD_DIM, KV_HEADS * HEAD_DIM

    has = (routes[:, :, None] == jnp.arange(LANES, dtype=jnp.int32)[None, None, :]).any(axis=1)
    has = has.astype(BF)
    cots = gather_rows(jnp.concatenate([cotangent, has], axis=1))
    pieces, slots = expert_pieces((gate_weight[0], up_weight[0], down_weight[0]), (1, 1, 0))

    cosine, sine = (jnp.asarray(table) for table in rope_tables(seq_len))
    gain_one, gain_two = attn_gain[None, :], moe_gain[None, :]

    normed, query, kv = call(
        project_kernel,
        (
            sds((tok_count, model_dim), BF),
            sds((tok_count, query_dim), BF),
            sds((tok_count, 2 * kv_dim), BF),
        ),
        4 * tok_count * model_dim * model_dim,
        5 * model_dim * model_dim,
    )(tokens, gain_one, query_weight, key_weight, value_weight, cosine, sine)

    if on_grid():
        kv_all = [kv, swap_core(kv)]
    else:
        kv_all = [lax.all_gather(kv, TP, axis=0, tiled=True)]

    attended, log_totals, hidden, moe_input, gates = call(
        attend_kernel,
        (
            sds((tok_count, query_dim), BF),
            sds((tok_count, LANES), F32),
            sds((tok_count, model_dim), F32),
            sds((tok_count, model_dim), BF),
            sds((tok_count, LANES), F32),
        ),
        4 * tok_count * model_dim * model_dim,
        5 * model_dim * model_dim,
    )(query, kv_all, segment_ids, proj_weight, tokens, gain_two, router_weight, has)

    rows = gather_rows(moe_input)
    done = []
    for index, part in enumerate(zip(rows, cots)):
        if on_grid() and not index:
            done.append(run_near(*part, pieces, slots, router_weight))
            continue
        *sums, acts, ggas, guas = run_expert(*part, pieces, slots, router_weight)
        done.append([*sums, *[[(array,) for array in arrays] for arrays in (acts, ggas, guas)]])
    outputs, grad_inputs, acts, ggas, guas = zip(*done)
    grad_rows_in = scatter_rows(grad_inputs)

    def flat(blocks):
        return [array for part in blocks for array in part]

    grads, parts = weight_grads(
        flat(rows), flat(cots), flat(acts), flat(ggas), flat(guas), slots, pieces[0][0].shape[1]
    )
    grad_gate, grad_up, grad_down = ending(grads, parts)
    blended = [part for part in scatter_rows(outputs) if part is not None]
    layer_out = (hidden + sum(part.astype(F32) for part in blended)).astype(BF)

    outs, scratch = sum_shapes(model_dim, model_dim + LANES)
    grad_rows_in = [part for part in grad_rows_in if part is not None]
    grad_hidden, grad_attended, *early = call(
        branch_kernel,
        [sds((tok_count, model_dim), F32), sds((tok_count, query_dim), BF), *outs],
        4 * tok_count * model_dim * model_dim,
        5 * model_dim * model_dim,
        scratch_shapes=scratch,
    )(
        grad_rows_in, hidden, gain_two, cotangent, gates, router_weight, moe_input, attended,
        proj_weight,
    )

    grad_query, grad_kv = call(
        attend_back_kernel,
        [sds((tok_count, query_dim), BF), sds((seq_len, 2 * kv_dim), BF)],
        4 * tok_count * model_dim * model_dim,
        5 * model_dim * model_dim,
    )(grad_attended, query, kv_all, log_totals, segment_ids, cosine, sine)
    if on_grid():
        normed = [normed, swap_core(normed)]
        grad_kv = [grad_kv, swap_core(grad_kv)]
        grad_query = [grad_query, swap_core(grad_query)]
    else:
        normed, grad_query = [normed], [grad_query]
        grad_kv = [lax.psum_scatter(grad_kv, TP, scatter_dimension=0, tiled=True)]

    outs, scratch = late_shapes(model_dim, query_dim + 2 * kv_dim + LANES)
    grad_tokens, *late = call(
        project_back_kernel,
        [sds((tok_count, model_dim), BF), *outs],
        8 * tok_count * model_dim * model_dim,
        9 * model_dim * model_dim,
        scratch_shapes=scratch + [pltpu.VMEM((tok_count * len(grad_kv), kv_dim), BF)],
    )(
        normed, grad_query, grad_kv, cosine, sine, query_weight, key_weight, value_weight, tokens,
        gain_one, grad_hidden,
    )
    early_widths, late_widths = (model_dim,), (query_dim, kv_dim, kv_dim)
    if on_grid():
        grad_proj, grad_router, gain_grad_two = finish(
            sum_everywhere(*share_core(*early)), early_widths, experts
        )
        *late, gain_grad_one = finish(sum_everywhere(*late), late_widths, 0)
        gain_grad_one, gain_grad_two = gain_grad_one.reshape(-1), gain_grad_two.reshape(-1)
        grad_router = grad_router.T
    else:
        early, late = (
            jnp.split(lax.psum(low.astype(F32), (EP, TP)), np.cumsum(widths), axis=1)
            for low, widths in ((early[0], early_widths), (late[0], late_widths))
        )
        grad_proj, side = early
        grad_router, gain_grad_two = side[:, :experts], side[:, LANES - 1]
        gain_grad_one = late.pop()[:, LANES - 1]
    return (
        layer_out,
        grad_tokens,
        *late,
        grad_proj,
        gain_grad_one,
        gain_grad_two,
        grad_router,
        grad_gate[None],
        grad_up[None],
        grad_down[None],
    )


def solution(mesh):
    placed = (
        P((EP, TP), None),
        P(EP, None),
        P((EP, TP), None),
        P((EP, TP), None),
        P(),
        P(),
        P(),
        P(),
        P(),
        P(),
        P(),
        P(EP, None, TP),
        P(EP, None, TP),
        P(EP, TP, None),
    )
    step = jax.shard_map(
        layer,
        mesh=mesh,
        in_specs=placed,
        out_specs=(
            P((EP, TP), None),
            P((EP, TP), None),
            P(),
            P(),
            P(),
            P(),
            P(),
            P(),
            P(),
            P(EP, None, TP),
            P(EP, None, TP),
            P(EP, TP, None),
        ),
        check_vma=False,
    )
    if mesh.shape[EP] != LINE * SIDE * SIDE or mesh.shape[TP] != SIDE:
        return step
    return step
```
